256 devices in a mesh: gx: 4 (over z_hi, core), gy: 4 (over x), gz: 16 (over y, z_lo).
Axes of the slice: x: 4, y: 4, z: 8 (z_hi: 2, z_lo: 4; z = z_hi * 4 + z_lo), core: 2. Of those that a mesh axis runs over, the one named last changes fastest.
Arguments:
- local_solution: float32 [3, 68, 180, 2048], P(None, 'gx', 'gy', 'gz'), may hold values from -6 to 6
- top_nodes: float32 [3, 68, 180, 16], P(None, 'gx', 'gy', 'gz'), may hold values from -6 to 6
- coarse_solution: float32 [3, 8192], P(None, 'gz'), may hold values from -6 to 6
- corner_dofs: int32 [4, 4, 16, 8], P('gx', 'gy', 'gz'), may hold values from 0 to 8191
- density: float32 [64, 176, 2048], P('gx', 'gy', 'gz'), may hold values from 0.1 to 1
- element_stiffness: float32 [24, 24], replicated, may hold values from -0.15 to 4.5, as said below
Outputs:
- filtered_sens: float32 [64, 176, 2048], P('gx', 'gy', 'gz')
- filtered_density: float32 [64, 176, 2048], P('gx', 'gy', 'gz')
The draws below stay inside these ranges and needn't reach their ends.
Inputs may be any that keep to these rules, and one draw needn't show every extreme that they name: element_stiffness is symmetric.
All inputs are finite; a program needn't handle non-finite values.
Results may differ from the reference program's by a relative error of at most 0.00005.
Values sent between devices are 32-bit elements; how exact they have to be, the bound alone decides.
A program may use at most 64 MiB of HBM per device.

```python
import jax
import jax.numpy as jnp
from jax import lax

CX = 16
CY = 44
CZ = 128
RADIUS = 3
NX = 64
NY = 176
NZ = 2048
NXN = 68
NYN = 180
NCOARSE = 8192
N_GX = 4
N_GY = 4
N_GZ = 16


def draw_element_stiffness(key, part):
    first_key, second_key = jax.random.split(key, 2)
    raw_off = jax.random.uniform(first_key, (24, 24), jnp.float32, -0.15, 0.15)
    diag_part = 4.0 + jax.random.uniform(second_key, (24,), jnp.float32, -0.5, 0.5)
    off_part = 0.5 * (raw_off + raw_off.T)
    identity = jnp.eye(24, dtype=jnp.float32)
    return off_part * (1.0 - identity) + identity * diag_part[:, None]


def touch_ends(result, rng, low, largest):
    longest = result.shape.index(max(result.shape))
    spots = []
    for shift in (0, 1):
        where = [jax.random.randint(jax.random.fold_in(rng, axis), (), 0, length) for axis, length in enumerate(result.shape)]
        where[longest] = (where[longest] + shift) % result.shape[longest]
        spots.append(tuple(where))
    return result.at[spots[0]].set(low).at[spots[1]].set(largest)


def shard_levels(stream_key, extent, cuts, smallest, largest):
    level, own = 1.0, jax.random.fold_in(stream_key, 6)
    for dim, parts in cuts:
        steps = jnp.exp(jax.random.uniform(jax.random.fold_in(own, dim), (parts,), jnp.float32, smallest / len(cuts), largest / len(cuts)))
        level = level * jnp.repeat(steps, extent[dim] // parts).reshape([-1 if axis == dim else 1 for axis in range(len(extent))])
    return level


def normal_values(stream_key, shape, deviation, bound, cuts=(), kind=jnp.bfloat16):
    factor_of = shard_levels(stream_key, shape, cuts, -0.22, 0.18) if cuts else 1.0
    result = jax.random.normal(stream_key, shape, jnp.float32) * deviation * factor_of
    return jnp.minimum(jnp.maximum(result, -bound), bound).astype(kind)


def setup_inputs(seed: int = 0) -> dict:
    splits = jax.random.split(jax.random.key(seed), 7)
    local_solution = normal_values(splits[0], (3, NXN, NYN, NZ), 1.0, 6.0, ((1, 4), (2, 4), (3, 16)), jnp.float32)
    top_nodes = normal_values(splits[1], (3, NXN, NYN, N_GZ), 1.0, 6.0, ((1, 4), (2, 4), (3, 16)), jnp.float32)
    coarse_solution = normal_values(splits[2], (3, NCOARSE), 1.0, 6.0, ((1, 16),), jnp.float32)
    corner_dofs = touch_ends(jax.random.randint(splits[3], (N_GX, N_GY, N_GZ, 8), 0, NCOARSE), jax.random.fold_in(splits[3], 1), 0, NCOARSE - 1).astype(jnp.int32)
    density = jnp.clip(0.1 + 0.9 * jax.random.uniform(splits[4], (NX, NY, NZ), jnp.float32) ** shard_levels(splits[4], (NX, NY, NZ), ((0, 4), (1, 4), (2, 16)), -0.2, 0.2), 0.1, 1.0)
    element_stiffness = draw_element_stiffness(jax.random.fold_in(splits[6], 71), 0)
    return {"local_solution": local_solution, "top_nodes": top_nodes, "coarse_solution": coarse_solution, "corner_dofs": corner_dofs, "density": density, "element_stiffness": element_stiffness}


penal_scale = -3.0 / 96.0


def recover(local_nodes, corner_vals):
    ex = local_nodes.shape[1] - 1
    ey = local_nodes.shape[2] - 1
    ez = local_nodes.shape[3] - 1
    ratio_x = jnp.arange(ex + 1, dtype=jnp.float32) / ex
    ratio_y = jnp.arange(ey + 1, dtype=jnp.float32) / ey
    ratio_z = jnp.arange(ez + 1, dtype=jnp.float32) / ez
    summed = local_nodes
    for corner in range(8):
        along_x = ratio_x if corner // 4 == 1 else 1.0 - ratio_x
        along_y = ratio_y if (corner // 2) % 2 == 1 else 1.0 - ratio_y
        along_z = ratio_z if corner % 2 == 1 else 1.0 - ratio_z
        basis = along_x[:, None, None] * along_y[None, :, None] * along_z[None, None, :]
        summed = summed + basis[None] * corner_vals[:, corner][:, None, None, None]
    return summed


def element_energy(node_block, stiffness):
    ex = node_block.shape[1] - 1
    ey = node_block.shape[2] - 1
    ez = node_block.shape[3] - 1

    def rows_energy(first_row):
        node_slab = lax.dynamic_slice_in_dim(node_block, first_row, 5, axis=1)
        columns = []
        for corner in range(8):
            shift_x = corner // 4
            shift_y = (corner // 2) % 2
            shift_z = corner % 2
            columns.append(node_slab[:, shift_x:shift_x + 4, shift_y:shift_y + ey, shift_z:shift_z + ez].reshape(3, -1))
        vectors = jnp.stack(columns, axis=1).reshape(24, -1)
        product = jnp.dot(stiffness, vectors, precision=lax.Precision.HIGHEST, preferred_element_type=jnp.float32)
        return jnp.sum(vectors * product, axis=0).reshape(4, ey, ez)

    starts = (jnp.arange(ex // 4, dtype=jnp.int32) * 4).astype(jnp.int32)
    energies = lax.map(rows_energy, starts)
    return energies.reshape(ex, ey, ez)


def smooth(field, axis, count):
    summed = None
    for offset in range(-RADIUS, RADIUS + 1):
        term_piece = lax.slice_in_dim(field, RADIUS + offset, RADIUS + offset + count, axis=axis)
        term_value = float(RADIUS + 1 - abs(offset)) * term_piece
        summed = term_value if summed is None else summed + term_value
    return summed


def conv_global(field):
    for axis in range(3):
        count = field.shape[axis]
        widths = [(0, 0), (0, 0), (0, 0)]
        widths[axis] = (RADIUS, RADIUS)
        field = smooth(jnp.pad(field, widths), axis, count)
    return field


def reference(local_solution, top_nodes, coarse_solution, corner_dofs, density, element_stiffness):
    blocks = N_GX * N_GY * N_GZ
    lower_part = local_solution.reshape(3, N_GX, CX + 1, N_GY, CY + 1, N_GZ, CZ)
    top_part = top_nodes.reshape(3, N_GX, CX + 1, N_GY, CY + 1, N_GZ, 1)
    grid = jnp.concatenate([lower_part, top_part], axis=6)
    grid = grid.transpose(1, 3, 5, 0, 2, 4, 6).reshape(blocks, 3, CX + 1, CY + 1, CZ + 1)
    indices = corner_dofs.reshape(-1).astype(jnp.int32)
    corner_vals = jnp.take(coarse_solution, indices, axis=1).reshape(3, blocks, 8).transpose(1, 0, 2)

    def recover_pair(pair):
        return recover(pair[0], pair[1])

    grid = lax.map(recover_pair, (grid, corner_vals))
    grid = grid.reshape(N_GX, N_GY, N_GZ, 3, CX + 1, CY + 1, CZ + 1)
    lower = grid[1:, :, :, :, 0]
    upper = grid[:-1, :, :, :, CX]
    middle = lower * 0.5 + upper * 0.5
    grid = grid.at[1:, :, :, :, 0].set(middle).at[:-1, :, :, :, CX].set(middle)
    lower = grid[:, 1:, :, :, :, 0]
    upper = grid[:, :-1, :, :, :, CY]
    middle = lower * 0.5 + upper * 0.5
    grid = grid.at[:, 1:, :, :, :, 0].set(middle).at[:, :-1, :, :, :, CY].set(middle)
    lower = grid[:, :, 1:, :, :, :, 0]
    upper = grid[:, :, :-1, :, :, :, CZ]
    middle = lower * 0.5 + upper * 0.5
    grid = grid.at[:, :, 1:, :, :, :, 0].set(middle).at[:, :, :-1, :, :, :, CZ].set(middle)
    grid = grid.reshape(blocks, 3, CX + 1, CY + 1, CZ + 1)

    def block_energy(node_block):
        return element_energy(node_block, element_stiffness)

    energy = lax.map(block_energy, grid)
    energy = energy.reshape(N_GX, N_GY, N_GZ, CX, CY, CZ).transpose(0, 3, 1, 4, 2, 5).reshape(NX, NY, NZ)
    sens = penal_scale * density * density * energy
    normalizer = conv_global(jnp.ones((NX, NY, NZ), jnp.float32))
    numerator = conv_global(density * sens)
    smooth_density = conv_global(density)
    return numerator / (density * normalizer), smooth_density / normalizer
```

```python
import jax
import jax.numpy as jnp
from jax import lax
from jax.sharding import PartitionSpec as P

RADIUS = 3


penal_scale = -3.0 / 96.0


def with_halo(shard, sides, width):
    for axis, dim in sides:
        count, length = (lax.axis_size(axis), shard.shape[dim])
        up = [(i, (i + 1) % count) for i in range(count - 1)]
        down = [(j, i) for i, j in up]
        last = lax.slice_in_dim(shard, length - width, length, axis=dim)
        initial = lax.slice_in_dim(shard, 0, width, axis=dim)
        before = lax.ppermute(last, axis, up)
        after = lax.ppermute(initial, axis, down)
        shard = jnp.concatenate([before, shard, after], axis=dim)
    return shard


def recover(local_nodes, corner_vals, ratio_z):
    ex = local_nodes.shape[1] - 1
    ey = local_nodes.shape[2] - 1
    ratio_x = jnp.arange(ex + 1, dtype=jnp.float32) / ex
    ratio_y = jnp.arange(ey + 1, dtype=jnp.float32) / ey
    summed = local_nodes
    for corner in range(8):
        along_x = ratio_x if corner // 4 == 1 else 1.0 - ratio_x
        along_y = ratio_y if corner // 2 % 2 == 1 else 1.0 - ratio_y
        along_z = ratio_z if corner % 2 == 1 else 1.0 - ratio_z
        basis = along_x[:, None, None] * along_y[None, :, None] * along_z[None, None, :]
        summed = summed + basis[None] * corner_vals[:, corner][:, None, None, None]
    return summed


def average_rows(extended, dim, has_lower, has_upper):
    inner = extended.shape[dim] - 2
    own_rows = lax.slice_in_dim(extended, 1, inner + 1, axis=dim)
    rim_low = lax.slice_in_dim(extended, 0, 1, axis=dim)
    rim_high = lax.slice_in_dim(extended, inner + 1, inner + 2, axis=dim)
    shape_row = [1] * extended.ndim
    shape_row[dim] = inner
    rows = jnp.arange(inner, dtype=jnp.int32).reshape(shape_row)
    is_low = rows == 0
    is_high = rows == inner - 1
    factor = jnp.where(is_low & has_lower, 0.5, jnp.where(is_high & has_upper, 0.5, 1.0))
    rim_part = jnp.where(is_low, rim_low, 0.0) + jnp.where(is_high, rim_high, 0.0)
    return own_rows * factor + rim_part * 0.5


def element_energy(lower_nodes, upper_nodes, stiffness):
    ex = lower_nodes.shape[1] - 1
    ey = lower_nodes.shape[2] - 1

    def rows_energy(first_row):
        slab_low = lax.dynamic_slice_in_dim(lower_nodes, first_row, 5, axis=1)
        slab_up = lax.dynamic_slice_in_dim(upper_nodes, first_row, 5, axis=1)
        columns = []
        for corner in range(8):
            shift_x = corner // 4
            shift_y = corner // 2 % 2
            source = slab_up if corner % 2 == 1 else slab_low
            columns.append(source[:, shift_x : shift_x + 4, shift_y : shift_y + ey, :])
        vectors = jnp.stack(columns, axis=1)
        vectors = vectors.reshape((24,) + vectors.shape[2:])
        product = jnp.einsum(
            "ij,jabc->iabc",
            stiffness,
            vectors,
            precision=lax.Precision.HIGHEST,
            preferred_element_type=jnp.float32,
        )
        return jnp.sum(vectors * product, axis=0)

    starts = jnp.arange(ex // 4, dtype=jnp.int32) * 4
    energies = lax.map(rows_energy, starts)
    return energies.reshape((ex,) + energies.shape[2:])


def smooth(field, axis, count):
    summed = None
    for offset in range(-RADIUS, RADIUS + 1):
        term_piece = lax.slice_in_dim(field, RADIUS + offset, RADIUS + offset + count, axis=axis)
        term_value = float(RADIUS + 1 - abs(offset)) * term_piece
        summed = term_value if summed is None else summed + term_value
    return summed


def edge_counts(count, position, parts):
    places = position * count + jnp.arange(count, dtype=jnp.int32)
    summed = None
    for offset in range(-RADIUS, RADIUS + 1):
        inside = ((places + offset >= 0) & (places + offset < count * parts)).astype(jnp.float32)
        term_value = float(RADIUS + 1 - abs(offset)) * inside
        summed = term_value if summed is None else summed + term_value
    return summed


def filter_field(field, sides):
    for axis, dim in sides:
        padded = with_halo(field, ((axis, dim),), RADIUS)
        field = smooth(padded, dim, field.shape[dim])
    return field


def local(local_solution, top_nodes, coarse_solution, corner_dofs, density, element_stiffness):
    count_x, count_y, count_z = density.shape
    index_x = lax.axis_index("gx")
    index_y = lax.axis_index("gy")
    index_z = lax.axis_index("gz")
    normalizer = (
        edge_counts(count_x, index_x, lax.axis_size("gx"))[:, None, None]
        * edge_counts(count_y, index_y, lax.axis_size("gy"))[None, :, None]
        * edge_counts(count_z, index_z, lax.axis_size("gz"))[None, None, :]
    )
    sides = (("gx", 0), ("gy", 1), ("gz", 2))
    smooth_density = filter_field(density, sides)
    wanted = corner_dofs.reshape(8)
    columns = lax.all_gather(coarse_solution, "gz", axis=1, tiled=True)
    matches = wanted[:, None] == jnp.arange(columns.shape[1], dtype=jnp.int32)[None, :]
    corner_vals = jnp.sum(jnp.where(matches[None], columns[:, None, :], 0.0), axis=2)
    depth = local_solution.shape[3]
    full = jnp.concatenate([local_solution, top_nodes], axis=3)
    nodes = recover(full, corner_vals, jnp.arange(depth + 1, dtype=jnp.float32) / depth)
    lower_x = index_x > 0
    upper_x = index_x < lax.axis_size("gx") - 1
    lower_y = index_y > 0
    upper_y = index_y < lax.axis_size("gy") - 1
    lower_z = index_z > 0
    upper_z = index_z < lax.axis_size("gz") - 1
    extended = with_halo(nodes, (("gx", 1), ("gy", 2)), 1)
    extended = average_rows(extended, 1, lower_x, upper_x)
    averaged = average_rows(extended, 2, lower_y, upper_y)
    extended = with_halo(averaged, (("gz", 3),), 1)
    averaged = average_rows(extended, 3, lower_z, upper_z)
    energy = element_energy(averaged[:, :, :, :depth], averaged[:, :, :, 1:], element_stiffness)
    sens = penal_scale * density * density * energy
    numerator = filter_field(density * sens, sides)
    return (numerator / (density * normalizer), smooth_density / normalizer)


def solution(mesh):
    in_specs = (
        P(None, "gx", "gy", "gz"),
        P(None, "gx", "gy", "gz"),
        P(None, "gz"),
        P("gx", "gy", "gz", None),
        P("gx", "gy", "gz"),
        P(),
    )
    out_specs = (P("gx", "gy", "gz"), P("gx", "gy", "gz"))
    return jax.shard_map(local, mesh=mesh, in_specs=in_specs, out_specs=out_specs, check_vma=False)
```

```python
import jax
import jax.numpy as jnp
from jax import lax
from jax.sharding import PartitionSpec as P

RADIUS = 3


penal_scale = -3.0 / 96.0


def with_halo(shard, sides, width):
    for axis, dim in sides:
        count, length = (lax.axis_size(axis), shard.shape[dim])
        up = [(i, (i + 1) % count) for i in range(count - 1)]
        down = [(j, i) for i, j in up]
        last = lax.slice_in_dim(shard, length - width, length, axis=dim)
        initial = lax.slice_in_dim(shard, 0, width, axis=dim)
        before = lax.ppermute(last, axis, up)
        after = lax.ppermute(initial, axis, down)
        shard = jnp.concatenate([before, shard, after], axis=dim)
    return shard


def recover(local_nodes, corner_vals, ratio_z):
    ex = local_nodes.shape[1] - 1
    ey = local_nodes.shape[2] - 1
    ratio_x = jnp.arange(ex + 1, dtype=jnp.float32) / ex
    ratio_y = jnp.arange(ey + 1, dtype=jnp.float32) / ey
    summed = local_nodes
    for corner in range(8):
        along_x = ratio_x if corner // 4 == 1 else 1.0 - ratio_x
        along_y = ratio_y if corner // 2 % 2 == 1 else 1.0 - ratio_y
        along_z = ratio_z if corner % 2 == 1 else 1.0 - ratio_z
        basis = along_x[:, None, None] * along_y[None, :, None] * along_z[None, None, :]
        summed = summed + basis[None] * corner_vals[:, corner][:, None, None, None]
    return summed


def average_rows(extended, dim, has_lower, has_upper):
    inner = extended.shape[dim] - 2
    own_rows = lax.slice_in_dim(extended, 1, inner + 1, axis=dim)
    rim_low = lax.slice_in_dim(extended, 0, 1, axis=dim)
    rim_high = lax.slice_in_dim(extended, inner + 1, inner + 2, axis=dim)
    shape_row = [1] * extended.ndim
    shape_row[dim] = inner
    rows = jnp.arange(inner, dtype=jnp.int32).reshape(shape_row)
    is_low = rows == 0
    is_high = rows == inner - 1
    factor = jnp.where(is_low & has_lower, 0.5, jnp.where(is_high & has_upper, 0.5, 1.0))
    rim_part = jnp.where(is_low, rim_low, 0.0) + jnp.where(is_high, rim_high, 0.0)
    return own_rows * factor + rim_part * 0.5


def element_energy(lower_nodes, upper_nodes, stiffness):
    ex = lower_nodes.shape[1] - 1
    ey = lower_nodes.shape[2] - 1

    def rows_energy(first_row):
        slab_low = lax.dynamic_slice_in_dim(lower_nodes, first_row, 5, axis=1)
        slab_up = lax.dynamic_slice_in_dim(upper_nodes, first_row, 5, axis=1)
        columns = []
        for corner in range(8):
            shift_x = corner // 4
            shift_y = corner // 2 % 2
            source = slab_up if corner % 2 == 1 else slab_low
            columns.append(source[:, shift_x : shift_x + 4, shift_y : shift_y + ey, :])
        vectors = jnp.stack(columns, axis=1)
        vectors = vectors.reshape((24,) + vectors.shape[2:])
        product = jnp.einsum(
            "ij,jabc->iabc",
            stiffness,
            vectors,
            precision=lax.Precision.HIGHEST,
            preferred_element_type=jnp.float32,
        )
        return jnp.sum(vectors * product, axis=0)

    starts = jnp.arange(ex // 4, dtype=jnp.int32) * 4
    energies = lax.map(rows_energy, starts)
    return energies.reshape((ex,) + energies.shape[2:])


def smooth(field, axis, count):
    summed = None
    for offset in range(-RADIUS, RADIUS + 1):
        term_piece = lax.slice_in_dim(field, RADIUS + offset, RADIUS + offset + count, axis=axis)
        term_value = float(RADIUS + 1 - abs(offset)) * term_piece
        summed = term_value if summed is None else summed + term_value
    return summed


def edge_counts(count, position, parts):
    places = position * count + jnp.arange(count, dtype=jnp.int32)
    summed = None
    for offset in range(-RADIUS, RADIUS + 1):
        inside = ((places + offset >= 0) & (places + offset < count * parts)).astype(jnp.float32)
        term_value = float(RADIUS + 1 - abs(offset)) * inside
        summed = term_value if summed is None else summed + term_value
    return summed


def filter_field(field, sides):
    for axis, dim in sides:
        padded = with_halo(field, ((axis, dim),), RADIUS)
        field = smooth(padded, dim, field.shape[dim])
    return field


def local(local_solution, top_nodes, coarse_solution, corner_dofs, density, element_stiffness):
    count_x, count_y, count_z = density.shape
    index_x = lax.axis_index("gx")
    index_y = lax.axis_index("gy")
    index_z = lax.axis_index("gz")
    normalizer = (
        edge_counts(count_x, index_x, lax.axis_size("gx"))[:, None, None]
        * edge_counts(count_y, index_y, lax.axis_size("gy"))[None, :, None]
        * edge_counts(count_z, index_z, lax.axis_size("gz"))[None, None, :]
    )
    sides = (("gx", 1), ("gy", 2), ("gz", 3))
    wanted = corner_dofs.reshape(8)
    parts = lax.axis_size("gz")
    spread = jnp.broadcast_to(coarse_solution[None], (parts,) + coarse_solution.shape)
    gathered = lax.all_to_all(spread, "gz", 0, 0, tiled=True)
    columns = gathered.transpose(1, 0, 2).reshape(coarse_solution.shape[0], -1)
    matches = wanted[:, None] == jnp.arange(columns.shape[1], dtype=jnp.int32)[None, :]
    corner_vals = jnp.sum(jnp.where(matches[None], columns[:, None, :], 0.0), axis=2)
    depth = local_solution.shape[3]
    full = jnp.concatenate([local_solution, top_nodes], axis=3)
    nodes = recover(full, corner_vals, jnp.arange(depth + 1, dtype=jnp.float32) / depth)
    lower_x = index_x > 0
    upper_x = index_x < lax.axis_size("gx") - 1
    lower_y = index_y > 0
    upper_y = index_y < lax.axis_size("gy") - 1
    lower_z = index_z > 0
    upper_z = index_z < lax.axis_size("gz") - 1
    extended = with_halo(nodes, (("gx", 1), ("gy", 2)), 1)
    extended = average_rows(extended, 1, lower_x, upper_x)
    averaged = average_rows(extended, 2, lower_y, upper_y)
    extended = with_halo(averaged, (("gz", 3),), 1)
    averaged = average_rows(extended, 3, lower_z, upper_z)
    energy = element_energy(averaged[:, :, :, :depth], averaged[:, :, :, 1:], element_stiffness)
    sens = penal_scale * density * density * energy
    smoothed = filter_field(jnp.stack([density * sens, density]), sides)
    numerator = smoothed[0]
    smooth_density = smoothed[1]
    return (numerator / (density * normalizer), smooth_density / normalizer)


def solution(mesh):
    in_specs = (
        P(None, "gx", "gy", "gz"),
        P(None, "gx", "gy", "gz"),
        P(None, "gz"),
        P("gx", "gy", "gz", None),
        P("gx", "gy", "gz"),
        P(),
    )
    out_specs = (P("gx", "gy", "gz"), P("gx", "gy", "gz"))
    return jax.shard_map(local, mesh=mesh, in_specs=in_specs, out_specs=out_specs, check_vma=False)
```

```python
import jax
import jax.numpy as jnp
from jax import lax
from jax.sharding import PartitionSpec as P

RADIUS = 3


penal_scale = -3.0 / 96.0


def with_halo(shard, sides, width):
    for axis, dim in sides:
        count, length = (lax.axis_size(axis), shard.shape[dim])
        up = [(i, (i + 1) % count) for i in range(count - 1)]
        down = [(j, i) for i, j in up]
        last = lax.slice_in_dim(shard, length - width, length, axis=dim)
        initial = lax.slice_in_dim(shard, 0, width, axis=dim)
        before = lax.ppermute(last, axis, up)
        after = lax.ppermute(initial, axis, down)
        shard = jnp.concatenate([before, shard, after], axis=dim)
    return shard


def recover(local_nodes, corner_vals, ratio_z):
    ex = local_nodes.shape[1] - 1
    ey = local_nodes.shape[2] - 1
    ratio_x = jnp.arange(ex + 1, dtype=jnp.float32) / ex
    ratio_y = jnp.arange(ey + 1, dtype=jnp.float32) / ey
    summed = local_nodes
    for corner in range(8):
        along_x = ratio_x if corner // 4 == 1 else 1.0 - ratio_x
        along_y = ratio_y if corner // 2 % 2 == 1 else 1.0 - ratio_y
        along_z = ratio_z if corner % 2 == 1 else 1.0 - ratio_z
        basis = along_x[:, None, None] * along_y[None, :, None] * along_z[None, None, :]
        summed = summed + basis[None] * corner_vals[:, corner][:, None, None, None]
    return summed


def average_rows(extended, dim, has_lower, has_upper):
    inner = extended.shape[dim] - 2
    own_rows = lax.slice_in_dim(extended, 1, inner + 1, axis=dim)
    rim_low = lax.slice_in_dim(extended, 0, 1, axis=dim)
    rim_high = lax.slice_in_dim(extended, inner + 1, inner + 2, axis=dim)
    shape_row = [1] * extended.ndim
    shape_row[dim] = inner
    rows = jnp.arange(inner, dtype=jnp.int32).reshape(shape_row)
    is_low = rows == 0
    is_high = rows == inner - 1
    factor = jnp.where(is_low & has_lower, 0.5, jnp.where(is_high & has_upper, 0.5, 1.0))
    rim_part = jnp.where(is_low, rim_low, 0.0) + jnp.where(is_high, rim_high, 0.0)
    return own_rows * factor + rim_part * 0.5


def element_energy(lower_nodes, upper_nodes, stiffness):
    ex = lower_nodes.shape[1] - 1
    ey = lower_nodes.shape[2] - 1

    def rows_energy(first_row):
        slab_low = lax.dynamic_slice_in_dim(lower_nodes, first_row, 5, axis=1)
        slab_up = lax.dynamic_slice_in_dim(upper_nodes, first_row, 5, axis=1)
        columns = []
        for corner in range(8):
            shift_x = corner // 4
            shift_y = corner // 2 % 2
            source = slab_up if corner % 2 == 1 else slab_low
            columns.append(source[:, shift_x : shift_x + 4, shift_y : shift_y + ey, :])
        vectors = jnp.stack(columns, axis=1)
        vectors = vectors.reshape((24,) + vectors.shape[2:])
        product = jnp.einsum(
            "ij,jabc->iabc",
            stiffness,
            vectors,
            precision=lax.Precision.HIGHEST,
            preferred_element_type=jnp.float32,
        )
        return jnp.sum(vectors * product, axis=0)

    energies = [rows_energy(first_row) for first_row in range(0, ex, 4)]
    return jnp.concatenate(energies, axis=0)


def block_energy(nodes, stiffness):
    ex, ey, ez = (nodes.shape[1] - 1, nodes.shape[2] - 1, nodes.shape[3] - 1)
    columns = []
    for corner in range(8):
        shift_x = corner // 4
        shift_y = corner // 2 % 2
        shift_z = corner % 2
        columns.append(nodes[:, shift_x : shift_x + ex, shift_y : shift_y + ey, shift_z : shift_z + ez])
    vectors = jnp.stack(columns, axis=1)
    vectors = vectors.reshape((24,) + vectors.shape[2:])
    product = jnp.einsum(
        "ij,jabc->iabc",
        stiffness,
        vectors,
        precision=lax.Precision.HIGHEST,
        preferred_element_type=jnp.float32,
    )
    return jnp.sum(vectors * product, axis=0)


def fix_faces(energy, averaged, stiffness):
    for dim in (1, 2, 3):
        count = energy.shape[dim - 1]
        for first in (0, count - 1):
            slab = lax.slice_in_dim(averaged, first, first + 2, axis=dim)
            energy = lax.dynamic_update_slice_in_dim(energy, block_energy(slab, stiffness), first, axis=dim - 1)
    return energy


def smooth(field, axis, count):
    summed = None
    for offset in range(-RADIUS, RADIUS + 1):
        term_piece = lax.slice_in_dim(field, RADIUS + offset, RADIUS + offset + count, axis=axis)
        term_value = float(RADIUS + 1 - abs(offset)) * term_piece
        summed = term_value if summed is None else summed + term_value
    return summed


def edge_counts(count, position, parts):
    places = position * count + jnp.arange(count, dtype=jnp.int32)
    summed = None
    for offset in range(-RADIUS, RADIUS + 1):
        inside = ((places + offset >= 0) & (places + offset < count * parts)).astype(jnp.float32)
        term_value = float(RADIUS + 1 - abs(offset)) * inside
        summed = term_value if summed is None else summed + term_value
    return summed


def filter_field(field, sides):
    for axis, dim in sides:
        padded = with_halo(field, ((axis, dim),), RADIUS)
        field = smooth(padded, dim, field.shape[dim])
    return field


def local(local_solution, top_nodes, coarse_solution, corner_dofs, density, element_stiffness):
    count_x, count_y, count_z = density.shape
    index_x = lax.axis_index("gx")
    index_y = lax.axis_index("gy")
    index_z = lax.axis_index("gz")
    normalizer = (
        edge_counts(count_x, index_x, lax.axis_size("gx"))[:, None, None]
        * edge_counts(count_y, index_y, lax.axis_size("gy"))[None, :, None]
        * edge_counts(count_z, index_z, lax.axis_size("gz"))[None, None, :]
    )
    sides = (("gx", 1), ("gy", 2), ("gz", 3))
    wanted = corner_dofs.reshape(8)
    parts = lax.axis_size("gz")
    spread = jnp.broadcast_to(coarse_solution[None], (parts,) + coarse_solution.shape)
    gathered = lax.all_to_all(spread, "gz", 0, 0, tiled=True)
    columns = gathered.transpose(1, 0, 2).reshape(coarse_solution.shape[0], -1)
    matches = wanted[:, None] == jnp.arange(columns.shape[1], dtype=jnp.int32)[None, :]
    corner_vals = jnp.sum(jnp.where(matches[None], columns[:, None, :], 0.0), axis=2)
    depth = local_solution.shape[3]
    full = jnp.concatenate([local_solution, top_nodes], axis=3)
    nodes = recover(full, corner_vals, jnp.arange(depth + 1, dtype=jnp.float32) / depth)
    lower_x = index_x > 0
    upper_x = index_x < lax.axis_size("gx") - 1
    lower_y = index_y > 0
    upper_y = index_y < lax.axis_size("gy") - 1
    lower_z = index_z > 0
    upper_z = index_z < lax.axis_size("gz") - 1
    extended = with_halo(nodes, (("gx", 1), ("gy", 2)), 1)
    extended = average_rows(extended, 1, lower_x, upper_x)
    averaged = average_rows(extended, 2, lower_y, upper_y)
    extended = with_halo(averaged, (("gz", 3),), 1)
    averaged = average_rows(extended, 3, lower_z, upper_z)
    interior = element_energy(nodes[:, :, :, :depth], nodes[:, :, :, 1:], element_stiffness)
    energy = fix_faces(interior, averaged, element_stiffness)
    sens = penal_scale * density * density * energy
    smoothed = filter_field(jnp.stack([density * sens, density]), sides)
    numerator = smoothed[0]
    smooth_density = smoothed[1]
    return (numerator / (density * normalizer), smooth_density / normalizer)


def solution(mesh):
    in_specs = (
        P(None, "gx", "gy", "gz"),
        P(None, "gx", "gy", "gz"),
        P(None, "gz"),
        P("gx", "gy", "gz", None),
        P("gx", "gy", "gz"),
        P(),
    )
    out_specs = (P("gx", "gy", "gz"), P("gx", "gy", "gz"))
    return jax.shard_map(local, mesh=mesh, in_specs=in_specs, out_specs=out_specs, check_vma=False)
```

```python
import functools

import jax
import jax.numpy as jnp
from jax import lax
from jax.sharding import PartitionSpec as P
from jax.experimental import pallas as pl
from jax.experimental.pallas import tpu as pltpu

RADIUS = 3


penal_scale = -3.0 / 96.0


def with_halo(shard, sides, width):
    for axis, dim in sides:
        count, length = (lax.axis_size(axis), shard.shape[dim])
        up = [(i, (i + 1) % count) for i in range(count - 1)]
        down = [(j, i) for i, j in up]
        last = lax.slice_in_dim(shard, length - width, length, axis=dim)
        initial = lax.slice_in_dim(shard, 0, width, axis=dim)
        before = lax.ppermute(last, axis, up)
        after = lax.ppermute(initial, axis, down)
        shard = jnp.concatenate([before, shard, after], axis=dim)
    return shard


def recover(local_nodes, corner_vals, ratio_z):
    ex = local_nodes.shape[1] - 1
    ey = local_nodes.shape[2] - 1
    ratio_x = jnp.arange(ex + 1, dtype=jnp.float32) / ex
    ratio_y = jnp.arange(ey + 1, dtype=jnp.float32) / ey
    summed = local_nodes
    for corner in range(8):
        along_x = ratio_x if corner // 4 == 1 else 1.0 - ratio_x
        along_y = ratio_y if corner // 2 % 2 == 1 else 1.0 - ratio_y
        along_z = ratio_z if corner % 2 == 1 else 1.0 - ratio_z
        basis = along_x[:, None, None] * along_y[None, :, None] * along_z[None, None, :]
        summed = summed + basis[None] * corner_vals[:, corner][:, None, None, None]
    return summed


def average_rows(extended, dim, has_lower, has_upper):
    inner = extended.shape[dim] - 2
    own_rows = lax.slice_in_dim(extended, 1, inner + 1, axis=dim)
    rim_low = lax.slice_in_dim(extended, 0, 1, axis=dim)
    rim_high = lax.slice_in_dim(extended, inner + 1, inner + 2, axis=dim)
    shape_row = [1] * extended.ndim
    shape_row[dim] = inner
    rows = jnp.arange(inner, dtype=jnp.int32).reshape(shape_row)
    is_low = rows == 0
    is_high = rows == inner - 1
    factor = jnp.where(is_low & has_lower, 0.5, jnp.where(is_high & has_upper, 0.5, 1.0))
    rim_part = jnp.where(is_low, rim_low, 0.0) + jnp.where(is_high, rim_high, 0.0)
    return own_rows * factor + rim_part * 0.5


def energy_kernel(weights, base, up_y, up_z, up_yz, out, *, count_x, chunks):
    sources = (base, up_z, up_y, up_yz)

    def row(i, carry):
        for first in chunks:
            vectors = []
            for component in range(3):
                for corner in range(8):
                    shift_x = corner // 4
                    source = sources[corner % 4]
                    vectors.append(source[component, i + shift_x, pl.ds(first, 8), :])
            total = None
            for a in range(24):
                inner = weights[a * 24 + a] * vectors[a]
                for b in range(a + 1, 24):
                    inner = inner + weights[a * 24 + b] * vectors[b]
                term = vectors[a] * inner
                total = term if total is None else total + term
            out[i, pl.ds(first, 8), :] = total
        return carry

    lax.fori_loop(0, count_x, row, 0)


def element_energy(nodes, stiffness):
    count_x = nodes.shape[1] - 1
    count_y = nodes.shape[2] - 1
    count_z = nodes.shape[3] - 1
    rows = -(-count_y // 8) * 8
    pad = ((0, 0), (0, 0), (0, rows - count_y), (0, 0))
    shifted = [
        jnp.pad(nodes[:, :, dy : dy + count_y, dz : dz + count_z], pad)
        for dy, dz in ((0, 0), (1, 0), (0, 1), (1, 1))
    ]
    upper = jnp.triu(stiffness + stiffness.T, 1) + jnp.diag(jnp.diagonal(stiffness))
    weights = upper.reshape(-1)
    kernel = functools.partial(energy_kernel, count_x=count_x, chunks=tuple(range(0, rows, 8)))
    vmem = pl.BlockSpec(memory_space=pltpu.VMEM)
    energy = pl.pallas_call(
        kernel,
        out_shape=jax.ShapeDtypeStruct((count_x, rows, count_z), jnp.float32),
        in_specs=[pl.BlockSpec(memory_space=pltpu.SMEM)] + [vmem] * 4,
        out_specs=vmem,
    )(weights, *shifted)
    return energy[:, :count_y, :]


def smooth(field, axis, count):
    summed = None
    for offset in range(-RADIUS, RADIUS + 1):
        term_piece = lax.slice_in_dim(field, RADIUS + offset, RADIUS + offset + count, axis=axis)
        term_value = float(RADIUS + 1 - abs(offset)) * term_piece
        summed = term_value if summed is None else summed + term_value
    return summed


def edge_counts(count, position, parts):
    places = position * count + jnp.arange(count, dtype=jnp.int32)
    summed = None
    for offset in range(-RADIUS, RADIUS + 1):
        inside = ((places + offset >= 0) & (places + offset < count * parts)).astype(jnp.float32)
        term_value = float(RADIUS + 1 - abs(offset)) * inside
        summed = term_value if summed is None else summed + term_value
    return summed


def filter_field(field, sides):
    for axis, dim in sides:
        padded = with_halo(field, ((axis, dim),), RADIUS)
        field = smooth(padded, dim, field.shape[dim])
    return field


def local(local_solution, top_nodes, coarse_solution, corner_dofs, density, element_stiffness):
    count_x, count_y, count_z = density.shape
    index_x = lax.axis_index("gx")
    index_y = lax.axis_index("gy")
    index_z = lax.axis_index("gz")
    normalizer = (
        edge_counts(count_x, index_x, lax.axis_size("gx"))[:, None, None]
        * edge_counts(count_y, index_y, lax.axis_size("gy"))[None, :, None]
        * edge_counts(count_z, index_z, lax.axis_size("gz"))[None, None, :]
    )
    sides = (("gx", 1), ("gy", 2), ("gz", 3))
    wanted = corner_dofs.reshape(8)
    parts = lax.axis_size("gz")
    spread = jnp.broadcast_to(coarse_solution[None], (parts,) + coarse_solution.shape)
    gathered = lax.all_to_all(spread, "gz", 0, 0, tiled=True)
    columns = gathered.transpose(1, 0, 2).reshape(coarse_solution.shape[0], -1)
    matches = wanted[:, None] == jnp.arange(columns.shape[1], dtype=jnp.int32)[None, :]
    corner_vals = jnp.sum(jnp.where(matches[None], columns[:, None, :], 0.0), axis=2)
    depth = local_solution.shape[3]
    full = jnp.concatenate([local_solution, top_nodes], axis=3)
    nodes = recover(full, corner_vals, jnp.arange(depth + 1, dtype=jnp.float32) / depth)
    lower_x = index_x > 0
    upper_x = index_x < lax.axis_size("gx") - 1
    lower_y = index_y > 0
    upper_y = index_y < lax.axis_size("gy") - 1
    lower_z = index_z > 0
    upper_z = index_z < lax.axis_size("gz") - 1
    extended = with_halo(nodes, (("gx", 1), ("gy", 2)), 1)
    extended = average_rows(extended, 1, lower_x, upper_x)
    averaged = average_rows(extended, 2, lower_y, upper_y)
    extended = with_halo(averaged, (("gz", 3),), 1)
    averaged = average_rows(extended, 3, lower_z, upper_z)
    energy = element_energy(averaged, element_stiffness)
    sens = penal_scale * density * density * energy
    smoothed = filter_field(jnp.stack([density * sens, density]), sides)
    numerator = smoothed[0]
    smooth_density = smoothed[1]
    return (numerator / (density * normalizer), smooth_density / normalizer)


def solution(mesh):
    in_specs = (
        P(None, "gx", "gy", "gz"),
        P(None, "gx", "gy", "gz"),
        P(None, "gz"),
        P("gx", "gy", "gz", None),
        P("gx", "gy", "gz"),
        P(),
    )
    out_specs = (P("gx", "gy", "gz"), P("gx", "gy", "gz"))
    return jax.shard_map(local, mesh=mesh, in_specs=in_specs, out_specs=out_specs, check_vma=False)
```

```python
import functools

import jax
import jax.numpy as jnp
from jax import lax
from jax.sharding import PartitionSpec as P
from jax.experimental import pallas as pl
from jax.experimental.pallas import tpu as pltpu

RADIUS = 3


penal_scale = -3.0 / 96.0


def halo_kernel(low, high, before, after, landed_before, landed_after, send_sem, recv_sem, *, axis, count):
    me = lax.axis_index(axis)
    has_lower = me > 0
    has_upper = me < count - 1
    mesh_ids = pl.DeviceIdType.MESH
    barrier = pltpu.get_barrier_semaphore()

    @pl.when(has_lower)
    def _():
        pl.semaphore_signal(barrier, 1, device_id={axis: me - 1}, device_id_type=mesh_ids)

    @pl.when(has_upper)
    def _():
        pl.semaphore_signal(barrier, 1, device_id={axis: me + 1}, device_id_type=mesh_ids)

    pl.semaphore_wait(barrier, has_lower.astype(jnp.int32) + has_upper.astype(jnp.int32))

    to_upper = pltpu.make_async_remote_copy(
        src_ref=high,
        dst_ref=landed_before,
        send_sem=send_sem.at[0],
        recv_sem=recv_sem.at[0],
        device_id={axis: me + 1},
        device_id_type=mesh_ids,
    )
    to_lower = pltpu.make_async_remote_copy(
        src_ref=low,
        dst_ref=landed_after,
        send_sem=send_sem.at[1],
        recv_sem=recv_sem.at[1],
        device_id={axis: me - 1},
        device_id_type=mesh_ids,
    )

    @pl.when(has_upper)
    def _():
        to_upper.start()

    @pl.when(has_lower)
    def _():
        to_lower.start()

    @pl.when(has_upper)
    def _():
        to_upper.wait_send()
        to_lower.wait_recv()
        after[...] = landed_after[...]

    @pl.when(has_lower)
    def _():
        to_lower.wait_send()
        to_upper.wait_recv()
        before[...] = landed_before[...]

    @pl.when(jnp.logical_not(has_upper))
    def _():
        after[...] = jnp.zeros(after.shape, after.dtype)

    @pl.when(jnp.logical_not(has_lower))
    def _():
        before[...] = jnp.zeros(before.shape, before.dtype)


HALO_IDS = {}


def exchange(low, high, axis):
    key = (axis, low.shape)
    if key not in HALO_IDS:
        HALO_IDS[key] = len(HALO_IDS)
    kernel = functools.partial(halo_kernel, axis=axis, count=lax.axis_size(axis))
    vmem = pl.BlockSpec(memory_space=pltpu.VMEM)
    slab = jax.ShapeDtypeStruct(low.shape, low.dtype)
    return pl.pallas_call(
        kernel,
        out_shape=(slab, slab),
        in_specs=[vmem, vmem],
        out_specs=(vmem, vmem),
        scratch_shapes=[
            pltpu.VMEM(low.shape, low.dtype),
            pltpu.VMEM(low.shape, low.dtype),
            pltpu.SemaphoreType.DMA((2,)),
            pltpu.SemaphoreType.DMA((2,)),
        ],
        compiler_params=pltpu.CompilerParams(collective_id=HALO_IDS[key], has_side_effects=True),
    )(low, high)


def with_halo(shard, sides, width):
    for axis, dim in sides:
        length = shard.shape[dim]
        last = lax.slice_in_dim(shard, length - width, length, axis=dim)
        initial = lax.slice_in_dim(shard, 0, width, axis=dim)
        before, after = exchange(initial, last, axis)
        shard = jnp.concatenate([before, shard, after], axis=dim)
    return shard


def recover(local_nodes, corner_vals, ratio_z):
    ex = local_nodes.shape[1] - 1
    ey = local_nodes.shape[2] - 1
    ratio_x = jnp.arange(ex + 1, dtype=jnp.float32) / ex
    ratio_y = jnp.arange(ey + 1, dtype=jnp.float32) / ey
    summed = local_nodes
    for corner in range(8):
        along_x = ratio_x if corner // 4 == 1 else 1.0 - ratio_x
        along_y = ratio_y if corner // 2 % 2 == 1 else 1.0 - ratio_y
        along_z = ratio_z if corner % 2 == 1 else 1.0 - ratio_z
        basis = along_x[:, None, None] * along_y[None, :, None] * along_z[None, None, :]
        summed = summed + basis[None] * corner_vals[:, corner][:, None, None, None]
    return summed


def average_rows(extended, dim, has_lower, has_upper):
    inner = extended.shape[dim] - 2
    own_rows = lax.slice_in_dim(extended, 1, inner + 1, axis=dim)
    rim_low = lax.slice_in_dim(extended, 0, 1, axis=dim)
    rim_high = lax.slice_in_dim(extended, inner + 1, inner + 2, axis=dim)
    shape_row = [1] * extended.ndim
    shape_row[dim] = inner
    rows = jnp.arange(inner, dtype=jnp.int32).reshape(shape_row)
    is_low = rows == 0
    is_high = rows == inner - 1
    factor = jnp.where(is_low & has_lower, 0.5, jnp.where(is_high & has_upper, 0.5, 1.0))
    rim_part = jnp.where(is_low, rim_low, 0.0) + jnp.where(is_high, rim_high, 0.0)
    return own_rows * factor + rim_part * 0.5


def energy_kernel(weights, base, up_y, up_z, up_yz, out, *, count_x, chunks):
    sources = (base, up_z, up_y, up_yz)

    def row(i, carry):
        for first in chunks:
            vectors = []
            for component in range(3):
                for corner in range(8):
                    shift_x = corner // 4
                    source = sources[corner % 4]
                    vectors.append(source[component, i + shift_x, pl.ds(first, 8), :])
            total = None
            for a in range(24):
                inner = weights[a * 24 + a] * vectors[a]
                for b in range(a + 1, 24):
                    inner = inner + weights[a * 24 + b] * vectors[b]
                term = vectors[a] * inner
                total = term if total is None else total + term
            out[i, pl.ds(first, 8), :] = total
        return carry

    lax.fori_loop(0, count_x, row, 0)


def element_energy(nodes, stiffness):
    count_x = nodes.shape[1] - 1
    count_y = nodes.shape[2] - 1
    count_z = nodes.shape[3] - 1
    rows = -(-count_y // 8) * 8
    pad = ((0, 0), (0, 0), (0, rows - count_y), (0, 0))
    shifted = [
        jnp.pad(nodes[:, :, dy : dy + count_y, dz : dz + count_z], pad)
        for dy, dz in ((0, 0), (1, 0), (0, 1), (1, 1))
    ]
    upper = jnp.triu(stiffness + stiffness.T, 1) + jnp.diag(jnp.diagonal(stiffness))
    weights = upper.reshape(-1)
    kernel = functools.partial(energy_kernel, count_x=count_x, chunks=tuple(range(0, rows, 8)))
    vmem = pl.BlockSpec(memory_space=pltpu.VMEM)
    energy = pl.pallas_call(
        kernel,
        out_shape=jax.ShapeDtypeStruct((count_x, rows, count_z), jnp.float32),
        in_specs=[pl.BlockSpec(memory_space=pltpu.SMEM)] + [vmem] * 4,
        out_specs=vmem,
    )(weights, *shifted)
    return energy[:, :count_y, :]


def smooth(field, axis, count):
    summed = None
    for offset in range(-RADIUS, RADIUS + 1):
        term_piece = lax.slice_in_dim(field, RADIUS + offset, RADIUS + offset + count, axis=axis)
        term_value = float(RADIUS + 1 - abs(offset)) * term_piece
        summed = term_value if summed is None else summed + term_value
    return summed


def edge_counts(count, position, parts):
    places = position * count + jnp.arange(count, dtype=jnp.int32)
    summed = None
    for offset in range(-RADIUS, RADIUS + 1):
        inside = ((places + offset >= 0) & (places + offset < count * parts)).astype(jnp.float32)
        term_value = float(RADIUS + 1 - abs(offset)) * inside
        summed = term_value if summed is None else summed + term_value
    return summed


def filter_field(field, sides):
    for axis, dim in sides:
        padded = with_halo(field, ((axis, dim),), RADIUS)
        field = smooth(padded, dim, field.shape[dim])
    return field


def local(local_solution, top_nodes, coarse_solution, corner_dofs, density, element_stiffness):
    count_x, count_y, count_z = density.shape
    index_x = lax.axis_index("gx")
    index_y = lax.axis_index("gy")
    index_z = lax.axis_index("gz")
    normalizer = (
        edge_counts(count_x, index_x, lax.axis_size("gx"))[:, None, None]
        * edge_counts(count_y, index_y, lax.axis_size("gy"))[None, :, None]
        * edge_counts(count_z, index_z, lax.axis_size("gz"))[None, None, :]
    )
    sides = (("gx", 1), ("gy", 2), ("gz", 3))
    wanted = corner_dofs.reshape(8)
    parts = lax.axis_size("gz")
    spread = jnp.broadcast_to(coarse_solution[None], (parts,) + coarse_solution.shape)
    gathered = lax.all_to_all(spread, "gz", 0, 0, tiled=True)
    columns = gathered.transpose(1, 0, 2).reshape(coarse_solution.shape[0], -1)
    matches = wanted[:, None] == jnp.arange(columns.shape[1], dtype=jnp.int32)[None, :]
    corner_vals = jnp.sum(jnp.where(matches[None], columns[:, None, :], 0.0), axis=2)
    depth = local_solution.shape[3]
    full = jnp.concatenate([local_solution, top_nodes], axis=3)
    nodes = recover(full, corner_vals, jnp.arange(depth + 1, dtype=jnp.float32) / depth)
    lower_x = index_x > 0
    upper_x = index_x < lax.axis_size("gx") - 1
    lower_y = index_y > 0
    upper_y = index_y < lax.axis_size("gy") - 1
    lower_z = index_z > 0
    upper_z = index_z < lax.axis_size("gz") - 1
    extended = with_halo(nodes, (("gx", 1), ("gy", 2)), 1)
    extended = average_rows(extended, 1, lower_x, upper_x)
    averaged = average_rows(extended, 2, lower_y, upper_y)
    extended = with_halo(averaged, (("gz", 3),), 1)
    averaged = average_rows(extended, 3, lower_z, upper_z)
    energy = element_energy(averaged, element_stiffness)
    sens = penal_scale * density * density * energy
    smoothed = filter_field(jnp.stack([density * sens, density]), sides)
    numerator = smoothed[0]
    smooth_density = smoothed[1]
    return (numerator / (density * normalizer), smooth_density / normalizer)


def solution(mesh):
    in_specs = (
        P(None, "gx", "gy", "gz"),
        P(None, "gx", "gy", "gz"),
        P(None, "gz"),
        P("gx", "gy", "gz", None),
        P("gx", "gy", "gz"),
        P(),
    )
    out_specs = (P("gx", "gy", "gz"), P("gx", "gy", "gz"))
    return jax.shard_map(local, mesh=mesh, in_specs=in_specs, out_specs=out_specs, check_vma=False)
```

```python
import functools

import jax
import jax.numpy as jnp
from jax import lax
from jax.sharding import PartitionSpec as P
from jax.experimental import pallas as pl
from jax.experimental.pallas import tpu as pltpu

RADIUS = 3


penal_scale = -3.0 / 96.0


def halo_kernel(low, high, before, after, landed_before, landed_after, send_sem, recv_sem, *, axis, count):
    me = lax.axis_index(axis)
    has_lower = me > 0
    has_upper = me < count - 1
    mesh_ids = pl.DeviceIdType.MESH
    barrier = pltpu.get_barrier_semaphore()

    @pl.when(has_lower)
    def _():
        pl.semaphore_signal(barrier, 1, device_id={axis: me - 1}, device_id_type=mesh_ids)

    @pl.when(has_upper)
    def _():
        pl.semaphore_signal(barrier, 1, device_id={axis: me + 1}, device_id_type=mesh_ids)

    pl.semaphore_wait(barrier, has_lower.astype(jnp.int32) + has_upper.astype(jnp.int32))

    to_upper = pltpu.make_async_remote_copy(
        src_ref=high,
        dst_ref=landed_before,
        send_sem=send_sem.at[0],
        recv_sem=recv_sem.at[0],
        device_id={axis: me + 1},
        device_id_type=mesh_ids,
    )
    to_lower = pltpu.make_async_remote_copy(
        src_ref=low,
        dst_ref=landed_after,
        send_sem=send_sem.at[1],
        recv_sem=recv_sem.at[1],
        device_id={axis: me - 1},
        device_id_type=mesh_ids,
    )

    @pl.when(has_upper)
    def _():
        to_upper.start()

    @pl.when(has_lower)
    def _():
        to_lower.start()

    @pl.when(has_upper)
    def _():
        to_upper.wait_send()
        to_lower.wait_recv()
        after[...] = landed_after[...]

    @pl.when(has_lower)
    def _():
        to_lower.wait_send()
        to_upper.wait_recv()
        before[...] = landed_before[...]

    @pl.when(jnp.logical_not(has_upper))
    def _():
        after[...] = jnp.zeros(after.shape, after.dtype)

    @pl.when(jnp.logical_not(has_lower))
    def _():
        before[...] = jnp.zeros(before.shape, before.dtype)


HALO_IDS = {}


def exchange(low, high, axis):
    key = (axis, low.shape)
    if key not in HALO_IDS:
        HALO_IDS[key] = len(HALO_IDS)
    kernel = functools.partial(halo_kernel, axis=axis, count=lax.axis_size(axis))
    vmem = pl.BlockSpec(memory_space=pltpu.VMEM)
    slab = jax.ShapeDtypeStruct(low.shape, low.dtype)
    return pl.pallas_call(
        kernel,
        out_shape=(slab, slab),
        in_specs=[vmem, vmem],
        out_specs=(vmem, vmem),
        scratch_shapes=[
            pltpu.VMEM(low.shape, low.dtype),
            pltpu.VMEM(low.shape, low.dtype),
            pltpu.SemaphoreType.DMA((2,)),
            pltpu.SemaphoreType.DMA((2,)),
        ],
        compiler_params=pltpu.CompilerParams(collective_id=HALO_IDS[key], has_side_effects=True),
    )(low, high)


def with_halo(shard, sides, width):
    for axis, dim in sides:
        length = shard.shape[dim]
        last = lax.slice_in_dim(shard, length - width, length, axis=dim)
        initial = lax.slice_in_dim(shard, 0, width, axis=dim)
        moved = jnp.moveaxis(initial, dim, 0).shape
        rows = (-1, moved[-1])
        before, after = exchange(
            jnp.moveaxis(initial, dim, 0).reshape(rows), jnp.moveaxis(last, dim, 0).reshape(rows), axis
        )
        before = jnp.moveaxis(before.reshape(moved), 0, dim)
        after = jnp.moveaxis(after.reshape(moved), 0, dim)
        shard = jnp.concatenate([before, shard, after], axis=dim)
    return shard


def recover(local_nodes, corner_vals, ratio_z):
    ex = local_nodes.shape[1] - 1
    ey = local_nodes.shape[2] - 1
    ratio_x = jnp.arange(ex + 1, dtype=jnp.float32) / ex
    ratio_y = jnp.arange(ey + 1, dtype=jnp.float32) / ey
    summed = local_nodes
    for corner in range(8):
        along_x = ratio_x if corner // 4 == 1 else 1.0 - ratio_x
        along_y = ratio_y if corner // 2 % 2 == 1 else 1.0 - ratio_y
        along_z = ratio_z if corner % 2 == 1 else 1.0 - ratio_z
        basis = along_x[:, None, None] * along_y[None, :, None] * along_z[None, None, :]
        summed = summed + basis[None] * corner_vals[:, corner][:, None, None, None]
    return summed


def average_rows(extended, dim, has_lower, has_upper):
    inner = extended.shape[dim] - 2
    own_rows = lax.slice_in_dim(extended, 1, inner + 1, axis=dim)
    rim_low = lax.slice_in_dim(extended, 0, 1, axis=dim)
    rim_high = lax.slice_in_dim(extended, inner + 1, inner + 2, axis=dim)
    shape_row = [1] * extended.ndim
    shape_row[dim] = inner
    rows = jnp.arange(inner, dtype=jnp.int32).reshape(shape_row)
    is_low = rows == 0
    is_high = rows == inner - 1
    factor = jnp.where(is_low & has_lower, 0.5, jnp.where(is_high & has_upper, 0.5, 1.0))
    rim_part = jnp.where(is_low, rim_low, 0.0) + jnp.where(is_high, rim_high, 0.0)
    return own_rows * factor + rim_part * 0.5


def energy_kernel(weights, base, up_y, up_z, up_yz, out, *, count_x, chunks):
    sources = (base, up_z, up_y, up_yz)

    def row(i, carry):
        for first in chunks:
            vectors = []
            for component in range(3):
                for corner in range(8):
                    shift_x = corner // 4
                    source = sources[corner % 4]
                    vectors.append(source[component, i + shift_x, pl.ds(first, 8), :])
            total = None
            for a in range(24):
                inner = weights[a * 24 + a] * vectors[a]
                for b in range(a + 1, 24):
                    inner = inner + weights[a * 24 + b] * vectors[b]
                term = vectors[a] * inner
                total = term if total is None else total + term
            out[i, pl.ds(first, 8), :] = total
        return carry

    lax.fori_loop(0, count_x, row, 0)


def element_energy(nodes, stiffness):
    count_x = nodes.shape[1] - 1
    count_y = nodes.shape[2] - 1
    count_z = nodes.shape[3] - 1
    rows = -(-count_y // 8) * 8
    pad = ((0, 0), (0, 0), (0, rows - count_y), (0, 0))
    shifted = [
        jnp.pad(nodes[:, :, dy : dy + count_y, dz : dz + count_z], pad)
        for dy, dz in ((0, 0), (1, 0), (0, 1), (1, 1))
    ]
    upper = jnp.triu(stiffness + stiffness.T, 1) + jnp.diag(jnp.diagonal(stiffness))
    weights = upper.reshape(-1)
    kernel = functools.partial(energy_kernel, count_x=count_x, chunks=tuple(range(0, rows, 8)))
    vmem = pl.BlockSpec(memory_space=pltpu.VMEM)
    energy = pl.pallas_call(
        kernel,
        out_shape=jax.ShapeDtypeStruct((count_x, rows, count_z), jnp.float32),
        in_specs=[pl.BlockSpec(memory_space=pltpu.SMEM)] + [vmem] * 4,
        out_specs=vmem,
    )(weights, *shifted)
    return energy[:, :count_y, :]


def smooth(field, axis, count):
    summed = None
    for offset in range(-RADIUS, RADIUS + 1):
        term_piece = lax.slice_in_dim(field, RADIUS + offset, RADIUS + offset + count, axis=axis)
        term_value = float(RADIUS + 1 - abs(offset)) * term_piece
        summed = term_value if summed is None else summed + term_value
    return summed


def edge_counts(count, position, parts):
    places = position * count + jnp.arange(count, dtype=jnp.int32)
    summed = None
    for offset in range(-RADIUS, RADIUS + 1):
        inside = ((places + offset >= 0) & (places + offset < count * parts)).astype(jnp.float32)
        term_value = float(RADIUS + 1 - abs(offset)) * inside
        summed = term_value if summed is None else summed + term_value
    return summed


def filter_field(field, sides):
    for axis, dim in sides:
        padded = with_halo(field, ((axis, dim),), RADIUS)
        field = smooth(padded, dim, field.shape[dim])
    return field


def local(local_solution, top_nodes, coarse_solution, corner_dofs, density, element_stiffness):
    count_x, count_y, count_z = density.shape
    index_x = lax.axis_index("gx")
    index_y = lax.axis_index("gy")
    index_z = lax.axis_index("gz")
    normalizer = (
        edge_counts(count_x, index_x, lax.axis_size("gx"))[:, None, None]
        * edge_counts(count_y, index_y, lax.axis_size("gy"))[None, :, None]
        * edge_counts(count_z, index_z, lax.axis_size("gz"))[None, None, :]
    )
    sides = (("gx", 1), ("gy", 2), ("gz", 3))
    wanted = corner_dofs.reshape(8)
    parts = lax.axis_size("gz")
    spread = jnp.broadcast_to(coarse_solution[None], (parts,) + coarse_solution.shape)
    gathered = lax.all_to_all(spread, "gz", 0, 0, tiled=True)
    columns = gathered.transpose(1, 0, 2).reshape(coarse_solution.shape[0], -1)
    matches = wanted[:, None] == jnp.arange(columns.shape[1], dtype=jnp.int32)[None, :]
    corner_vals = jnp.sum(jnp.where(matches[None], columns[:, None, :], 0.0), axis=2)
    depth = local_solution.shape[3]
    full = jnp.concatenate([local_solution, top_nodes], axis=3)
    nodes = recover(full, corner_vals, jnp.arange(depth + 1, dtype=jnp.float32) / depth)
    lower_x = index_x > 0
    upper_x = index_x < lax.axis_size("gx") - 1
    lower_y = index_y > 0
    upper_y = index_y < lax.axis_size("gy") - 1
    lower_z = index_z > 0
    upper_z = index_z < lax.axis_size("gz") - 1
    extended = with_halo(nodes, (("gx", 1), ("gy", 2)), 1)
    extended = average_rows(extended, 1, lower_x, upper_x)
    averaged = average_rows(extended, 2, lower_y, upper_y)
    extended = with_halo(averaged, (("gz", 3),), 1)
    averaged = average_rows(extended, 3, lower_z, upper_z)
    energy = element_energy(averaged, element_stiffness)
    sens = penal_scale * density * density * energy
    smoothed = filter_field(jnp.stack([density * sens, density]), sides)
    numerator = smoothed[0]
    smooth_density = smoothed[1]
    return (numerator / (density * normalizer), smooth_density / normalizer)


def solution(mesh):
    in_specs = (
        P(None, "gx", "gy", "gz"),
        P(None, "gx", "gy", "gz"),
        P(None, "gz"),
        P("gx", "gy", "gz", None),
        P("gx", "gy", "gz"),
        P(),
    )
    out_specs = (P("gx", "gy", "gz"), P("gx", "gy", "gz"))
    return jax.shard_map(local, mesh=mesh, in_specs=in_specs, out_specs=out_specs, check_vma=False)
```

```python
import functools

import jax
import jax.numpy as jnp
from jax import lax
from jax.sharding import PartitionSpec as P
from jax.experimental import pallas as pl
from jax.experimental.pallas import tpu as pltpu

RADIUS = 3


penal_scale = -3.0 / 96.0


def halo_kernel(low, high, before, after, landed_before, landed_after, send_sem, recv_sem, *, axis, count):
    me = lax.axis_index(axis)
    has_lower = me > 0
    has_upper = me < count - 1
    mesh_ids = pl.DeviceIdType.MESH
    barrier = pltpu.get_barrier_semaphore()

    @pl.when(has_lower)
    def _():
        pl.semaphore_signal(barrier, 1, device_id={axis: me - 1}, device_id_type=mesh_ids)

    @pl.when(has_upper)
    def _():
        pl.semaphore_signal(barrier, 1, device_id={axis: me + 1}, device_id_type=mesh_ids)

    pl.semaphore_wait(barrier, has_lower.astype(jnp.int32) + has_upper.astype(jnp.int32))

    to_upper = pltpu.make_async_remote_copy(
        src_ref=high,
        dst_ref=landed_before,
        send_sem=send_sem.at[0],
        recv_sem=recv_sem.at[0],
        device_id={axis: me + 1},
        device_id_type=mesh_ids,
    )
    to_lower = pltpu.make_async_remote_copy(
        src_ref=low,
        dst_ref=landed_after,
        send_sem=send_sem.at[1],
        recv_sem=recv_sem.at[1],
        device_id={axis: me - 1},
        device_id_type=mesh_ids,
    )

    @pl.when(has_upper)
    def _():
        to_upper.start()

    @pl.when(has_lower)
    def _():
        to_lower.start()

    @pl.when(has_upper)
    def _():
        to_upper.wait_send()
        to_lower.wait_recv()
        after[...] = landed_after[...]

    @pl.when(has_lower)
    def _():
        to_lower.wait_send()
        to_upper.wait_recv()
        before[...] = landed_before[...]

    @pl.when(jnp.logical_not(has_upper))
    def _():
        after[...] = jnp.zeros(after.shape, after.dtype)

    @pl.when(jnp.logical_not(has_lower))
    def _():
        before[...] = jnp.zeros(before.shape, before.dtype)


HALO_IDS = {}


def exchange(low, high, axis):
    key = (axis, low.shape)
    if key not in HALO_IDS:
        HALO_IDS[key] = len(HALO_IDS)
    kernel = functools.partial(halo_kernel, axis=axis, count=lax.axis_size(axis))
    vmem = pl.BlockSpec(memory_space=pltpu.VMEM)
    slab = jax.ShapeDtypeStruct(low.shape, low.dtype)
    return pl.pallas_call(
        kernel,
        out_shape=(slab, slab),
        in_specs=[vmem, vmem],
        out_specs=(vmem, vmem),
        scratch_shapes=[
            pltpu.VMEM(low.shape, low.dtype),
            pltpu.VMEM(low.shape, low.dtype),
            pltpu.SemaphoreType.DMA((2,)),
            pltpu.SemaphoreType.DMA((2,)),
        ],
        compiler_params=pltpu.CompilerParams(collective_id=HALO_IDS[key], has_side_effects=True),
    )(low, high)


def gather_kernel(shard, out, landed, send_sem, recv_sem, *, axis, count):
    me = lax.axis_index(axis)
    mesh_ids = pl.DeviceIdType.MESH
    barrier = pltpu.get_barrier_semaphore()
    for peer in range(count):

        @pl.when(peer != me)
        def _():
            pl.semaphore_signal(barrier, 1, device_id={axis: peer}, device_id_type=mesh_ids)

    pl.semaphore_wait(barrier, count - 1)
    copies = []
    for peer in range(count):
        copies.append(
            pltpu.make_async_remote_copy(
                src_ref=shard,
                dst_ref=landed.at[me],
                send_sem=send_sem.at[peer],
                recv_sem=recv_sem.at[me],
                device_id={axis: peer},
                device_id_type=mesh_ids,
            )
        )

        @pl.when(peer != me)
        def _():
            copies[peer].start()

    for peer in range(count):
        incoming = pltpu.make_async_remote_copy(
            src_ref=shard,
            dst_ref=landed.at[peer],
            send_sem=send_sem.at[peer],
            recv_sem=recv_sem.at[peer],
            device_id={axis: peer},
            device_id_type=mesh_ids,
        )

        @pl.when(peer != me)
        def _():
            copies[peer].wait_send()
            incoming.wait_recv()
            out[peer] = landed[peer]

    out[me] = shard[...]


def gather_peers(shard, axis):
    count = lax.axis_size(axis)
    kernel = functools.partial(gather_kernel, axis=axis, count=count)
    vmem = pl.BlockSpec(memory_space=pltpu.VMEM)
    stacked = (count,) + shard.shape
    return pl.pallas_call(
        kernel,
        out_shape=jax.ShapeDtypeStruct(stacked, shard.dtype),
        in_specs=[vmem],
        out_specs=vmem,
        scratch_shapes=[
            pltpu.VMEM(stacked, shard.dtype),
            pltpu.SemaphoreType.DMA((count,)),
            pltpu.SemaphoreType.DMA((count,)),
        ],
        compiler_params=pltpu.CompilerParams(collective_id=100, has_side_effects=True),
    )(shard)


def with_halo(shard, sides, width):
    for axis, dim in sides:
        length = shard.shape[dim]
        last = lax.slice_in_dim(shard, length - width, length, axis=dim)
        initial = lax.slice_in_dim(shard, 0, width, axis=dim)
        moved = jnp.moveaxis(initial, dim, 0).shape
        rows = (-1, moved[-1])
        before, after = exchange(
            jnp.moveaxis(initial, dim, 0).reshape(rows), jnp.moveaxis(last, dim, 0).reshape(rows), axis
        )
        before = jnp.moveaxis(before.reshape(moved), 0, dim)
        after = jnp.moveaxis(after.reshape(moved), 0, dim)
        shard = jnp.concatenate([before, shard, after], axis=dim)
    return shard


def recover(local_nodes, corner_vals, ratio_z):
    ex = local_nodes.shape[1] - 1
    ey = local_nodes.shape[2] - 1
    ratio_x = jnp.arange(ex + 1, dtype=jnp.float32) / ex
    ratio_y = jnp.arange(ey + 1, dtype=jnp.float32) / ey
    summed = local_nodes
    for corner in range(8):
        along_x = ratio_x if corner // 4 == 1 else 1.0 - ratio_x
        along_y = ratio_y if corner // 2 % 2 == 1 else 1.0 - ratio_y
        along_z = ratio_z if corner % 2 == 1 else 1.0 - ratio_z
        basis = along_x[:, None, None] * along_y[None, :, None] * along_z[None, None, :]
        summed = summed + basis[None] * corner_vals[:, corner][:, None, None, None]
    return summed


def average_rows(extended, dim, has_lower, has_upper):
    inner = extended.shape[dim] - 2
    own_rows = lax.slice_in_dim(extended, 1, inner + 1, axis=dim)
    rim_low = lax.slice_in_dim(extended, 0, 1, axis=dim)
    rim_high = lax.slice_in_dim(extended, inner + 1, inner + 2, axis=dim)
    shape_row = [1] * extended.ndim
    shape_row[dim] = inner
    rows = jnp.arange(inner, dtype=jnp.int32).reshape(shape_row)
    is_low = rows == 0
    is_high = rows == inner - 1
    factor = jnp.where(is_low & has_lower, 0.5, jnp.where(is_high & has_upper, 0.5, 1.0))
    rim_part = jnp.where(is_low, rim_low, 0.0) + jnp.where(is_high, rim_high, 0.0)
    return own_rows * factor + rim_part * 0.5


def energy_kernel(weights, shifted, out, *, count_x, chunks):
    sources = (shifted.at[0], shifted.at[2], shifted.at[1], shifted.at[3])

    def row(i, carry):
        for first in chunks:
            vectors = []
            for component in range(3):
                for corner in range(8):
                    shift_x = corner // 4
                    source = sources[corner % 4]
                    vectors.append(source[component, i + shift_x, pl.ds(first, 8), :])
            total = None
            for a in range(24):
                inner = weights[a * 24 + a] * vectors[a]
                for b in range(a + 1, 24):
                    inner = inner + weights[a * 24 + b] * vectors[b]
                term = vectors[a] * inner
                total = term if total is None else total + term
            out[i, pl.ds(first, 8), :] = total
        return carry

    lax.fori_loop(0, count_x, row, 0)


def element_energy(nodes, stiffness):
    count_x = nodes.shape[1] - 1
    count_y = nodes.shape[2] - 1
    count_z = nodes.shape[3] - 1
    rows = -(-count_y // 8) * 8
    pad = ((0, 0), (0, 0), (0, rows - count_y), (0, 0))
    shifted = jnp.stack(
        [
            jnp.pad(nodes[:, :, dy : dy + count_y, dz : dz + count_z], pad)
            for dy, dz in ((0, 0), (1, 0), (0, 1), (1, 1))
        ]
    )
    upper = jnp.triu(stiffness + stiffness.T, 1) + jnp.diag(jnp.diagonal(stiffness))
    weights = upper.reshape(-1)
    kernel = functools.partial(energy_kernel, count_x=count_x, chunks=tuple(range(0, rows, 8)))
    vmem = pl.BlockSpec(memory_space=pltpu.VMEM)
    energy = pl.pallas_call(
        kernel,
        out_shape=jax.ShapeDtypeStruct((count_x, rows, count_z), jnp.float32),
        in_specs=[pl.BlockSpec(memory_space=pltpu.SMEM), vmem],
        out_specs=vmem,
    )(weights, shifted)
    return energy[:, :count_y, :]


def smooth(field, axis, count):
    summed = None
    for offset in range(-RADIUS, RADIUS + 1):
        term_piece = lax.slice_in_dim(field, RADIUS + offset, RADIUS + offset + count, axis=axis)
        term_value = float(RADIUS + 1 - abs(offset)) * term_piece
        summed = term_value if summed is None else summed + term_value
    return summed


def edge_counts(count, position, parts):
    places = position * count + jnp.arange(count, dtype=jnp.int32)
    summed = None
    for offset in range(-RADIUS, RADIUS + 1):
        inside = ((places + offset >= 0) & (places + offset < count * parts)).astype(jnp.float32)
        term_value = float(RADIUS + 1 - abs(offset)) * inside
        summed = term_value if summed is None else summed + term_value
    return summed


def filter_field(field, sides):
    for axis, dim in sides:
        padded = with_halo(field, ((axis, dim),), RADIUS)
        field = smooth(padded, dim, field.shape[dim])
    return field


def local(local_solution, top_nodes, coarse_solution, corner_dofs, density, element_stiffness):
    count_x, count_y, count_z = density.shape
    index_x = lax.axis_index("gx")
    index_y = lax.axis_index("gy")
    index_z = lax.axis_index("gz")
    normalizer = (
        edge_counts(count_x, index_x, lax.axis_size("gx"))[:, None, None]
        * edge_counts(count_y, index_y, lax.axis_size("gy"))[None, :, None]
        * edge_counts(count_z, index_z, lax.axis_size("gz"))[None, None, :]
    )
    sides = (("gx", 1), ("gy", 2), ("gz", 3))
    wanted = corner_dofs.reshape(8)
    gathered = gather_peers(coarse_solution, "gz")
    columns = gathered.transpose(1, 0, 2).reshape(coarse_solution.shape[0], -1)
    matches = wanted[:, None] == jnp.arange(columns.shape[1], dtype=jnp.int32)[None, :]
    corner_vals = jnp.sum(jnp.where(matches[None], columns[:, None, :], 0.0), axis=2)
    depth = local_solution.shape[3]
    full = jnp.concatenate([local_solution, top_nodes], axis=3)
    nodes = recover(full, corner_vals, jnp.arange(depth + 1, dtype=jnp.float32) / depth)
    lower_x = index_x > 0
    upper_x = index_x < lax.axis_size("gx") - 1
    lower_y = index_y > 0
    upper_y = index_y < lax.axis_size("gy") - 1
    lower_z = index_z > 0
    upper_z = index_z < lax.axis_size("gz") - 1
    extended = with_halo(nodes, (("gx", 1), ("gy", 2)), 1)
    extended = average_rows(extended, 1, lower_x, upper_x)
    averaged = average_rows(extended, 2, lower_y, upper_y)
    extended = with_halo(averaged, (("gz", 3),), 1)
    averaged = average_rows(extended, 3, lower_z, upper_z)
    energy = element_energy(averaged, element_stiffness)
    sens = penal_scale * density * density * energy
    smoothed = filter_field(jnp.stack([density * sens, density]), sides)
    numerator = smoothed[0]
    smooth_density = smoothed[1]
    return (numerator / (density * normalizer), smooth_density / normalizer)


def solution(mesh):
    in_specs = (
        P(None, "gx", "gy", "gz"),
        P(None, "gx", "gy", "gz"),
        P(None, "gz"),
        P("gx", "gy", "gz", None),
        P("gx", "gy", "gz"),
        P(),
    )
    out_specs = (P("gx", "gy", "gz"), P("gx", "gy", "gz"))
    return jax.shard_map(local, mesh=mesh, in_specs=in_specs, out_specs=out_specs, check_vma=False)
```

```python
import functools
import math

import jax
import jax.numpy as jnp
from jax import lax
from jax.sharding import PartitionSpec as P
from jax.experimental import pallas as pl
from jax.experimental.pallas import tpu as pltpu

RADIUS = 3


penal_scale = -3.0 / 96.0


def halo_kernel(low, high, before, after, landed_before, landed_after, send_sem, recv_sem, *, axis, count):
    me = lax.axis_index(axis)
    has_lower = me > 0
    has_upper = me < count - 1
    mesh_ids = pl.DeviceIdType.MESH
    barrier = pltpu.get_barrier_semaphore()

    @pl.when(has_lower)
    def _():
        pl.semaphore_signal(barrier, 1, device_id={axis: me - 1}, device_id_type=mesh_ids)

    @pl.when(has_upper)
    def _():
        pl.semaphore_signal(barrier, 1, device_id={axis: me + 1}, device_id_type=mesh_ids)

    pl.semaphore_wait(barrier, has_lower.astype(jnp.int32) + has_upper.astype(jnp.int32))

    to_upper = pltpu.make_async_remote_copy(
        src_ref=high,
        dst_ref=landed_before,
        send_sem=send_sem.at[0],
        recv_sem=recv_sem.at[0],
        device_id={axis: me + 1},
        device_id_type=mesh_ids,
    )
    to_lower = pltpu.make_async_remote_copy(
        src_ref=low,
        dst_ref=landed_after,
        send_sem=send_sem.at[1],
        recv_sem=recv_sem.at[1],
        device_id={axis: me - 1},
        device_id_type=mesh_ids,
    )

    @pl.when(has_upper)
    def _():
        to_upper.start()

    @pl.when(has_lower)
    def _():
        to_lower.start()

    @pl.when(has_upper)
    def _():
        to_upper.wait_send()
        to_lower.wait_recv()
        after[...] = landed_after[...]

    @pl.when(has_lower)
    def _():
        to_lower.wait_send()
        to_upper.wait_recv()
        before[...] = landed_before[...]

    @pl.when(jnp.logical_not(has_upper))
    def _():
        after[...] = jnp.zeros(after.shape, after.dtype)

    @pl.when(jnp.logical_not(has_lower))
    def _():
        before[...] = jnp.zeros(before.shape, before.dtype)


HALO_IDS = {}


def exchange(low, high, axis):
    key = (axis, low.shape)
    if key not in HALO_IDS:
        HALO_IDS[key] = len(HALO_IDS)
    kernel = functools.partial(halo_kernel, axis=axis, count=lax.axis_size(axis))
    vmem = pl.BlockSpec(memory_space=pltpu.VMEM)
    slab = jax.ShapeDtypeStruct(low.shape, low.dtype)
    return pl.pallas_call(
        kernel,
        out_shape=(slab, slab),
        in_specs=[vmem, vmem],
        out_specs=(vmem, vmem),
        scratch_shapes=[
            pltpu.VMEM(low.shape, low.dtype),
            pltpu.VMEM(low.shape, low.dtype),
            pltpu.SemaphoreType.DMA((2,)),
            pltpu.SemaphoreType.DMA((2,)),
        ],
        compiler_params=pltpu.CompilerParams(collective_id=HALO_IDS[key], has_side_effects=True),
    )(low, high)


def gather_kernel(shard, out, landed, send_sem, recv_sem, *, axis, count):
    me = lax.axis_index(axis)
    mesh_ids = pl.DeviceIdType.MESH
    barrier = pltpu.get_barrier_semaphore()
    for peer in range(count):

        @pl.when(peer != me)
        def _():
            pl.semaphore_signal(barrier, 1, device_id={axis: peer}, device_id_type=mesh_ids)

    pl.semaphore_wait(barrier, count - 1)
    copies = []
    for peer in range(count):
        copies.append(
            pltpu.make_async_remote_copy(
                src_ref=shard,
                dst_ref=landed.at[me],
                send_sem=send_sem.at[peer],
                recv_sem=recv_sem.at[me],
                device_id={axis: peer},
                device_id_type=mesh_ids,
            )
        )

        @pl.when(peer != me)
        def _():
            copies[peer].start()

    for peer in range(count):
        incoming = pltpu.make_async_remote_copy(
            src_ref=shard,
            dst_ref=landed.at[peer],
            send_sem=send_sem.at[peer],
            recv_sem=recv_sem.at[peer],
            device_id={axis: peer},
            device_id_type=mesh_ids,
        )

        @pl.when(peer != me)
        def _():
            copies[peer].wait_send()
            incoming.wait_recv()
            out[peer] = landed[peer]

    out[me] = shard[...]


def gather_peers(shard, axis):
    count = lax.axis_size(axis)
    kernel = functools.partial(gather_kernel, axis=axis, count=count)
    vmem = pl.BlockSpec(memory_space=pltpu.VMEM)
    stacked = (count,) + shard.shape
    return pl.pallas_call(
        kernel,
        out_shape=jax.ShapeDtypeStruct(stacked, shard.dtype),
        in_specs=[vmem],
        out_specs=vmem,
        scratch_shapes=[
            pltpu.VMEM(stacked, shard.dtype),
            pltpu.SemaphoreType.DMA((count,)),
            pltpu.SemaphoreType.DMA((count,)),
        ],
        compiler_params=pltpu.CompilerParams(collective_id=100, has_side_effects=True),
    )(shard)


def with_halo(shard, sides, width):
    for axis, dim in sides:
        length = shard.shape[dim]
        last = lax.slice_in_dim(shard, length - width, length, axis=dim)
        initial = lax.slice_in_dim(shard, 0, width, axis=dim)
        tiled = math.prod(initial.shape[:-2]) * -(-initial.shape[-2] // 8) * 8 * -(-initial.shape[-1] // 128) * 128
        if tiled <= 3 * initial.size:
            before, after = exchange(initial, last, axis)
        else:
            moved = jnp.moveaxis(initial, dim, 0).shape
            rows = (-1, moved[-1])
            before, after = exchange(
                jnp.moveaxis(initial, dim, 0).reshape(rows), jnp.moveaxis(last, dim, 0).reshape(rows), axis
            )
            before = jnp.moveaxis(before.reshape(moved), 0, dim)
            after = jnp.moveaxis(after.reshape(moved), 0, dim)
        shard = jnp.concatenate([before, shard, after], axis=dim)
    return shard


def recover(local_nodes, corner_vals, ratio_z):
    ex = local_nodes.shape[1] - 1
    ey = local_nodes.shape[2] - 1
    ratio_x = jnp.arange(ex + 1, dtype=jnp.float32) / ex
    ratio_y = jnp.arange(ey + 1, dtype=jnp.float32) / ey
    summed = local_nodes
    for corner in range(8):
        along_x = ratio_x if corner // 4 == 1 else 1.0 - ratio_x
        along_y = ratio_y if corner // 2 % 2 == 1 else 1.0 - ratio_y
        along_z = ratio_z if corner % 2 == 1 else 1.0 - ratio_z
        basis = along_x[:, None, None] * along_y[None, :, None] * along_z[None, None, :]
        summed = summed + basis[None] * corner_vals[:, corner][:, None, None, None]
    return summed


def average_rows(extended, dim, has_lower, has_upper):
    inner = extended.shape[dim] - 2
    own_rows = lax.slice_in_dim(extended, 1, inner + 1, axis=dim)
    rim_low = lax.slice_in_dim(extended, 0, 1, axis=dim)
    rim_high = lax.slice_in_dim(extended, inner + 1, inner + 2, axis=dim)
    shape_row = [1] * extended.ndim
    shape_row[dim] = inner
    rows = jnp.arange(inner, dtype=jnp.int32).reshape(shape_row)
    is_low = rows == 0
    is_high = rows == inner - 1
    factor = jnp.where(is_low & has_lower, 0.5, jnp.where(is_high & has_upper, 0.5, 1.0))
    rim_part = jnp.where(is_low, rim_low, 0.0) + jnp.where(is_high, rim_high, 0.0)
    return own_rows * factor + rim_part * 0.5


def energy_kernel(weights, shifted, out, *, count_x, chunks):
    sources = (shifted.at[0], shifted.at[2], shifted.at[1], shifted.at[3])

    def row(i, carry):
        for first in chunks:
            vectors = []
            for component in range(3):
                for corner in range(8):
                    shift_x = corner // 4
                    source = sources[corner % 4]
                    vectors.append(source[component, i + shift_x, pl.ds(first, 8), :])
            total = None
            for a in range(24):
                inner = weights[a * 24 + a] * vectors[a]
                for b in range(a + 1, 24):
                    inner = inner + weights[a * 24 + b] * vectors[b]
                term = vectors[a] * inner
                total = term if total is None else total + term
            out[i, pl.ds(first, 8), :] = total
        return carry

    lax.fori_loop(0, count_x, row, 0)


def element_energy(nodes, stiffness):
    count_x = nodes.shape[1] - 1
    count_y = nodes.shape[2] - 1
    count_z = nodes.shape[3] - 1
    rows = -(-count_y // 8) * 8
    pad = ((0, 0), (0, 0), (0, rows - count_y), (0, 0))
    shifted = jnp.stack(
        [
            jnp.pad(nodes[:, :, dy : dy + count_y, dz : dz + count_z], pad)
            for dy, dz in ((0, 0), (1, 0), (0, 1), (1, 1))
        ]
    )
    upper = jnp.triu(stiffness + stiffness.T, 1) + jnp.diag(jnp.diagonal(stiffness))
    weights = upper.reshape(-1)
    kernel = functools.partial(energy_kernel, count_x=count_x, chunks=tuple(range(0, rows, 8)))
    vmem = pl.BlockSpec(memory_space=pltpu.VMEM)
    energy = pl.pallas_call(
        kernel,
        out_shape=jax.ShapeDtypeStruct((count_x, rows, count_z), jnp.float32),
        in_specs=[pl.BlockSpec(memory_space=pltpu.SMEM), vmem],
        out_specs=vmem,
    )(weights, shifted)
    return energy[:, :count_y, :]


def smooth(field, axis, count):
    summed = None
    for offset in range(-RADIUS, RADIUS + 1):
        term_piece = lax.slice_in_dim(field, RADIUS + offset, RADIUS + offset + count, axis=axis)
        term_value = float(RADIUS + 1 - abs(offset)) * term_piece
        summed = term_value if summed is None else summed + term_value
    return summed


def edge_counts(count, position, parts):
    places = position * count + jnp.arange(count, dtype=jnp.int32)
    summed = None
    for offset in range(-RADIUS, RADIUS + 1):
        inside = ((places + offset >= 0) & (places + offset < count * parts)).astype(jnp.float32)
        term_value = float(RADIUS + 1 - abs(offset)) * inside
        summed = term_value if summed is None else summed + term_value
    return summed


def filter_field(field, sides):
    for axis, dim in sides:
        padded = with_halo(field, ((axis, dim),), RADIUS)
        field = smooth(padded, dim, field.shape[dim])
    return field


def local(local_solution, top_nodes, coarse_solution, corner_dofs, density, element_stiffness):
    count_x, count_y, count_z = density.shape
    index_x = lax.axis_index("gx")
    index_y = lax.axis_index("gy")
    index_z = lax.axis_index("gz")
    normalizer = (
        edge_counts(count_x, index_x, lax.axis_size("gx"))[:, None, None]
        * edge_counts(count_y, index_y, lax.axis_size("gy"))[None, :, None]
        * edge_counts(count_z, index_z, lax.axis_size("gz"))[None, None, :]
    )
    sides = (("gx", 1), ("gy", 2), ("gz", 3))
    wanted = corner_dofs.reshape(8)
    gathered = gather_peers(coarse_solution, "gz")
    columns = gathered.transpose(1, 0, 2).reshape(coarse_solution.shape[0], -1)
    matches = wanted[:, None] == jnp.arange(columns.shape[1], dtype=jnp.int32)[None, :]
    corner_vals = jnp.sum(jnp.where(matches[None], columns[:, None, :], 0.0), axis=2)
    depth = local_solution.shape[3]
    full = jnp.concatenate([local_solution, top_nodes], axis=3)
    nodes = recover(full, corner_vals, jnp.arange(depth + 1, dtype=jnp.float32) / depth)
    lower_x = index_x > 0
    upper_x = index_x < lax.axis_size("gx") - 1
    lower_y = index_y > 0
    upper_y = index_y < lax.axis_size("gy") - 1
    lower_z = index_z > 0
    upper_z = index_z < lax.axis_size("gz") - 1
    extended = with_halo(nodes, (("gx", 1), ("gy", 2)), 1)
    extended = average_rows(extended, 1, lower_x, upper_x)
    averaged = average_rows(extended, 2, lower_y, upper_y)
    extended = with_halo(averaged, (("gz", 3),), 1)
    averaged = average_rows(extended, 3, lower_z, upper_z)
    energy = element_energy(averaged, element_stiffness)
    sens = penal_scale * density * density * energy
    smoothed = filter_field(jnp.stack([density * sens, density]), sides)
    numerator = smoothed[0]
    smooth_density = smoothed[1]
    return (numerator / (density * normalizer), smooth_density / normalizer)


def solution(mesh):
    in_specs = (
        P(None, "gx", "gy", "gz"),
        P(None, "gx", "gy", "gz"),
        P(None, "gz"),
        P("gx", "gy", "gz", None),
        P("gx", "gy", "gz"),
        P(),
    )
    out_specs = (P("gx", "gy", "gz"), P("gx", "gy", "gz"))
    return jax.shard_map(local, mesh=mesh, in_specs=in_specs, out_specs=out_specs, check_vma=False)
```

```python
import functools
import math

import jax
import jax.numpy as jnp
from jax import lax
from jax.sharding import PartitionSpec as P
from jax.experimental import pallas as pl
from jax.experimental.pallas import tpu as pltpu

RADIUS = 3


penal_scale = -3.0 / 96.0


def halo_kernel(low, high, before, after, landed_before, landed_after, send_sem, recv_sem, *, axis, count):
    me = lax.axis_index(axis)
    has_lower = me > 0
    has_upper = me < count - 1
    mesh_ids = pl.DeviceIdType.MESH
    barrier = pltpu.get_barrier_semaphore()

    @pl.when(has_lower)
    def _():
        pl.semaphore_signal(barrier, 1, device_id={axis: me - 1}, device_id_type=mesh_ids)

    @pl.when(has_upper)
    def _():
        pl.semaphore_signal(barrier, 1, device_id={axis: me + 1}, device_id_type=mesh_ids)

    pl.semaphore_wait(barrier, has_lower.astype(jnp.int32) + has_upper.astype(jnp.int32))

    to_upper = pltpu.make_async_remote_copy(
        src_ref=high,
        dst_ref=landed_before,
        send_sem=send_sem.at[0],
        recv_sem=recv_sem.at[0],
        device_id={axis: me + 1},
        device_id_type=mesh_ids,
    )
    to_lower = pltpu.make_async_remote_copy(
        src_ref=low,
        dst_ref=landed_after,
        send_sem=send_sem.at[1],
        recv_sem=recv_sem.at[1],
        device_id={axis: me - 1},
        device_id_type=mesh_ids,
    )

    @pl.when(has_upper)
    def _():
        to_upper.start()

    @pl.when(has_lower)
    def _():
        to_lower.start()

    @pl.when(has_upper)
    def _():
        to_upper.wait_send()
        to_lower.wait_recv()
        after[...] = landed_after[...]

    @pl.when(has_lower)
    def _():
        to_lower.wait_send()
        to_upper.wait_recv()
        before[...] = landed_before[...]

    @pl.when(jnp.logical_not(has_upper))
    def _():
        after[...] = jnp.zeros(after.shape, after.dtype)

    @pl.when(jnp.logical_not(has_lower))
    def _():
        before[...] = jnp.zeros(before.shape, before.dtype)


HALO_IDS = {}


def exchange(low, high, axis):
    key = (axis, low.shape)
    if key not in HALO_IDS:
        HALO_IDS[key] = len(HALO_IDS)
    kernel = functools.partial(halo_kernel, axis=axis, count=lax.axis_size(axis))
    vmem = pl.BlockSpec(memory_space=pltpu.VMEM)
    slab = jax.ShapeDtypeStruct(low.shape, low.dtype)
    return pl.pallas_call(
        kernel,
        out_shape=(slab, slab),
        in_specs=[vmem, vmem],
        out_specs=(vmem, vmem),
        scratch_shapes=[
            pltpu.VMEM(low.shape, low.dtype),
            pltpu.VMEM(low.shape, low.dtype),
            pltpu.SemaphoreType.DMA((2,)),
            pltpu.SemaphoreType.DMA((2,)),
        ],
        compiler_params=pltpu.CompilerParams(collective_id=HALO_IDS[key], has_side_effects=True),
    )(low, high)


def gather_kernel(shard, out, landed, send_sem, recv_sem, *, axis, count):
    me = lax.axis_index(axis)
    mesh_ids = pl.DeviceIdType.MESH
    barrier = pltpu.get_barrier_semaphore()
    for peer in range(count):

        @pl.when(peer != me)
        def _():
            pl.semaphore_signal(barrier, 1, device_id={axis: peer}, device_id_type=mesh_ids)

    pl.semaphore_wait(barrier, count - 1)
    copies = []
    for peer in range(count):
        copies.append(
            pltpu.make_async_remote_copy(
                src_ref=shard,
                dst_ref=landed.at[me],
                send_sem=send_sem.at[peer],
                recv_sem=recv_sem.at[me],
                device_id={axis: peer},
                device_id_type=mesh_ids,
            )
        )

        @pl.when(peer != me)
        def _():
            copies[peer].start()

    for peer in range(count):
        incoming = pltpu.make_async_remote_copy(
            src_ref=shard,
            dst_ref=landed.at[peer],
            send_sem=send_sem.at[peer],
            recv_sem=recv_sem.at[peer],
            device_id={axis: peer},
            device_id_type=mesh_ids,
        )

        @pl.when(peer != me)
        def _():
            copies[peer].wait_send()
            incoming.wait_recv()
            out[peer] = landed[peer]

    out[me] = shard[...]


def gather_peers(shard, axis):
    count = lax.axis_size(axis)
    kernel = functools.partial(gather_kernel, axis=axis, count=count)
    vmem = pl.BlockSpec(memory_space=pltpu.VMEM)
    stacked = (count,) + shard.shape
    return pl.pallas_call(
        kernel,
        out_shape=jax.ShapeDtypeStruct(stacked, shard.dtype),
        in_specs=[vmem],
        out_specs=vmem,
        scratch_shapes=[
            pltpu.VMEM(stacked, shard.dtype),
            pltpu.SemaphoreType.DMA((count,)),
            pltpu.SemaphoreType.DMA((count,)),
        ],
        compiler_params=pltpu.CompilerParams(collective_id=100, has_side_effects=True),
    )(shard)


def with_halo(shard, sides, width):
    for axis, dim in sides:
        length = shard.shape[dim]
        last = lax.slice_in_dim(shard, length - width, length, axis=dim)
        initial = lax.slice_in_dim(shard, 0, width, axis=dim)
        tiled = math.prod(initial.shape[:-2]) * -(-initial.shape[-2] // 8) * 8 * -(-initial.shape[-1] // 128) * 128
        if tiled <= 3 * initial.size:
            before, after = exchange(initial, last, axis)
        else:
            moved = jnp.moveaxis(initial, dim, 0).shape
            rows = (-1, moved[-1])
            before, after = exchange(
                jnp.moveaxis(initial, dim, 0).reshape(rows), jnp.moveaxis(last, dim, 0).reshape(rows), axis
            )
            before = jnp.moveaxis(before.reshape(moved), 0, dim)
            after = jnp.moveaxis(after.reshape(moved), 0, dim)
        shard = jnp.concatenate([before, shard, after], axis=dim)
    return shard


def recover(local_nodes, corner_vals, ratio_z):
    ex = local_nodes.shape[1] - 1
    ey = local_nodes.shape[2] - 1
    ratio_x = jnp.arange(ex + 1, dtype=jnp.float32) / ex
    ratio_y = jnp.arange(ey + 1, dtype=jnp.float32) / ey
    summed = local_nodes
    for corner in range(8):
        along_x = ratio_x if corner // 4 == 1 else 1.0 - ratio_x
        along_y = ratio_y if corner // 2 % 2 == 1 else 1.0 - ratio_y
        along_z = ratio_z if corner % 2 == 1 else 1.0 - ratio_z
        basis = along_x[:, None, None] * along_y[None, :, None] * along_z[None, None, :]
        summed = summed + basis[None] * corner_vals[:, corner][:, None, None, None]
    return summed


def average_rows(extended, dim, has_lower, has_upper):
    inner = extended.shape[dim] - 2
    own_rows = lax.slice_in_dim(extended, 1, inner + 1, axis=dim)
    rim_low = lax.slice_in_dim(extended, 0, 1, axis=dim)
    rim_high = lax.slice_in_dim(extended, inner + 1, inner + 2, axis=dim)
    shape_row = [1] * extended.ndim
    shape_row[dim] = inner
    rows = jnp.arange(inner, dtype=jnp.int32).reshape(shape_row)
    is_low = rows == 0
    is_high = rows == inner - 1
    factor = jnp.where(is_low & has_lower, 0.5, jnp.where(is_high & has_upper, 0.5, 1.0))
    rim_part = jnp.where(is_low, rim_low, 0.0) + jnp.where(is_high, rim_high, 0.0)
    return own_rows * factor + rim_part * 0.5


def energy_kernel(weights, shifted, out, *, count_x, chunks):
    sources = (shifted.at[0], shifted.at[2], shifted.at[1], shifted.at[3])

    def row(i, carry):
        for first in chunks:
            vectors = []
            for component in range(3):
                for corner in range(8):
                    shift_x = corner // 4
                    source = sources[corner % 4]
                    vectors.append(source[component, i + shift_x, pl.ds(first, 16), :])
            total = None
            for a in range(24):
                inner = weights[a * 24 + a] * vectors[a]
                for b in range(a + 1, 24):
                    inner = inner + weights[a * 24 + b] * vectors[b]
                term = vectors[a] * inner
                total = term if total is None else total + term
            out[i, pl.ds(first, 16), :] = total
        return carry

    lax.fori_loop(0, count_x, row, 0)


def element_energy(nodes, stiffness):
    count_x = nodes.shape[1] - 1
    count_y = nodes.shape[2] - 1
    count_z = nodes.shape[3] - 1
    rows = -(-count_y // 16) * 16
    pad = ((0, 0), (0, 0), (0, rows - count_y), (0, 0))
    shifted = jnp.stack(
        [
            jnp.pad(nodes[:, :, dy : dy + count_y, dz : dz + count_z], pad)
            for dy, dz in ((0, 0), (1, 0), (0, 1), (1, 1))
        ]
    )
    upper = jnp.triu(stiffness + stiffness.T, 1) + jnp.diag(jnp.diagonal(stiffness))
    weights = upper.reshape(-1)
    kernel = functools.partial(energy_kernel, count_x=count_x, chunks=tuple(range(0, rows, 16)))
    vmem = pl.BlockSpec(memory_space=pltpu.VMEM)
    energy = pl.pallas_call(
        kernel,
        out_shape=jax.ShapeDtypeStruct((count_x, rows, count_z), jnp.float32),
        in_specs=[pl.BlockSpec(memory_space=pltpu.SMEM), vmem],
        out_specs=vmem,
    )(weights, shifted)
    return energy[:, :count_y, :]


def smooth(field, axis, count):
    summed = None
    for offset in range(-RADIUS, RADIUS + 1):
        term_piece = lax.slice_in_dim(field, RADIUS + offset, RADIUS + offset + count, axis=axis)
        term_value = float(RADIUS + 1 - abs(offset)) * term_piece
        summed = term_value if summed is None else summed + term_value
    return summed


def edge_counts(count, position, parts):
    places = position * count + jnp.arange(count, dtype=jnp.int32)
    summed = None
    for offset in range(-RADIUS, RADIUS + 1):
        inside = ((places + offset >= 0) & (places + offset < count * parts)).astype(jnp.float32)
        term_value = float(RADIUS + 1 - abs(offset)) * inside
        summed = term_value if summed is None else summed + term_value
    return summed


def filter_field(field, sides):
    for axis, dim in sides:
        padded = with_halo(field, ((axis, dim),), RADIUS)
        field = smooth(padded, dim, field.shape[dim])
    return field


def local(local_solution, top_nodes, coarse_solution, corner_dofs, density, element_stiffness):
    count_x, count_y, count_z = density.shape
    index_x = lax.axis_index("gx")
    index_y = lax.axis_index("gy")
    index_z = lax.axis_index("gz")
    normalizer = (
        edge_counts(count_x, index_x, lax.axis_size("gx"))[:, None, None]
        * edge_counts(count_y, index_y, lax.axis_size("gy"))[None, :, None]
        * edge_counts(count_z, index_z, lax.axis_size("gz"))[None, None, :]
    )
    sides = (("gx", 1), ("gy", 2), ("gz", 3))
    wanted = corner_dofs.reshape(8)
    gathered = gather_peers(coarse_solution, "gz")
    columns = gathered.transpose(1, 0, 2).reshape(coarse_solution.shape[0], -1)
    matches = wanted[:, None] == jnp.arange(columns.shape[1], dtype=jnp.int32)[None, :]
    corner_vals = jnp.sum(jnp.where(matches[None], columns[:, None, :], 0.0), axis=2)
    depth = local_solution.shape[3]
    full = jnp.concatenate([local_solution, top_nodes], axis=3)
    nodes = recover(full, corner_vals, jnp.arange(depth + 1, dtype=jnp.float32) / depth)
    lower_x = index_x > 0
    upper_x = index_x < lax.axis_size("gx") - 1
    lower_y = index_y > 0
    upper_y = index_y < lax.axis_size("gy") - 1
    lower_z = index_z > 0
    upper_z = index_z < lax.axis_size("gz") - 1
    extended = with_halo(nodes, (("gx", 1), ("gy", 2)), 1)
    extended = average_rows(extended, 1, lower_x, upper_x)
    averaged = average_rows(extended, 2, lower_y, upper_y)
    extended = with_halo(averaged, (("gz", 3),), 1)
    averaged = average_rows(extended, 3, lower_z, upper_z)
    energy = element_energy(averaged, element_stiffness)
    sens = penal_scale * density * density * energy
    smoothed = filter_field(jnp.stack([density * sens, density]), sides)
    numerator = smoothed[0]
    smooth_density = smoothed[1]
    return (numerator / (density * normalizer), smooth_density / normalizer)


def solution(mesh):
    in_specs = (
        P(None, "gx", "gy", "gz"),
        P(None, "gx", "gy", "gz"),
        P(None, "gz"),
        P("gx", "gy", "gz", None),
        P("gx", "gy", "gz"),
        P(),
    )
    out_specs = (P("gx", "gy", "gz"), P("gx", "gy", "gz"))
    return jax.shard_map(local, mesh=mesh, in_specs=in_specs, out_specs=out_specs, check_vma=False)
```

```python
import functools
import math

import jax
import jax.numpy as jnp
from jax import lax
from jax.sharding import PartitionSpec as P
from jax.experimental import pallas as pl
from jax.experimental.pallas import tpu as pltpu

RADIUS = 3


penal_scale = -3.0 / 96.0


def halo_kernel(low, high, before, after, landed_before, landed_after, send_sem, recv_sem, *, axis, count):
    me = lax.axis_index(axis)
    has_lower = me > 0
    has_upper = me < count - 1
    mesh_ids = pl.DeviceIdType.MESH
    barrier = pltpu.get_barrier_semaphore()

    @pl.when(has_lower)
    def _():
        pl.semaphore_signal(barrier, 1, device_id={axis: me - 1}, device_id_type=mesh_ids)

    @pl.when(has_upper)
    def _():
        pl.semaphore_signal(barrier, 1, device_id={axis: me + 1}, device_id_type=mesh_ids)

    pl.semaphore_wait(barrier, has_lower.astype(jnp.int32) + has_upper.astype(jnp.int32))

    to_upper = pltpu.make_async_remote_copy(
        src_ref=high,
        dst_ref=landed_before,
        send_sem=send_sem.at[0],
        recv_sem=recv_sem.at[0],
        device_id={axis: me + 1},
        device_id_type=mesh_ids,
    )
    to_lower = pltpu.make_async_remote_copy(
        src_ref=low,
        dst_ref=landed_after,
        send_sem=send_sem.at[1],
        recv_sem=recv_sem.at[1],
        device_id={axis: me - 1},
        device_id_type=mesh_ids,
    )

    @pl.when(has_upper)
    def _():
        to_upper.start()

    @pl.when(has_lower)
    def _():
        to_lower.start()

    @pl.when(has_upper)
    def _():
        to_upper.wait_send()
        to_lower.wait_recv()
        after[...] = landed_after[...]

    @pl.when(has_lower)
    def _():
        to_lower.wait_send()
        to_upper.wait_recv()
        before[...] = landed_before[...]

    @pl.when(jnp.logical_not(has_upper))
    def _():
        after[...] = jnp.zeros(after.shape, after.dtype)

    @pl.when(jnp.logical_not(has_lower))
    def _():
        before[...] = jnp.zeros(before.shape, before.dtype)


HALO_IDS = {}


def exchange(low, high, axis):
    key = (axis, low.shape)
    if key not in HALO_IDS:
        HALO_IDS[key] = len(HALO_IDS)
    kernel = functools.partial(halo_kernel, axis=axis, count=lax.axis_size(axis))
    vmem = pl.BlockSpec(memory_space=pltpu.VMEM)
    slab = jax.ShapeDtypeStruct(low.shape, low.dtype)
    return pl.pallas_call(
        kernel,
        out_shape=(slab, slab),
        in_specs=[vmem, vmem],
        out_specs=(vmem, vmem),
        scratch_shapes=[
            pltpu.VMEM(low.shape, low.dtype),
            pltpu.VMEM(low.shape, low.dtype),
            pltpu.SemaphoreType.DMA((2,)),
            pltpu.SemaphoreType.DMA((2,)),
        ],
        compiler_params=pltpu.CompilerParams(collective_id=HALO_IDS[key], has_side_effects=True),
    )(low, high)


def gather_kernel(shard, out, landed, send_sem, recv_sem, *, axis, count):
    me = lax.axis_index(axis)
    mesh_ids = pl.DeviceIdType.MESH
    barrier = pltpu.get_barrier_semaphore()
    for peer in range(count):

        @pl.when(peer != me)
        def _():
            pl.semaphore_signal(barrier, 1, device_id={axis: peer}, device_id_type=mesh_ids)

    pl.semaphore_wait(barrier, count - 1)
    copies = []
    for peer in range(count):
        copies.append(
            pltpu.make_async_remote_copy(
                src_ref=shard,
                dst_ref=landed.at[me],
                send_sem=send_sem.at[peer],
                recv_sem=recv_sem.at[me],
                device_id={axis: peer},
                device_id_type=mesh_ids,
            )
        )

        @pl.when(peer != me)
        def _():
            copies[peer].start()

    for peer in range(count):
        incoming = pltpu.make_async_remote_copy(
            src_ref=shard,
            dst_ref=landed.at[peer],
            send_sem=send_sem.at[peer],
            recv_sem=recv_sem.at[peer],
            device_id={axis: peer},
            device_id_type=mesh_ids,
        )

        @pl.when(peer != me)
        def _():
            copies[peer].wait_send()
            incoming.wait_recv()
            out[peer] = landed[peer]

    out[me] = shard[...]


def gather_peers(shard, axis):
    count = lax.axis_size(axis)
    kernel = functools.partial(gather_kernel, axis=axis, count=count)
    vmem = pl.BlockSpec(memory_space=pltpu.VMEM)
    stacked = (count,) + shard.shape
    return pl.pallas_call(
        kernel,
        out_shape=jax.ShapeDtypeStruct(stacked, shard.dtype),
        in_specs=[vmem],
        out_specs=vmem,
        scratch_shapes=[
            pltpu.VMEM(stacked, shard.dtype),
            pltpu.SemaphoreType.DMA((count,)),
            pltpu.SemaphoreType.DMA((count,)),
        ],
        compiler_params=pltpu.CompilerParams(collective_id=100, has_side_effects=True),
    )(shard)


def plane_kernel(*refs, axes, sizes, offsets):
    count = len(offsets)
    sends = refs[:count]
    outs = refs[count : 2 * count]
    landed = refs[2 * count : 3 * count]
    send_sem, recv_sem = refs[3 * count :]
    me = [lax.axis_index(axis) for axis in axes]
    mesh_ids = pl.DeviceIdType.MESH

    def exists(offset):
        inside = None
        for position, step, size in zip(me, offset, sizes):
            if step == 0:
                continue
            here = (position + step >= 0) & (position + step < size)
            inside = here if inside is None else inside & here
        return inside

    def target(offset):
        return {axis: position + step for axis, position, step in zip(axes, me, offset)}

    barrier = pltpu.get_barrier_semaphore()
    expected = 0
    for offset in offsets:

        @pl.when(exists(offset))
        def _():
            pl.semaphore_signal(barrier, 1, device_id=target(offset), device_id_type=mesh_ids)

        expected = expected + exists(offset).astype(jnp.int32)
    pl.semaphore_wait(barrier, expected)
    slot = {offset: k for k, offset in enumerate(offsets)}
    outgoing = []
    for k, offset in enumerate(offsets):
        back = slot[tuple(-step for step in offset)]
        outgoing.append(
            pltpu.make_async_remote_copy(
                src_ref=sends[k],
                dst_ref=landed[back],
                send_sem=send_sem.at[k],
                recv_sem=recv_sem.at[back],
                device_id=target(offset),
                device_id_type=mesh_ids,
            )
        )

        @pl.when(exists(offset))
        def _():
            outgoing[k].start()

    for k, offset in enumerate(offsets):
        back = slot[tuple(-step for step in offset)]
        incoming = pltpu.make_async_remote_copy(
            src_ref=sends[back],
            dst_ref=landed[k],
            send_sem=send_sem.at[back],
            recv_sem=recv_sem.at[k],
            device_id=target(offset),
            device_id_type=mesh_ids,
        )

        @pl.when(exists(offset))
        def _():
            outgoing[k].wait_send()
            incoming.wait_recv()
            outs[k][...] = landed[k][...]

        @pl.when(jnp.logical_not(exists(offset)))
        def _():
            outs[k][...] = jnp.zeros(outs[k].shape, outs[k].dtype)


def as_rows(piece, thin):
    tiled = math.prod(piece.shape[:-2]) * -(-piece.shape[-2] // 8) * 8 * -(-piece.shape[-1] // 128) * 128
    if tiled <= 3 * piece.size:
        return piece, None
    moved = jnp.moveaxis(piece, thin, tuple(range(len(thin))))
    return moved.reshape(-1, moved.shape[-1]), moved.shape


def from_rows(piece, moved, thin):
    if moved is None:
        return piece
    return jnp.moveaxis(piece.reshape(moved), tuple(range(len(thin))), thin)


def with_plane_halo(shard, axes, dims, width):
    offsets = [(ox, oy) for ox in (-1, 0, 1) for oy in (-1, 0, 1) if (ox, oy) != (0, 0)]
    pieces = []
    layouts = []
    for offset in offsets:
        piece = shard
        thin = []
        for step, dim in zip(offset, dims):
            length = piece.shape[dim]
            if step == 1:
                piece = lax.slice_in_dim(piece, length - width, length, axis=dim)
            elif step == -1:
                piece = lax.slice_in_dim(piece, 0, width, axis=dim)
            if step != 0:
                thin.append(dim)
        piece, moved = as_rows(piece, thin)
        pieces.append(piece)
        layouts.append((moved, thin))
    key = ("plane",) + tuple(piece.shape for piece in pieces)
    if key not in HALO_IDS:
        HALO_IDS[key] = len(HALO_IDS)
    sizes = tuple(lax.axis_size(axis) for axis in axes)
    kernel = functools.partial(plane_kernel, axes=axes, sizes=sizes, offsets=tuple(offsets))
    vmem = pl.BlockSpec(memory_space=pltpu.VMEM)
    shapes = tuple(jax.ShapeDtypeStruct(piece.shape, piece.dtype) for piece in pieces)
    received = pl.pallas_call(
        kernel,
        out_shape=shapes,
        in_specs=[vmem] * len(pieces),
        out_specs=tuple([vmem] * len(pieces)),
        scratch_shapes=[pltpu.VMEM(piece.shape, piece.dtype) for piece in pieces]
        + [pltpu.SemaphoreType.DMA((len(pieces),)), pltpu.SemaphoreType.DMA((len(pieces),))],
        compiler_params=pltpu.CompilerParams(collective_id=HALO_IDS[key], has_side_effects=True),
    )(*pieces)
    got = {offset: from_rows(piece, *layout) for offset, piece, layout in zip(offsets, received, layouts)}
    got[(0, 0)] = shard
    rows = []
    for ox in (-1, 0, 1):
        rows.append(jnp.concatenate([got[(ox, oy)] for oy in (-1, 0, 1)], axis=dims[1]))
    return jnp.concatenate(rows, axis=dims[0])


def with_halo(shard, sides, width):
    for axis, dim in sides:
        length = shard.shape[dim]
        last = lax.slice_in_dim(shard, length - width, length, axis=dim)
        initial = lax.slice_in_dim(shard, 0, width, axis=dim)
        tiled = math.prod(initial.shape[:-2]) * -(-initial.shape[-2] // 8) * 8 * -(-initial.shape[-1] // 128) * 128
        if tiled <= 3 * initial.size:
            before, after = exchange(initial, last, axis)
        else:
            moved = jnp.moveaxis(initial, dim, 0).shape
            rows = (-1, moved[-1])
            before, after = exchange(
                jnp.moveaxis(initial, dim, 0).reshape(rows), jnp.moveaxis(last, dim, 0).reshape(rows), axis
            )
            before = jnp.moveaxis(before.reshape(moved), 0, dim)
            after = jnp.moveaxis(after.reshape(moved), 0, dim)
        shard = jnp.concatenate([before, shard, after], axis=dim)
    return shard


def recover(local_nodes, corner_vals, ratio_z):
    ex = local_nodes.shape[1] - 1
    ey = local_nodes.shape[2] - 1
    ratio_x = jnp.arange(ex + 1, dtype=jnp.float32) / ex
    ratio_y = jnp.arange(ey + 1, dtype=jnp.float32) / ey
    summed = local_nodes
    for corner in range(8):
        along_x = ratio_x if corner // 4 == 1 else 1.0 - ratio_x
        along_y = ratio_y if corner // 2 % 2 == 1 else 1.0 - ratio_y
        along_z = ratio_z if corner % 2 == 1 else 1.0 - ratio_z
        basis = along_x[:, None, None] * along_y[None, :, None] * along_z[None, None, :]
        summed = summed + basis[None] * corner_vals[:, corner][:, None, None, None]
    return summed


def average_rows(extended, dim, has_lower, has_upper):
    inner = extended.shape[dim] - 2
    own_rows = lax.slice_in_dim(extended, 1, inner + 1, axis=dim)
    rim_low = lax.slice_in_dim(extended, 0, 1, axis=dim)
    rim_high = lax.slice_in_dim(extended, inner + 1, inner + 2, axis=dim)
    shape_row = [1] * extended.ndim
    shape_row[dim] = inner
    rows = jnp.arange(inner, dtype=jnp.int32).reshape(shape_row)
    is_low = rows == 0
    is_high = rows == inner - 1
    factor = jnp.where(is_low & has_lower, 0.5, jnp.where(is_high & has_upper, 0.5, 1.0))
    rim_part = jnp.where(is_low, rim_low, 0.0) + jnp.where(is_high, rim_high, 0.0)
    return own_rows * factor + rim_part * 0.5


def energy_kernel(weights, shifted, out, *, count_x, chunks):
    sources = (shifted.at[0], shifted.at[2], shifted.at[1], shifted.at[3])

    def row(i, carry):
        for first in chunks:
            vectors = []
            for component in range(3):
                for corner in range(8):
                    shift_x = corner // 4
                    source = sources[corner % 4]
                    vectors.append(source[component, i + shift_x, pl.ds(first, 8), :])
            total = None
            for a in range(24):
                inner = weights[a * 24 + a] * vectors[a]
                for b in range(a + 1, 24):
                    inner = inner + weights[a * 24 + b] * vectors[b]
                term = vectors[a] * inner
                total = term if total is None else total + term
            out[i, pl.ds(first, 8), :] = total
        return carry

    lax.fori_loop(0, count_x, row, 0)


def element_energy(nodes, stiffness):
    count_x = nodes.shape[1] - 1
    count_y = nodes.shape[2] - 1
    count_z = nodes.shape[3] - 1
    rows = -(-count_y // 8) * 8
    pad = ((0, 0), (0, 0), (0, rows - count_y), (0, 0))
    shifted = jnp.stack(
        [
            jnp.pad(nodes[:, :, dy : dy + count_y, dz : dz + count_z], pad)
            for dy, dz in ((0, 0), (1, 0), (0, 1), (1, 1))
        ]
    )
    upper = jnp.triu(stiffness + stiffness.T, 1) + jnp.diag(jnp.diagonal(stiffness))
    weights = upper.reshape(-1)
    kernel = functools.partial(energy_kernel, count_x=count_x, chunks=tuple(range(0, rows, 8)))
    vmem = pl.BlockSpec(memory_space=pltpu.VMEM)
    energy = pl.pallas_call(
        kernel,
        out_shape=jax.ShapeDtypeStruct((count_x, rows, count_z), jnp.float32),
        in_specs=[pl.BlockSpec(memory_space=pltpu.SMEM), vmem],
        out_specs=vmem,
    )(weights, shifted)
    return energy[:, :count_y, :]


def smooth(field, axis, count):
    summed = None
    for offset in range(-RADIUS, RADIUS + 1):
        term_piece = lax.slice_in_dim(field, RADIUS + offset, RADIUS + offset + count, axis=axis)
        term_value = float(RADIUS + 1 - abs(offset)) * term_piece
        summed = term_value if summed is None else summed + term_value
    return summed


def edge_counts(count, position, parts):
    places = position * count + jnp.arange(count, dtype=jnp.int32)
    summed = None
    for offset in range(-RADIUS, RADIUS + 1):
        inside = ((places + offset >= 0) & (places + offset < count * parts)).astype(jnp.float32)
        term_value = float(RADIUS + 1 - abs(offset)) * inside
        summed = term_value if summed is None else summed + term_value
    return summed


def filter_field(field, sides):
    (axis_x, dim_x), (axis_y, dim_y), (axis_z, dim_z) = sides
    count_x, count_y = field.shape[dim_x], field.shape[dim_y]
    padded = with_plane_halo(field, (axis_x, axis_y), (dim_x, dim_y), RADIUS)
    field = smooth(smooth(padded, dim_x, count_x), dim_y, count_y)
    padded = with_halo(field, ((axis_z, dim_z),), RADIUS)
    return smooth(padded, dim_z, field.shape[dim_z])


def local(local_solution, top_nodes, coarse_solution, corner_dofs, density, element_stiffness):
    count_x, count_y, count_z = density.shape
    index_x = lax.axis_index("gx")
    index_y = lax.axis_index("gy")
    index_z = lax.axis_index("gz")
    normalizer = (
        edge_counts(count_x, index_x, lax.axis_size("gx"))[:, None, None]
        * edge_counts(count_y, index_y, lax.axis_size("gy"))[None, :, None]
        * edge_counts(count_z, index_z, lax.axis_size("gz"))[None, None, :]
    )
    sides = (("gx", 1), ("gy", 2), ("gz", 3))
    wanted = corner_dofs.reshape(8)
    gathered = gather_peers(coarse_solution, "gz")
    columns = gathered.transpose(1, 0, 2).reshape(coarse_solution.shape[0], -1)
    matches = wanted[:, None] == jnp.arange(columns.shape[1], dtype=jnp.int32)[None, :]
    corner_vals = jnp.sum(jnp.where(matches[None], columns[:, None, :], 0.0), axis=2)
    depth = local_solution.shape[3]
    full = jnp.concatenate([local_solution, top_nodes], axis=3)
    nodes = recover(full, corner_vals, jnp.arange(depth + 1, dtype=jnp.float32) / depth)
    lower_x = index_x > 0
    upper_x = index_x < lax.axis_size("gx") - 1
    lower_y = index_y > 0
    upper_y = index_y < lax.axis_size("gy") - 1
    lower_z = index_z > 0
    upper_z = index_z < lax.axis_size("gz") - 1
    extended = with_plane_halo(nodes, ("gx", "gy"), (1, 2), 1)
    extended = average_rows(extended, 1, lower_x, upper_x)
    averaged = average_rows(extended, 2, lower_y, upper_y)
    extended = with_halo(averaged, (("gz", 3),), 1)
    averaged = average_rows(extended, 3, lower_z, upper_z)
    energy = element_energy(averaged, element_stiffness)
    sens = penal_scale * density * density * energy
    smoothed = filter_field(jnp.stack([density * sens, density]), sides)
    numerator = smoothed[0]
    smooth_density = smoothed[1]
    return (numerator / (density * normalizer), smooth_density / normalizer)


def solution(mesh):
    in_specs = (
        P(None, "gx", "gy", "gz"),
        P(None, "gx", "gy", "gz"),
        P(None, "gz"),
        P("gx", "gy", "gz", None),
        P("gx", "gy", "gz"),
        P(),
    )
    out_specs = (P("gx", "gy", "gz"), P("gx", "gy", "gz"))
    return jax.shard_map(local, mesh=mesh, in_specs=in_specs, out_specs=out_specs, check_vma=False)
```

```python
import functools
import math

import jax
import jax.numpy as jnp
from jax import lax
from jax.sharding import PartitionSpec as P
from jax.experimental import pallas as pl
from jax.experimental.pallas import tpu as pltpu

RADIUS = 3


penal_scale = -3.0 / 96.0


def halo_kernel(low, high, before, after, landed_before, landed_after, send_sem, recv_sem, *, axis, count):
    me = lax.axis_index(axis)
    has_lower = me > 0
    has_upper = me < count - 1
    mesh_ids = pl.DeviceIdType.MESH
    barrier = pltpu.get_barrier_semaphore()

    @pl.when(has_lower)
    def _():
        pl.semaphore_signal(barrier, 1, device_id={axis: me - 1}, device_id_type=mesh_ids)

    @pl.when(has_upper)
    def _():
        pl.semaphore_signal(barrier, 1, device_id={axis: me + 1}, device_id_type=mesh_ids)

    pl.semaphore_wait(barrier, has_lower.astype(jnp.int32) + has_upper.astype(jnp.int32))

    to_upper = pltpu.make_async_remote_copy(
        src_ref=high,
        dst_ref=landed_before,
        send_sem=send_sem.at[0],
        recv_sem=recv_sem.at[0],
        device_id={axis: me + 1},
        device_id_type=mesh_ids,
    )
    to_lower = pltpu.make_async_remote_copy(
        src_ref=low,
        dst_ref=landed_after,
        send_sem=send_sem.at[1],
        recv_sem=recv_sem.at[1],
        device_id={axis: me - 1},
        device_id_type=mesh_ids,
    )

    @pl.when(has_upper)
    def _():
        to_upper.start()

    @pl.when(has_lower)
    def _():
        to_lower.start()

    @pl.when(has_upper)
    def _():
        to_upper.wait_send()
        to_lower.wait_recv()
        after[...] = landed_after[...]

    @pl.when(has_lower)
    def _():
        to_lower.wait_send()
        to_upper.wait_recv()
        before[...] = landed_before[...]

    @pl.when(jnp.logical_not(has_upper))
    def _():
        after[...] = jnp.zeros(after.shape, after.dtype)

    @pl.when(jnp.logical_not(has_lower))
    def _():
        before[...] = jnp.zeros(before.shape, before.dtype)


HALO_IDS = {}


def exchange(low, high, axis):
    key = (axis, low.shape)
    if key not in HALO_IDS:
        HALO_IDS[key] = len(HALO_IDS)
    kernel = functools.partial(halo_kernel, axis=axis, count=lax.axis_size(axis))
    vmem = pl.BlockSpec(memory_space=pltpu.VMEM)
    slab = jax.ShapeDtypeStruct(low.shape, low.dtype)
    return pl.pallas_call(
        kernel,
        out_shape=(slab, slab),
        in_specs=[vmem, vmem],
        out_specs=(vmem, vmem),
        scratch_shapes=[
            pltpu.VMEM(low.shape, low.dtype),
            pltpu.VMEM(low.shape, low.dtype),
            pltpu.SemaphoreType.DMA((2,)),
            pltpu.SemaphoreType.DMA((2,)),
        ],
        compiler_params=pltpu.CompilerParams(collective_id=HALO_IDS[key], has_side_effects=True),
    )(low, high)


def gather_kernel(shard, out, landed, send_sem, recv_sem, *, axis, count):
    me = lax.axis_index(axis)
    mesh_ids = pl.DeviceIdType.MESH
    barrier = pltpu.get_barrier_semaphore()
    for peer in range(count):

        @pl.when(peer != me)
        def _():
            pl.semaphore_signal(barrier, 1, device_id={axis: peer}, device_id_type=mesh_ids)

    pl.semaphore_wait(barrier, count - 1)
    copies = []
    for peer in range(count):
        copies.append(
            pltpu.make_async_remote_copy(
                src_ref=shard,
                dst_ref=landed.at[me],
                send_sem=send_sem.at[peer],
                recv_sem=recv_sem.at[me],
                device_id={axis: peer},
                device_id_type=mesh_ids,
            )
        )

        @pl.when(peer != me)
        def _():
            copies[peer].start()

    for peer in range(count):
        incoming = pltpu.make_async_remote_copy(
            src_ref=shard,
            dst_ref=landed.at[peer],
            send_sem=send_sem.at[peer],
            recv_sem=recv_sem.at[peer],
            device_id={axis: peer},
            device_id_type=mesh_ids,
        )

        @pl.when(peer != me)
        def _():
            copies[peer].wait_send()
            incoming.wait_recv()
            out[peer] = landed[peer]

    out[me] = shard[...]


def gather_peers(shard, axis):
    count = lax.axis_size(axis)
    kernel = functools.partial(gather_kernel, axis=axis, count=count)
    vmem = pl.BlockSpec(memory_space=pltpu.VMEM)
    stacked = (count,) + shard.shape
    return pl.pallas_call(
        kernel,
        out_shape=jax.ShapeDtypeStruct(stacked, shard.dtype),
        in_specs=[vmem],
        out_specs=vmem,
        scratch_shapes=[
            pltpu.VMEM(stacked, shard.dtype),
            pltpu.SemaphoreType.DMA((count,)),
            pltpu.SemaphoreType.DMA((count,)),
        ],
        compiler_params=pltpu.CompilerParams(collective_id=100, has_side_effects=True),
    )(shard)


def plane_kernel(*refs, axes, sizes, offsets):
    count = len(offsets)
    sends = refs[:count]
    outs = refs[count : 2 * count]
    landed = refs[2 * count : 3 * count]
    send_sem, recv_sem = refs[3 * count :]
    me = [lax.axis_index(axis) for axis in axes]
    mesh_ids = pl.DeviceIdType.MESH

    def exists(offset):
        inside = None
        for position, step, size in zip(me, offset, sizes):
            if step == 0:
                continue
            here = (position + step >= 0) & (position + step < size)
            inside = here if inside is None else inside & here
        return inside

    def target(offset):
        return {axis: position + step for axis, position, step in zip(axes, me, offset)}

    barrier = pltpu.get_barrier_semaphore()
    expected = 0
    for offset in offsets:

        @pl.when(exists(offset))
        def _():
            pl.semaphore_signal(barrier, 1, device_id=target(offset), device_id_type=mesh_ids)

        expected = expected + exists(offset).astype(jnp.int32)
    pl.semaphore_wait(barrier, expected)
    slot = {offset: k for k, offset in enumerate(offsets)}
    outgoing = []
    for k, offset in enumerate(offsets):
        back = slot[tuple(-step for step in offset)]
        outgoing.append(
            pltpu.make_async_remote_copy(
                src_ref=sends[k],
                dst_ref=landed[back],
                send_sem=send_sem.at[k],
                recv_sem=recv_sem.at[back],
                device_id=target(offset),
                device_id_type=mesh_ids,
            )
        )

        @pl.when(exists(offset))
        def _():
            outgoing[k].start()

    for k, offset in enumerate(offsets):
        back = slot[tuple(-step for step in offset)]
        incoming = pltpu.make_async_remote_copy(
            src_ref=sends[back],
            dst_ref=landed[k],
            send_sem=send_sem.at[back],
            recv_sem=recv_sem.at[k],
            device_id=target(offset),
            device_id_type=mesh_ids,
        )

        @pl.when(exists(offset))
        def _():
            outgoing[k].wait_send()
            incoming.wait_recv()
            outs[k][...] = landed[k][...]

        @pl.when(jnp.logical_not(exists(offset)))
        def _():
            outs[k][...] = jnp.zeros(outs[k].shape, outs[k].dtype)


def as_rows(piece, thin):
    tiled = math.prod(piece.shape[:-2]) * -(-piece.shape[-2] // 8) * 8 * -(-piece.shape[-1] // 128) * 128
    if tiled <= 3 * piece.size:
        return piece, None
    moved = jnp.moveaxis(piece, thin, tuple(range(len(thin))))
    return moved.reshape(-1, moved.shape[-1]), moved.shape


def from_rows(piece, moved, thin):
    if moved is None:
        return piece
    return jnp.moveaxis(piece.reshape(moved), tuple(range(len(thin))), thin)


def with_plane_halo(shard, axes, dims, width):
    offsets = [(ox, oy) for ox in (-1, 0, 1) for oy in (-1, 0, 1) if (ox, oy) != (0, 0)]
    pieces = []
    layouts = []
    for offset in offsets:
        piece = shard
        thin = []
        for step, dim in zip(offset, dims):
            length = piece.shape[dim]
            if step == 1:
                piece = lax.slice_in_dim(piece, length - width, length, axis=dim)
            elif step == -1:
                piece = lax.slice_in_dim(piece, 0, width, axis=dim)
            if step != 0:
                thin.append(dim)
        piece, moved = as_rows(piece, thin)
        pieces.append(piece)
        layouts.append((moved, thin))
    key = ("plane",) + tuple(piece.shape for piece in pieces)
    if key not in HALO_IDS:
        HALO_IDS[key] = len(HALO_IDS)
    sizes = tuple(lax.axis_size(axis) for axis in axes)
    kernel = functools.partial(plane_kernel, axes=axes, sizes=sizes, offsets=tuple(offsets))
    vmem = pl.BlockSpec(memory_space=pltpu.VMEM)
    shapes = tuple(jax.ShapeDtypeStruct(piece.shape, piece.dtype) for piece in pieces)
    received = pl.pallas_call(
        kernel,
        out_shape=shapes,
        in_specs=[vmem] * len(pieces),
        out_specs=tuple([vmem] * len(pieces)),
        scratch_shapes=[pltpu.VMEM(piece.shape, piece.dtype) for piece in pieces]
        + [pltpu.SemaphoreType.DMA((len(pieces),)), pltpu.SemaphoreType.DMA((len(pieces),))],
        compiler_params=pltpu.CompilerParams(collective_id=HALO_IDS[key], has_side_effects=True),
    )(*pieces)
    got = {offset: from_rows(piece, *layout) for offset, piece, layout in zip(offsets, received, layouts)}
    got[(0, 0)] = shard
    rows = []
    for ox in (-1, 0, 1):
        rows.append(jnp.concatenate([got[(ox, oy)] for oy in (-1, 0, 1)], axis=dims[1]))
    return jnp.concatenate(rows, axis=dims[0])


def with_halo(shard, sides, width):
    for axis, dim in sides:
        length = shard.shape[dim]
        last = lax.slice_in_dim(shard, length - width, length, axis=dim)
        initial = lax.slice_in_dim(shard, 0, width, axis=dim)
        tiled = math.prod(initial.shape[:-2]) * -(-initial.shape[-2] // 8) * 8 * -(-initial.shape[-1] // 128) * 128
        if tiled <= 3 * initial.size:
            before, after = exchange(initial, last, axis)
        else:
            moved = jnp.moveaxis(initial, dim, 0).shape
            rows = (-1, moved[-1])
            before, after = exchange(
                jnp.moveaxis(initial, dim, 0).reshape(rows), jnp.moveaxis(last, dim, 0).reshape(rows), axis
            )
            before = jnp.moveaxis(before.reshape(moved), 0, dim)
            after = jnp.moveaxis(after.reshape(moved), 0, dim)
        shard = jnp.concatenate([before, shard, after], axis=dim)
    return shard


def recover(local_nodes, corner_vals, ratio_z):
    ex = local_nodes.shape[1] - 1
    ey = local_nodes.shape[2] - 1
    ratio_x = jnp.arange(ex + 1, dtype=jnp.float32) / ex
    ratio_y = jnp.arange(ey + 1, dtype=jnp.float32) / ey
    planes = []
    for high_z in (0, 1):
        plane = None
        for corner in range(high_z, 8, 2):
            along_x = ratio_x if corner // 4 == 1 else 1.0 - ratio_x
            along_y = ratio_y if corner // 2 % 2 == 1 else 1.0 - ratio_y
            basis = along_x[:, None] * along_y[None, :]
            term = basis[None] * corner_vals[:, corner][:, None, None]
            plane = term if plane is None else plane + term
        planes.append(plane[:, :, :, None])
    return local_nodes + planes[0] * (1.0 - ratio_z) + planes[1] * ratio_z


def average_rows(extended, dim, has_lower, has_upper):
    inner = extended.shape[dim] - 2
    own_rows = lax.slice_in_dim(extended, 1, inner + 1, axis=dim)
    rim_low = lax.slice_in_dim(extended, 0, 1, axis=dim)
    rim_high = lax.slice_in_dim(extended, inner + 1, inner + 2, axis=dim)
    shape_row = [1] * extended.ndim
    shape_row[dim] = inner
    rows = jnp.arange(inner, dtype=jnp.int32).reshape(shape_row)
    is_low = rows == 0
    is_high = rows == inner - 1
    factor = jnp.where(is_low & has_lower, 0.5, jnp.where(is_high & has_upper, 0.5, 1.0))
    rim_part = jnp.where(is_low, rim_low, 0.0) + jnp.where(is_high, rim_high, 0.0)
    return own_rows * factor + rim_part * 0.5


def energy_kernel(weights, shifted, out, *, count_x, chunks):
    sources = (shifted.at[0], shifted.at[2], shifted.at[1], shifted.at[3])

    def row(i, carry):
        for first in chunks:
            vectors = []
            for component in range(3):
                for corner in range(8):
                    shift_x = corner // 4
                    source = sources[corner % 4]
                    vectors.append(source[component, i + shift_x, pl.ds(first, 8), :])
            total = None
            for a in range(24):
                inner = weights[a * 24 + a] * vectors[a]
                for b in range(a + 1, 24):
                    inner = inner + weights[a * 24 + b] * vectors[b]
                term = vectors[a] * inner
                total = term if total is None else total + term
            out[i, pl.ds(first, 8), :] = total
        return carry

    lax.fori_loop(0, count_x, row, 0)


def element_energy(nodes, stiffness):
    count_x = nodes.shape[1] - 1
    count_y = nodes.shape[2] - 1
    count_z = nodes.shape[3] - 1
    rows = -(-count_y // 8) * 8
    pad = ((0, 0), (0, 0), (0, rows - count_y), (0, 0))
    shifted = jnp.stack(
        [
            jnp.pad(nodes[:, :, dy : dy + count_y, dz : dz + count_z], pad)
            for dy, dz in ((0, 0), (1, 0), (0, 1), (1, 1))
        ]
    )
    upper = jnp.triu(stiffness + stiffness.T, 1) + jnp.diag(jnp.diagonal(stiffness))
    weights = upper.reshape(-1)
    kernel = functools.partial(energy_kernel, count_x=count_x, chunks=tuple(range(0, rows, 8)))
    vmem = pl.BlockSpec(memory_space=pltpu.VMEM)
    energy = pl.pallas_call(
        kernel,
        out_shape=jax.ShapeDtypeStruct((count_x, rows, count_z), jnp.float32),
        in_specs=[pl.BlockSpec(memory_space=pltpu.SMEM), vmem],
        out_specs=vmem,
    )(weights, shifted)
    return energy[:, :count_y, :]


def smooth(field, axis, count):
    summed = None
    for offset in range(-RADIUS, RADIUS + 1):
        term_piece = lax.slice_in_dim(field, RADIUS + offset, RADIUS + offset + count, axis=axis)
        term_value = float(RADIUS + 1 - abs(offset)) * term_piece
        summed = term_value if summed is None else summed + term_value
    return summed


def edge_counts(count, position, parts):
    places = position * count + jnp.arange(count, dtype=jnp.int32)
    summed = None
    for offset in range(-RADIUS, RADIUS + 1):
        inside = ((places + offset >= 0) & (places + offset < count * parts)).astype(jnp.float32)
        term_value = float(RADIUS + 1 - abs(offset)) * inside
        summed = term_value if summed is None else summed + term_value
    return summed


def filter_field(field, sides):
    (axis_x, dim_x), (axis_y, dim_y), (axis_z, dim_z) = sides
    count_x, count_y = field.shape[dim_x], field.shape[dim_y]
    padded = with_plane_halo(field, (axis_x, axis_y), (dim_x, dim_y), RADIUS)
    field = smooth(smooth(padded, dim_x, count_x), dim_y, count_y)
    padded = with_halo(field, ((axis_z, dim_z),), RADIUS)
    return smooth(padded, dim_z, field.shape[dim_z])


def local(local_solution, top_nodes, coarse_solution, corner_dofs, density, element_stiffness):
    count_x, count_y, count_z = density.shape
    index_x = lax.axis_index("gx")
    index_y = lax.axis_index("gy")
    index_z = lax.axis_index("gz")
    normalizer = (
        edge_counts(count_x, index_x, lax.axis_size("gx"))[:, None, None]
        * edge_counts(count_y, index_y, lax.axis_size("gy"))[None, :, None]
        * edge_counts(count_z, index_z, lax.axis_size("gz"))[None, None, :]
    )
    sides = (("gx", 1), ("gy", 2), ("gz", 3))
    wanted = corner_dofs.reshape(8)
    gathered = gather_peers(coarse_solution, "gz")
    columns = gathered.transpose(1, 0, 2).reshape(coarse_solution.shape[0], -1)
    matches = wanted[:, None] == jnp.arange(columns.shape[1], dtype=jnp.int32)[None, :]
    corner_vals = jnp.sum(jnp.where(matches[None], columns[:, None, :], 0.0), axis=2)
    depth = local_solution.shape[3]
    full = jnp.concatenate([local_solution, top_nodes], axis=3)
    nodes = recover(full, corner_vals, jnp.arange(depth + 1, dtype=jnp.float32) / depth)
    lower_x = index_x > 0
    upper_x = index_x < lax.axis_size("gx") - 1
    lower_y = index_y > 0
    upper_y = index_y < lax.axis_size("gy") - 1
    lower_z = index_z > 0
    upper_z = index_z < lax.axis_size("gz") - 1
    extended = with_plane_halo(nodes, ("gx", "gy"), (1, 2), 1)
    extended = average_rows(extended, 1, lower_x, upper_x)
    averaged = average_rows(extended, 2, lower_y, upper_y)
    extended = with_halo(averaged, (("gz", 3),), 1)
    averaged = average_rows(extended, 3, lower_z, upper_z)
    energy = element_energy(averaged, element_stiffness)
    sens = penal_scale * density * density * energy
    smoothed = filter_field(jnp.stack([density * sens, density]), sides)
    numerator = smoothed[0]
    smooth_density = smoothed[1]
    return (numerator / (density * normalizer), smooth_density / normalizer)


def solution(mesh):
    in_specs = (
        P(None, "gx", "gy", "gz"),
        P(None, "gx", "gy", "gz"),
        P(None, "gz"),
        P("gx", "gy", "gz", None),
        P("gx", "gy", "gz"),
        P(),
    )
    out_specs = (P("gx", "gy", "gz"), P("gx", "gy", "gz"))
    return jax.shard_map(local, mesh=mesh, in_specs=in_specs, out_specs=out_specs, check_vma=False)
```

```python
import functools
import math

import jax
import jax.numpy as jnp
from jax import lax
from jax.sharding import PartitionSpec as P
from jax.experimental import pallas as pl
from jax.experimental.pallas import tpu as pltpu

RADIUS = 3


penal_scale = -3.0 / 96.0


def halo_kernel(low, high, before, after, landed_before, landed_after, send_sem, recv_sem, *, axis, count):
    me = lax.axis_index(axis)
    has_lower = me > 0
    has_upper = me < count - 1
    mesh_ids = pl.DeviceIdType.MESH
    barrier = pltpu.get_barrier_semaphore()

    @pl.when(has_lower)
    def _():
        pl.semaphore_signal(barrier, 1, device_id={axis: me - 1}, device_id_type=mesh_ids)

    @pl.when(has_upper)
    def _():
        pl.semaphore_signal(barrier, 1, device_id={axis: me + 1}, device_id_type=mesh_ids)

    pl.semaphore_wait(barrier, has_lower.astype(jnp.int32) + has_upper.astype(jnp.int32))

    to_upper = pltpu.make_async_remote_copy(
        src_ref=high,
        dst_ref=landed_before,
        send_sem=send_sem.at[0],
        recv_sem=recv_sem.at[0],
        device_id={axis: me + 1},
        device_id_type=mesh_ids,
    )
    to_lower = pltpu.make_async_remote_copy(
        src_ref=low,
        dst_ref=landed_after,
        send_sem=send_sem.at[1],
        recv_sem=recv_sem.at[1],
        device_id={axis: me - 1},
        device_id_type=mesh_ids,
    )

    @pl.when(has_upper)
    def _():
        to_upper.start()

    @pl.when(has_lower)
    def _():
        to_lower.start()

    @pl.when(has_upper)
    def _():
        to_upper.wait_send()
        to_lower.wait_recv()
        after[...] = landed_after[...]

    @pl.when(has_lower)
    def _():
        to_lower.wait_send()
        to_upper.wait_recv()
        before[...] = landed_before[...]

    @pl.when(jnp.logical_not(has_upper))
    def _():
        after[...] = jnp.zeros(after.shape, after.dtype)

    @pl.when(jnp.logical_not(has_lower))
    def _():
        before[...] = jnp.zeros(before.shape, before.dtype)


HALO_IDS = {}


def exchange(low, high, axis):
    key = (axis, low.shape)
    if key not in HALO_IDS:
        HALO_IDS[key] = len(HALO_IDS)
    kernel = functools.partial(halo_kernel, axis=axis, count=lax.axis_size(axis))
    vmem = pl.BlockSpec(memory_space=pltpu.VMEM)
    slab = jax.ShapeDtypeStruct(low.shape, low.dtype)
    return pl.pallas_call(
        kernel,
        out_shape=(slab, slab),
        in_specs=[vmem, vmem],
        out_specs=(vmem, vmem),
        scratch_shapes=[
            pltpu.VMEM(low.shape, low.dtype),
            pltpu.VMEM(low.shape, low.dtype),
            pltpu.SemaphoreType.DMA((2,)),
            pltpu.SemaphoreType.DMA((2,)),
        ],
        compiler_params=pltpu.CompilerParams(collective_id=HALO_IDS[key], has_side_effects=True),
    )(low, high)


def gather_kernel(shard, out, landed, send_sem, recv_sem, *, axis, count):
    me = lax.axis_index(axis)
    mesh_ids = pl.DeviceIdType.MESH
    barrier = pltpu.get_barrier_semaphore()
    for peer in range(count):

        @pl.when(peer != me)
        def _():
            pl.semaphore_signal(barrier, 1, device_id={axis: peer}, device_id_type=mesh_ids)

    pl.semaphore_wait(barrier, count - 1)
    copies = []
    for peer in range(count):
        copies.append(
            pltpu.make_async_remote_copy(
                src_ref=shard,
                dst_ref=landed.at[me],
                send_sem=send_sem.at[peer],
                recv_sem=recv_sem.at[me],
                device_id={axis: peer},
                device_id_type=mesh_ids,
            )
        )

        @pl.when(peer != me)
        def _():
            copies[peer].start()

    for peer in range(count):
        incoming = pltpu.make_async_remote_copy(
            src_ref=shard,
            dst_ref=landed.at[peer],
            send_sem=send_sem.at[peer],
            recv_sem=recv_sem.at[peer],
            device_id={axis: peer},
            device_id_type=mesh_ids,
        )

        @pl.when(peer != me)
        def _():
            copies[peer].wait_send()
            incoming.wait_recv()
            out[peer] = landed[peer]

    out[me] = shard[...]


def gather_peers(shard, axis):
    count = lax.axis_size(axis)
    kernel = functools.partial(gather_kernel, axis=axis, count=count)
    vmem = pl.BlockSpec(memory_space=pltpu.VMEM)
    stacked = (count,) + shard.shape
    return pl.pallas_call(
        kernel,
        out_shape=jax.ShapeDtypeStruct(stacked, shard.dtype),
        in_specs=[vmem],
        out_specs=vmem,
        scratch_shapes=[
            pltpu.VMEM(stacked, shard.dtype),
            pltpu.SemaphoreType.DMA((count,)),
            pltpu.SemaphoreType.DMA((count,)),
        ],
        compiler_params=pltpu.CompilerParams(collective_id=100, has_side_effects=True),
    )(shard)


def plane_kernel(*refs, axes, sizes, offsets):
    count = len(offsets)
    sends = refs[:count]
    outs = refs[count : 2 * count]
    landed = refs[2 * count : 3 * count]
    send_sem, recv_sem = refs[3 * count :]
    me = [lax.axis_index(axis) for axis in axes]
    mesh_ids = pl.DeviceIdType.MESH

    def exists(offset):
        inside = None
        for position, step, size in zip(me, offset, sizes):
            if step == 0:
                continue
            here = (position + step >= 0) & (position + step < size)
            inside = here if inside is None else inside & here
        return inside

    def target(offset):
        return {axis: position + step for axis, position, step in zip(axes, me, offset)}

    barrier = pltpu.get_barrier_semaphore()
    expected = 0
    for offset in offsets:

        @pl.when(exists(offset))
        def _():
            pl.semaphore_signal(barrier, 1, device_id=target(offset), device_id_type=mesh_ids)

        expected = expected + exists(offset).astype(jnp.int32)
    pl.semaphore_wait(barrier, expected)
    slot = {offset: k for k, offset in enumerate(offsets)}
    outgoing = []
    for k, offset in enumerate(offsets):
        back = slot[tuple(-step for step in offset)]
        outgoing.append(
            pltpu.make_async_remote_copy(
                src_ref=sends[k],
                dst_ref=landed[back],
                send_sem=send_sem.at[k],
                recv_sem=recv_sem.at[back],
                device_id=target(offset),
                device_id_type=mesh_ids,
            )
        )

        @pl.when(exists(offset))
        def _():
            outgoing[k].start()

    for k, offset in enumerate(offsets):
        back = slot[tuple(-step for step in offset)]
        incoming = pltpu.make_async_remote_copy(
            src_ref=sends[back],
            dst_ref=landed[k],
            send_sem=send_sem.at[back],
            recv_sem=recv_sem.at[k],
            device_id=target(offset),
            device_id_type=mesh_ids,
        )

        @pl.when(exists(offset))
        def _():
            outgoing[k].wait_send()
            incoming.wait_recv()
            outs[k][...] = landed[k][...]

        @pl.when(jnp.logical_not(exists(offset)))
        def _():
            outs[k][...] = jnp.zeros(outs[k].shape, outs[k].dtype)


def as_rows(piece, thin):
    tiled = math.prod(piece.shape[:-2]) * -(-piece.shape[-2] // 8) * 8 * -(-piece.shape[-1] // 128) * 128
    if tiled <= 3 * piece.size or tiled <= 65536:
        return piece, None
    moved = jnp.moveaxis(piece, thin, tuple(range(len(thin))))
    return moved.reshape(-1, moved.shape[-1]), moved.shape


def from_rows(piece, moved, thin):
    if moved is None:
        return piece
    return jnp.moveaxis(piece.reshape(moved), tuple(range(len(thin))), thin)


def with_plane_halo(shard, axes, dims, width):
    offsets = [(ox, oy) for ox in (-1, 0, 1) for oy in (-1, 0, 1) if (ox, oy) != (0, 0)]
    pieces = []
    layouts = []
    for offset in offsets:
        piece = shard
        thin = []
        for step, dim in zip(offset, dims):
            length = piece.shape[dim]
            if step == 1:
                piece = lax.slice_in_dim(piece, length - width, length, axis=dim)
            elif step == -1:
                piece = lax.slice_in_dim(piece, 0, width, axis=dim)
            if step != 0:
                thin.append(dim)
        piece, moved = as_rows(piece, thin)
        pieces.append(piece)
        layouts.append((moved, thin))
    key = ("plane",) + tuple(piece.shape for piece in pieces)
    if key not in HALO_IDS:
        HALO_IDS[key] = len(HALO_IDS)
    sizes = tuple(lax.axis_size(axis) for axis in axes)
    kernel = functools.partial(plane_kernel, axes=axes, sizes=sizes, offsets=tuple(offsets))
    vmem = pl.BlockSpec(memory_space=pltpu.VMEM)
    shapes = tuple(jax.ShapeDtypeStruct(piece.shape, piece.dtype) for piece in pieces)
    received = pl.pallas_call(
        kernel,
        out_shape=shapes,
        in_specs=[vmem] * len(pieces),
        out_specs=tuple([vmem] * len(pieces)),
        scratch_shapes=[pltpu.VMEM(piece.shape, piece.dtype) for piece in pieces]
        + [pltpu.SemaphoreType.DMA((len(pieces),)), pltpu.SemaphoreType.DMA((len(pieces),))],
        compiler_params=pltpu.CompilerParams(collective_id=HALO_IDS[key], has_side_effects=True),
    )(*pieces)
    got = {offset: from_rows(piece, *layout) for offset, piece, layout in zip(offsets, received, layouts)}
    got[(0, 0)] = shard
    rows = []
    for ox in (-1, 0, 1):
        rows.append(jnp.concatenate([got[(ox, oy)] for oy in (-1, 0, 1)], axis=dims[1]))
    return jnp.concatenate(rows, axis=dims[0])


def with_halo(shard, sides, width):
    for axis, dim in sides:
        length = shard.shape[dim]
        last = lax.slice_in_dim(shard, length - width, length, axis=dim)
        initial = lax.slice_in_dim(shard, 0, width, axis=dim)
        tiled = math.prod(initial.shape[:-2]) * -(-initial.shape[-2] // 8) * 8 * -(-initial.shape[-1] // 128) * 128
        if tiled <= 3 * initial.size:
            before, after = exchange(initial, last, axis)
        else:
            moved = jnp.moveaxis(initial, dim, 0).shape
            rows = (-1, moved[-1])
            before, after = exchange(
                jnp.moveaxis(initial, dim, 0).reshape(rows), jnp.moveaxis(last, dim, 0).reshape(rows), axis
            )
            before = jnp.moveaxis(before.reshape(moved), 0, dim)
            after = jnp.moveaxis(after.reshape(moved), 0, dim)
        shard = jnp.concatenate([before, shard, after], axis=dim)
    return shard


def recover(local_nodes, corner_vals, ratio_z):
    ex = local_nodes.shape[1] - 1
    ey = local_nodes.shape[2] - 1
    ratio_x = jnp.arange(ex + 1, dtype=jnp.float32) / ex
    ratio_y = jnp.arange(ey + 1, dtype=jnp.float32) / ey
    planes = []
    for high_z in (0, 1):
        plane = None
        for corner in range(high_z, 8, 2):
            along_x = ratio_x if corner // 4 == 1 else 1.0 - ratio_x
            along_y = ratio_y if corner // 2 % 2 == 1 else 1.0 - ratio_y
            basis = along_x[:, None] * along_y[None, :]
            term = basis[None] * corner_vals[:, corner][:, None, None]
            plane = term if plane is None else plane + term
        planes.append(plane[:, :, :, None])
    return local_nodes + planes[0] * (1.0 - ratio_z) + planes[1] * ratio_z


def average_rows(extended, dim, has_lower, has_upper):
    inner = extended.shape[dim] - 2
    own_rows = lax.slice_in_dim(extended, 1, inner + 1, axis=dim)
    rim_low = lax.slice_in_dim(extended, 0, 1, axis=dim)
    rim_high = lax.slice_in_dim(extended, inner + 1, inner + 2, axis=dim)
    shape_row = [1] * extended.ndim
    shape_row[dim] = inner
    rows = jnp.arange(inner, dtype=jnp.int32).reshape(shape_row)
    is_low = rows == 0
    is_high = rows == inner - 1
    factor = jnp.where(is_low & has_lower, 0.5, jnp.where(is_high & has_upper, 0.5, 1.0))
    rim_part = jnp.where(is_low, rim_low, 0.0) + jnp.where(is_high, rim_high, 0.0)
    return own_rows * factor + rim_part * 0.5


def energy_kernel(stiffness, shifted, out, weights, *, count_x, chunks):
    sources = (shifted.at[0], shifted.at[2], shifted.at[1], shifted.at[3])
    for a in range(24):
        weights[a * 24 + a] = stiffness[a, a]
        for b in range(a + 1, 24):
            weights[a * 24 + b] = stiffness[a, b] + stiffness[b, a]

    def row(i, carry):
        for first in chunks:
            vectors = []
            for component in range(3):
                for corner in range(8):
                    shift_x = corner // 4
                    source = sources[corner % 4]
                    vectors.append(source[component, i + shift_x, pl.ds(first, 8), :])
            total = None
            for a in range(24):
                inner = weights[a * 24 + a] * vectors[a]
                for b in range(a + 1, 24):
                    inner = inner + weights[a * 24 + b] * vectors[b]
                term = vectors[a] * inner
                total = term if total is None else total + term
            out[i, pl.ds(first, 8), :] = total
        return carry

    lax.fori_loop(0, count_x, row, 0)


def element_energy(nodes, stiffness):
    count_x = nodes.shape[1] - 1
    count_y = nodes.shape[2] - 1
    count_z = nodes.shape[3] - 1
    rows = -(-count_y // 8) * 8
    pad = ((0, 0), (0, 0), (0, rows - count_y), (0, 0))
    shifted = jnp.stack(
        [
            jnp.pad(nodes[:, :, dy : dy + count_y, dz : dz + count_z], pad)
            for dy, dz in ((0, 0), (1, 0), (0, 1), (1, 1))
        ]
    )
    kernel = functools.partial(energy_kernel, count_x=count_x, chunks=tuple(range(0, rows, 8)))
    vmem = pl.BlockSpec(memory_space=pltpu.VMEM)
    energy = pl.pallas_call(
        kernel,
        out_shape=jax.ShapeDtypeStruct((count_x, rows, count_z), jnp.float32),
        in_specs=[pl.BlockSpec(memory_space=pltpu.SMEM), vmem],
        out_specs=vmem,
        scratch_shapes=[pltpu.SMEM((24 * 24,), jnp.float32)],
    )(stiffness, shifted)
    return energy[:, :count_y, :]


def smooth(field, axis, count):
    summed = None
    for offset in range(-RADIUS, RADIUS + 1):
        term_piece = lax.slice_in_dim(field, RADIUS + offset, RADIUS + offset + count, axis=axis)
        term_value = float(RADIUS + 1 - abs(offset)) * term_piece
        summed = term_value if summed is None else summed + term_value
    return summed


def edge_counts(count, position, parts):
    places = position * count + jnp.arange(count, dtype=jnp.int32)
    summed = None
    for offset in range(-RADIUS, RADIUS + 1):
        inside = ((places + offset >= 0) & (places + offset < count * parts)).astype(jnp.float32)
        term_value = float(RADIUS + 1 - abs(offset)) * inside
        summed = term_value if summed is None else summed + term_value
    return summed


def filter_field(field, sides):
    (axis_x, dim_x), (axis_y, dim_y), (axis_z, dim_z) = sides
    count_x, count_y = field.shape[dim_x], field.shape[dim_y]
    padded = with_plane_halo(field, (axis_x, axis_y), (dim_x, dim_y), RADIUS)
    field = smooth(smooth(padded, dim_x, count_x), dim_y, count_y)
    padded = with_halo(field, ((axis_z, dim_z),), RADIUS)
    return smooth(padded, dim_z, field.shape[dim_z])


def local(local_solution, top_nodes, coarse_solution, corner_dofs, density, element_stiffness):
    count_x, count_y, count_z = density.shape
    index_x = lax.axis_index("gx")
    index_y = lax.axis_index("gy")
    index_z = lax.axis_index("gz")
    normalizer = (
        edge_counts(count_x, index_x, lax.axis_size("gx"))[:, None, None]
        * edge_counts(count_y, index_y, lax.axis_size("gy"))[None, :, None]
        * edge_counts(count_z, index_z, lax.axis_size("gz"))[None, None, :]
    )
    sides = (("gx", 1), ("gy", 2), ("gz", 3))
    wanted = corner_dofs.reshape(8)
    gathered = gather_peers(coarse_solution, "gz")
    columns = gathered.transpose(1, 0, 2).reshape(coarse_solution.shape[0], -1)
    matches = wanted[:, None] == jnp.arange(columns.shape[1], dtype=jnp.int32)[None, :]
    corner_vals = jnp.sum(jnp.where(matches[None], columns[:, None, :], 0.0), axis=2)
    depth = local_solution.shape[3]
    full = jnp.concatenate([local_solution, top_nodes], axis=3)
    nodes = recover(full, corner_vals, jnp.arange(depth + 1, dtype=jnp.float32) / depth)
    lower_x = index_x > 0
    upper_x = index_x < lax.axis_size("gx") - 1
    lower_y = index_y > 0
    upper_y = index_y < lax.axis_size("gy") - 1
    lower_z = index_z > 0
    upper_z = index_z < lax.axis_size("gz") - 1
    extended = with_plane_halo(nodes, ("gx", "gy"), (1, 2), 1)
    extended = average_rows(extended, 1, lower_x, upper_x)
    averaged = average_rows(extended, 2, lower_y, upper_y)
    extended = with_halo(averaged, (("gz", 3),), 1)
    averaged = average_rows(extended, 3, lower_z, upper_z)
    energy = element_energy(averaged, element_stiffness)
    sens = penal_scale * density * density * energy
    smoothed = filter_field(jnp.stack([density * sens, density]), sides)
    numerator = smoothed[0]
    smooth_density = smoothed[1]
    return (numerator / (density * normalizer), smooth_density / normalizer)


def solution(mesh):
    in_specs = (
        P(None, "gx", "gy", "gz"),
        P(None, "gx", "gy", "gz"),
        P(None, "gz"),
        P("gx", "gy", "gz", None),
        P("gx", "gy", "gz"),
        P(),
    )
    out_specs = (P("gx", "gy", "gz"), P("gx", "gy", "gz"))
    return jax.shard_map(local, mesh=mesh, in_specs=in_specs, out_specs=out_specs, check_vma=False)
```

```python
import functools
import math

import jax
import jax.numpy as jnp
from jax import lax
from jax.sharding import PartitionSpec as P
from jax.experimental import pallas as pl
from jax.experimental.pallas import tpu as pltpu

RADIUS = 3


penal_scale = -3.0 / 96.0


def halo_kernel(low, high, before, after, landed_before, landed_after, send_sem, recv_sem, *, axis, count):
    me = lax.axis_index(axis)
    has_lower = me > 0
    has_upper = me < count - 1
    mesh_ids = pl.DeviceIdType.MESH
    barrier = pltpu.get_barrier_semaphore()

    @pl.when(has_lower)
    def _():
        pl.semaphore_signal(barrier, 1, device_id={axis: me - 1}, device_id_type=mesh_ids)

    @pl.when(has_upper)
    def _():
        pl.semaphore_signal(barrier, 1, device_id={axis: me + 1}, device_id_type=mesh_ids)

    pl.semaphore_wait(barrier, has_lower.astype(jnp.int32) + has_upper.astype(jnp.int32))

    to_upper = pltpu.make_async_remote_copy(
        src_ref=high,
        dst_ref=landed_before,
        send_sem=send_sem.at[0],
        recv_sem=recv_sem.at[0],
        device_id={axis: me + 1},
        device_id_type=mesh_ids,
    )
    to_lower = pltpu.make_async_remote_copy(
        src_ref=low,
        dst_ref=landed_after,
        send_sem=send_sem.at[1],
        recv_sem=recv_sem.at[1],
        device_id={axis: me - 1},
        device_id_type=mesh_ids,
    )

    @pl.when(has_upper)
    def _():
        to_upper.start()

    @pl.when(has_lower)
    def _():
        to_lower.start()

    @pl.when(has_upper)
    def _():
        to_upper.wait_send()
        to_lower.wait_recv()
        after[...] = landed_after[...]

    @pl.when(has_lower)
    def _():
        to_lower.wait_send()
        to_upper.wait_recv()
        before[...] = landed_before[...]

    @pl.when(jnp.logical_not(has_upper))
    def _():
        after[...] = jnp.zeros(after.shape, after.dtype)

    @pl.when(jnp.logical_not(has_lower))
    def _():
        before[...] = jnp.zeros(before.shape, before.dtype)


HALO_IDS = {}


def exchange(low, high, axis):
    key = (axis, low.shape)
    if key not in HALO_IDS:
        HALO_IDS[key] = len(HALO_IDS)
    kernel = functools.partial(halo_kernel, axis=axis, count=lax.axis_size(axis))
    vmem = pl.BlockSpec(memory_space=pltpu.VMEM)
    slab = jax.ShapeDtypeStruct(low.shape, low.dtype)
    return pl.pallas_call(
        kernel,
        out_shape=(slab, slab),
        in_specs=[vmem, vmem],
        out_specs=(vmem, vmem),
        scratch_shapes=[
            pltpu.VMEM(low.shape, low.dtype),
            pltpu.VMEM(low.shape, low.dtype),
            pltpu.SemaphoreType.DMA((2,)),
            pltpu.SemaphoreType.DMA((2,)),
        ],
        compiler_params=pltpu.CompilerParams(collective_id=HALO_IDS[key], has_side_effects=True),
    )(low, high)


def gather_kernel(shard, out, landed, send_sem, recv_sem, *, axis, count):
    me = lax.axis_index(axis)
    mesh_ids = pl.DeviceIdType.MESH
    barrier = pltpu.get_barrier_semaphore()
    for peer in range(count):

        @pl.when(peer != me)
        def _():
            pl.semaphore_signal(barrier, 1, device_id={axis: peer}, device_id_type=mesh_ids)

    pl.semaphore_wait(barrier, count - 1)
    copies = []
    for peer in range(count):
        copies.append(
            pltpu.make_async_remote_copy(
                src_ref=shard,
                dst_ref=landed.at[me],
                send_sem=send_sem.at[peer],
                recv_sem=recv_sem.at[me],
                device_id={axis: peer},
                device_id_type=mesh_ids,
            )
        )

        @pl.when(peer != me)
        def _():
            copies[peer].start()

    for peer in range(count):
        incoming = pltpu.make_async_remote_copy(
            src_ref=shard,
            dst_ref=landed.at[peer],
            send_sem=send_sem.at[peer],
            recv_sem=recv_sem.at[peer],
            device_id={axis: peer},
            device_id_type=mesh_ids,
        )

        @pl.when(peer != me)
        def _():
            copies[peer].wait_send()
            incoming.wait_recv()
            out[peer] = landed[peer]

    out[me] = shard[...]


def gather_peers(shard, axis):
    count = lax.axis_size(axis)
    kernel = functools.partial(gather_kernel, axis=axis, count=count)
    vmem = pl.BlockSpec(memory_space=pltpu.VMEM)
    stacked = (count,) + shard.shape
    return pl.pallas_call(
        kernel,
        out_shape=jax.ShapeDtypeStruct(stacked, shard.dtype),
        in_specs=[vmem],
        out_specs=vmem,
        scratch_shapes=[
            pltpu.VMEM(stacked, shard.dtype),
            pltpu.SemaphoreType.DMA((count,)),
            pltpu.SemaphoreType.DMA((count,)),
        ],
        compiler_params=pltpu.CompilerParams(collective_id=100, has_side_effects=True),
    )(shard)


def plane_kernel(*refs, axes, sizes, offsets):
    count = len(offsets)
    sends = refs[:count]
    outs = refs[count : 2 * count]
    landed = refs[2 * count : 3 * count]
    send_sem, recv_sem = refs[3 * count :]
    me = [lax.axis_index(axis) for axis in axes]
    mesh_ids = pl.DeviceIdType.MESH

    def exists(offset):
        inside = None
        for position, step, size in zip(me, offset, sizes):
            if step == 0:
                continue
            here = (position + step >= 0) & (position + step < size)
            inside = here if inside is None else inside & here
        return inside

    def target(offset):
        return {axis: position + step for axis, position, step in zip(axes, me, offset)}

    barrier = pltpu.get_barrier_semaphore()
    expected = 0
    for offset in offsets:

        @pl.when(exists(offset))
        def _():
            pl.semaphore_signal(barrier, 1, device_id=target(offset), device_id_type=mesh_ids)

        expected = expected + exists(offset).astype(jnp.int32)
    pl.semaphore_wait(barrier, expected)
    slot = {offset: k for k, offset in enumerate(offsets)}
    outgoing = []
    for k, offset in enumerate(offsets):
        back = slot[tuple(-step for step in offset)]
        outgoing.append(
            pltpu.make_async_remote_copy(
                src_ref=sends[k],
                dst_ref=landed[back],
                send_sem=send_sem.at[k],
                recv_sem=recv_sem.at[back],
                device_id=target(offset),
                device_id_type=mesh_ids,
            )
        )

        @pl.when(exists(offset))
        def _():
            outgoing[k].start()

    for k, offset in enumerate(offsets):
        back = slot[tuple(-step for step in offset)]
        incoming = pltpu.make_async_remote_copy(
            src_ref=sends[back],
            dst_ref=landed[k],
            send_sem=send_sem.at[back],
            recv_sem=recv_sem.at[k],
            device_id=target(offset),
            device_id_type=mesh_ids,
        )

        @pl.when(exists(offset))
        def _():
            outgoing[k].wait_send()
            incoming.wait_recv()
            outs[k][...] = landed[k][...]

        @pl.when(jnp.logical_not(exists(offset)))
        def _():
            outs[k][...] = jnp.zeros(outs[k].shape, outs[k].dtype)


def as_rows(piece, thin):
    tiled = math.prod(piece.shape[:-2]) * -(-piece.shape[-2] // 8) * 8 * -(-piece.shape[-1] // 128) * 128
    if tiled <= 3 * piece.size or tiled <= 65536:
        return piece, None
    moved = jnp.moveaxis(piece, thin, tuple(range(len(thin))))
    return moved.reshape(-1, moved.shape[-1]), moved.shape


def from_rows(piece, moved, thin):
    if moved is None:
        return piece
    return jnp.moveaxis(piece.reshape(moved), tuple(range(len(thin))), thin)


def with_plane_halo(shard, axes, dims, width):
    offsets = [(ox, oy) for ox in (-1, 0, 1) for oy in (-1, 0, 1) if (ox, oy) != (0, 0)]
    pieces = []
    layouts = []
    for offset in offsets:
        piece = shard
        thin = []
        for step, dim in zip(offset, dims):
            length = piece.shape[dim]
            if step == 1:
                piece = lax.slice_in_dim(piece, length - width, length, axis=dim)
            elif step == -1:
                piece = lax.slice_in_dim(piece, 0, width, axis=dim)
            if step != 0:
                thin.append(dim)
        piece, moved = as_rows(piece, thin)
        pieces.append(piece)
        layouts.append((moved, thin))
    key = ("plane",) + tuple(piece.shape for piece in pieces)
    if key not in HALO_IDS:
        HALO_IDS[key] = len(HALO_IDS)
    sizes = tuple(lax.axis_size(axis) for axis in axes)
    kernel = functools.partial(plane_kernel, axes=axes, sizes=sizes, offsets=tuple(offsets))
    vmem = pl.BlockSpec(memory_space=pltpu.VMEM)
    shapes = tuple(jax.ShapeDtypeStruct(piece.shape, piece.dtype) for piece in pieces)
    received = pl.pallas_call(
        kernel,
        out_shape=shapes,
        in_specs=[vmem] * len(pieces),
        out_specs=tuple([vmem] * len(pieces)),
        scratch_shapes=[pltpu.VMEM(piece.shape, piece.dtype) for piece in pieces]
        + [pltpu.SemaphoreType.DMA((len(pieces),)), pltpu.SemaphoreType.DMA((len(pieces),))],
        compiler_params=pltpu.CompilerParams(collective_id=HALO_IDS[key], has_side_effects=True),
    )(*pieces)
    got = {offset: from_rows(piece, *layout) for offset, piece, layout in zip(offsets, received, layouts)}
    got[(0, 0)] = shard
    rows = []
    for ox in (-1, 0, 1):
        rows.append(jnp.concatenate([got[(ox, oy)] for oy in (-1, 0, 1)], axis=dims[1]))
    return jnp.concatenate(rows, axis=dims[0])


def with_halo(shard, sides, width):
    for axis, dim in sides:
        length = shard.shape[dim]
        last = lax.slice_in_dim(shard, length - width, length, axis=dim)
        initial = lax.slice_in_dim(shard, 0, width, axis=dim)
        tiled = math.prod(initial.shape[:-2]) * -(-initial.shape[-2] // 8) * 8 * -(-initial.shape[-1] // 128) * 128
        if tiled <= 3 * initial.size:
            before, after = exchange(initial, last, axis)
        else:
            moved = jnp.moveaxis(initial, dim, 0).shape
            rows = (-1, moved[-1])
            before, after = exchange(
                jnp.moveaxis(initial, dim, 0).reshape(rows), jnp.moveaxis(last, dim, 0).reshape(rows), axis
            )
            before = jnp.moveaxis(before.reshape(moved), 0, dim)
            after = jnp.moveaxis(after.reshape(moved), 0, dim)
        shard = jnp.concatenate([before, shard, after], axis=dim)
    return shard


def recover(local_nodes, corner_vals, ratio_z):
    ex = local_nodes.shape[1] - 1
    ey = local_nodes.shape[2] - 1
    ratio_x = jnp.arange(ex + 1, dtype=jnp.float32) / ex
    ratio_y = jnp.arange(ey + 1, dtype=jnp.float32) / ey
    planes = []
    for high_z in (0, 1):
        plane = None
        for corner in range(high_z, 8, 2):
            along_x = ratio_x if corner // 4 == 1 else 1.0 - ratio_x
            along_y = ratio_y if corner // 2 % 2 == 1 else 1.0 - ratio_y
            basis = along_x[:, None] * along_y[None, :]
            term = basis[None] * corner_vals[:, corner][:, None, None]
            plane = term if plane is None else plane + term
        planes.append(plane[:, :, :, None])
    return local_nodes + planes[0] * (1.0 - ratio_z) + planes[1] * ratio_z


def average_rows(extended, dim, has_lower, has_upper):
    inner = extended.shape[dim] - 2
    own_rows = lax.slice_in_dim(extended, 1, inner + 1, axis=dim)
    rim_low = lax.slice_in_dim(extended, 0, 1, axis=dim)
    rim_high = lax.slice_in_dim(extended, inner + 1, inner + 2, axis=dim)
    shape_row = [1] * extended.ndim
    shape_row[dim] = inner
    rows = jnp.arange(inner, dtype=jnp.int32).reshape(shape_row)
    is_low = rows == 0
    is_high = rows == inner - 1
    factor = jnp.where(is_low & has_lower, 0.5, jnp.where(is_high & has_upper, 0.5, 1.0))
    rim_part = jnp.where(is_low, rim_low, 0.0) + jnp.where(is_high, rim_high, 0.0)
    return own_rows * factor + rim_part * 0.5


def energy_kernel(stiffness, shifted, out, weights, *, count_x, chunks):
    sources = (shifted.at[0], shifted.at[2], shifted.at[1], shifted.at[3])
    for a in range(24):
        weights[a * 24 + a] = stiffness[a, a]
        for b in range(a + 1, 24):
            weights[a * 24 + b] = stiffness[a, b] + stiffness[b, a]

    def row(i, carry):
        for first in chunks:
            vectors = []
            for component in range(3):
                for corner in range(8):
                    shift_x = corner // 4
                    source = sources[corner % 4]
                    vectors.append(source[component, i + shift_x, pl.ds(first, 8), :])
            total = None
            for a in range(24):
                inner = weights[a * 24 + a] * vectors[a]
                for b in range(a + 1, 24):
                    inner = inner + weights[a * 24 + b] * vectors[b]
                term = vectors[a] * inner
                total = term if total is None else total + term
            if first % 8 == 0:
                out[i, pl.ds(first, 8), :] = total
            else:
                keep = 8 - first % 8
                out[i, pl.ds(first + 8 - keep, keep), :] = total[8 - keep :]
        return carry

    lax.fori_loop(0, count_x, row, 0)


def element_energy(nodes, stiffness):
    count_x = nodes.shape[1] - 1
    count_y = nodes.shape[2] - 1
    count_z = nodes.shape[3] - 1
    shifted = jnp.stack(
        [nodes[:, :, dy : dy + count_y, dz : dz + count_z] for dy, dz in ((0, 0), (1, 0), (0, 1), (1, 1))]
    )
    chunks = tuple(range(0, count_y - 7, 8))
    if count_y % 8:
        chunks = chunks + (count_y - 8,)
    kernel = functools.partial(energy_kernel, count_x=count_x, chunks=chunks)
    vmem = pl.BlockSpec(memory_space=pltpu.VMEM)
    energy = pl.pallas_call(
        kernel,
        out_shape=jax.ShapeDtypeStruct((count_x, count_y, count_z), jnp.float32),
        in_specs=[pl.BlockSpec(memory_space=pltpu.SMEM), vmem],
        out_specs=vmem,
        scratch_shapes=[pltpu.SMEM((24 * 24,), jnp.float32)],
    )(stiffness, shifted)
    return energy


def smooth(field, axis, count):
    summed = None
    for offset in range(-RADIUS, RADIUS + 1):
        term_piece = lax.slice_in_dim(field, RADIUS + offset, RADIUS + offset + count, axis=axis)
        term_value = float(RADIUS + 1 - abs(offset)) * term_piece
        summed = term_value if summed is None else summed + term_value
    return summed


def edge_counts(count, position, parts):
    places = position * count + jnp.arange(count, dtype=jnp.int32)
    summed = None
    for offset in range(-RADIUS, RADIUS + 1):
        inside = ((places + offset >= 0) & (places + offset < count * parts)).astype(jnp.float32)
        term_value = float(RADIUS + 1 - abs(offset)) * inside
        summed = term_value if summed is None else summed + term_value
    return summed


def filter_field(field, sides):
    (axis_x, dim_x), (axis_y, dim_y), (axis_z, dim_z) = sides
    count_x, count_y = field.shape[dim_x], field.shape[dim_y]
    padded = with_plane_halo(field, (axis_x, axis_y), (dim_x, dim_y), RADIUS)
    field = smooth(smooth(padded, dim_x, count_x), dim_y, count_y)
    padded = with_halo(field, ((axis_z, dim_z),), RADIUS)
    return smooth(padded, dim_z, field.shape[dim_z])


def local(local_solution, top_nodes, coarse_solution, corner_dofs, density, element_stiffness):
    count_x, count_y, count_z = density.shape
    index_x = lax.axis_index("gx")
    index_y = lax.axis_index("gy")
    index_z = lax.axis_index("gz")
    normalizer = (
        edge_counts(count_x, index_x, lax.axis_size("gx"))[:, None, None]
        * edge_counts(count_y, index_y, lax.axis_size("gy"))[None, :, None]
        * edge_counts(count_z, index_z, lax.axis_size("gz"))[None, None, :]
    )
    sides = (("gx", 1), ("gy", 2), ("gz", 3))
    wanted = corner_dofs.reshape(8)
    gathered = gather_peers(coarse_solution, "gz")
    columns = gathered.transpose(1, 0, 2).reshape(coarse_solution.shape[0], -1)
    matches = wanted[:, None] == jnp.arange(columns.shape[1], dtype=jnp.int32)[None, :]
    corner_vals = jnp.sum(jnp.where(matches[None], columns[:, None, :], 0.0), axis=2)
    depth = local_solution.shape[3]
    full = jnp.concatenate([local_solution, top_nodes], axis=3)
    nodes = recover(full, corner_vals, jnp.arange(depth + 1, dtype=jnp.float32) / depth)
    lower_x = index_x > 0
    upper_x = index_x < lax.axis_size("gx") - 1
    lower_y = index_y > 0
    upper_y = index_y < lax.axis_size("gy") - 1
    lower_z = index_z > 0
    upper_z = index_z < lax.axis_size("gz") - 1
    extended = with_plane_halo(nodes, ("gx", "gy"), (1, 2), 1)
    extended = average_rows(extended, 1, lower_x, upper_x)
    averaged = average_rows(extended, 2, lower_y, upper_y)
    extended = with_halo(averaged, (("gz", 3),), 1)
    averaged = average_rows(extended, 3, lower_z, upper_z)
    energy = element_energy(averaged, element_stiffness)
    sens = penal_scale * density * density * energy
    smoothed = filter_field(jnp.stack([density * sens, density]), sides)
    numerator = smoothed[0]
    smooth_density = smoothed[1]
    return (numerator / (density * normalizer), smooth_density / normalizer)


def solution(mesh):
    in_specs = (
        P(None, "gx", "gy", "gz"),
        P(None, "gx", "gy", "gz"),
        P(None, "gz"),
        P("gx", "gy", "gz", None),
        P("gx", "gy", "gz"),
        P(),
    )
    out_specs = (P("gx", "gy", "gz"), P("gx", "gy", "gz"))
    return jax.shard_map(local, mesh=mesh, in_specs=in_specs, out_specs=out_specs, check_vma=False)
```

```python
import functools
import math

import jax
import jax.numpy as jnp
from jax import lax
from jax.sharding import PartitionSpec as P
from jax.experimental import pallas as pl
from jax.experimental.pallas import tpu as pltpu

RADIUS = 3


penal_scale = -3.0 / 96.0


def halo_kernel(low, high, before, after, landed_before, landed_after, send_sem, recv_sem, *, axis, count):
    me = lax.axis_index(axis)
    has_lower = me > 0
    has_upper = me < count - 1
    mesh_ids = pl.DeviceIdType.MESH
    barrier = pltpu.get_barrier_semaphore()

    @pl.when(has_lower)
    def _():
        pl.semaphore_signal(barrier, 1, device_id={axis: me - 1}, device_id_type=mesh_ids)

    @pl.when(has_upper)
    def _():
        pl.semaphore_signal(barrier, 1, device_id={axis: me + 1}, device_id_type=mesh_ids)

    pl.semaphore_wait(barrier, has_lower.astype(jnp.int32) + has_upper.astype(jnp.int32))

    to_upper = pltpu.make_async_remote_copy(
        src_ref=high,
        dst_ref=landed_before,
        send_sem=send_sem.at[0],
        recv_sem=recv_sem.at[0],
        device_id={axis: me + 1},
        device_id_type=mesh_ids,
    )
    to_lower = pltpu.make_async_remote_copy(
        src_ref=low,
        dst_ref=landed_after,
        send_sem=send_sem.at[1],
        recv_sem=recv_sem.at[1],
        device_id={axis: me - 1},
        device_id_type=mesh_ids,
    )

    @pl.when(has_upper)
    def _():
        to_upper.start()

    @pl.when(has_lower)
    def _():
        to_lower.start()

    @pl.when(has_upper)
    def _():
        to_upper.wait_send()
        to_lower.wait_recv()
        after[...] = landed_after[...]

    @pl.when(has_lower)
    def _():
        to_lower.wait_send()
        to_upper.wait_recv()
        before[...] = landed_before[...]

    @pl.when(jnp.logical_not(has_upper))
    def _():
        after[...] = jnp.zeros(after.shape, after.dtype)

    @pl.when(jnp.logical_not(has_lower))
    def _():
        before[...] = jnp.zeros(before.shape, before.dtype)


HALO_IDS = {}


def exchange(low, high, axis):
    key = (axis, low.shape)
    if key not in HALO_IDS:
        HALO_IDS[key] = len(HALO_IDS)
    kernel = functools.partial(halo_kernel, axis=axis, count=lax.axis_size(axis))
    vmem = pl.BlockSpec(memory_space=pltpu.VMEM)
    slab = jax.ShapeDtypeStruct(low.shape, low.dtype)
    return pl.pallas_call(
        kernel,
        out_shape=(slab, slab),
        in_specs=[vmem, vmem],
        out_specs=(vmem, vmem),
        scratch_shapes=[
            pltpu.VMEM(low.shape, low.dtype),
            pltpu.VMEM(low.shape, low.dtype),
            pltpu.SemaphoreType.DMA((2,)),
            pltpu.SemaphoreType.DMA((2,)),
        ],
        compiler_params=pltpu.CompilerParams(collective_id=HALO_IDS[key], has_side_effects=True),
    )(low, high)


def gather_kernel(shard, out, landed, send_sem, recv_sem, *, axis, count):
    me = lax.axis_index(axis)
    mesh_ids = pl.DeviceIdType.MESH
    barrier = pltpu.get_barrier_semaphore()
    for peer in range(count):

        @pl.when(peer != me)
        def _():
            pl.semaphore_signal(barrier, 1, device_id={axis: peer}, device_id_type=mesh_ids)

    pl.semaphore_wait(barrier, count - 1)
    copies = []
    for peer in range(count):
        copies.append(
            pltpu.make_async_remote_copy(
                src_ref=shard,
                dst_ref=landed.at[me],
                send_sem=send_sem.at[peer],
                recv_sem=recv_sem.at[me],
                device_id={axis: peer},
                device_id_type=mesh_ids,
            )
        )

        @pl.when(peer != me)
        def _():
            copies[peer].start()

    for peer in range(count):
        incoming = pltpu.make_async_remote_copy(
            src_ref=shard,
            dst_ref=landed.at[peer],
            send_sem=send_sem.at[peer],
            recv_sem=recv_sem.at[peer],
            device_id={axis: peer},
            device_id_type=mesh_ids,
        )

        @pl.when(peer != me)
        def _():
            copies[peer].wait_send()
            incoming.wait_recv()
            out[peer] = landed[peer]

    out[me] = shard[...]


def gather_peers(shard, axis):
    count = lax.axis_size(axis)
    kernel = functools.partial(gather_kernel, axis=axis, count=count)
    vmem = pl.BlockSpec(memory_space=pltpu.VMEM)
    stacked = (count,) + shard.shape
    return pl.pallas_call(
        kernel,
        out_shape=jax.ShapeDtypeStruct(stacked, shard.dtype),
        in_specs=[vmem],
        out_specs=vmem,
        scratch_shapes=[
            pltpu.VMEM(stacked, shard.dtype),
            pltpu.SemaphoreType.DMA((count,)),
            pltpu.SemaphoreType.DMA((count,)),
        ],
        compiler_params=pltpu.CompilerParams(collective_id=100, has_side_effects=True),
    )(shard)


def plane_kernel(*refs, axes, sizes, offsets):
    count = len(offsets)
    sends = refs[:count]
    outs = refs[count : 2 * count]
    landed = refs[2 * count : 3 * count]
    send_sem, recv_sem = refs[3 * count :]
    me = [lax.axis_index(axis) for axis in axes]
    mesh_ids = pl.DeviceIdType.MESH

    def exists(offset):
        inside = None
        for position, step, size in zip(me, offset, sizes):
            if step == 0:
                continue
            here = (position + step >= 0) & (position + step < size)
            inside = here if inside is None else inside & here
        return inside

    def target(offset):
        return {axis: position + step for axis, position, step in zip(axes, me, offset)}

    barrier = pltpu.get_barrier_semaphore()
    expected = 0
    for offset in offsets:

        @pl.when(exists(offset))
        def _():
            pl.semaphore_signal(barrier, 1, device_id=target(offset), device_id_type=mesh_ids)

        expected = expected + exists(offset).astype(jnp.int32)
    pl.semaphore_wait(barrier, expected)
    slot = {offset: k for k, offset in enumerate(offsets)}
    outgoing = []
    for k, offset in enumerate(offsets):
        back = slot[tuple(-step for step in offset)]
        outgoing.append(
            pltpu.make_async_remote_copy(
                src_ref=sends[k],
                dst_ref=landed[back],
                send_sem=send_sem.at[k],
                recv_sem=recv_sem.at[back],
                device_id=target(offset),
                device_id_type=mesh_ids,
            )
        )

        @pl.when(exists(offset))
        def _():
            outgoing[k].start()

    for k, offset in enumerate(offsets):
        back = slot[tuple(-step for step in offset)]
        incoming = pltpu.make_async_remote_copy(
            src_ref=sends[back],
            dst_ref=landed[k],
            send_sem=send_sem.at[back],
            recv_sem=recv_sem.at[k],
            device_id=target(offset),
            device_id_type=mesh_ids,
        )

        @pl.when(exists(offset))
        def _():
            outgoing[k].wait_send()
            incoming.wait_recv()
            outs[k][...] = landed[k][...]

        @pl.when(jnp.logical_not(exists(offset)))
        def _():
            outs[k][...] = jnp.zeros(outs[k].shape, outs[k].dtype)


def as_rows(piece, thin):
    tiled = math.prod(piece.shape[:-2]) * -(-piece.shape[-2] // 8) * 8 * -(-piece.shape[-1] // 128) * 128
    if tiled <= 3 * piece.size or tiled <= 65536:
        return piece, None
    moved = jnp.moveaxis(piece, thin, tuple(range(len(thin))))
    return moved.reshape(-1, moved.shape[-1]), moved.shape


def from_rows(piece, moved, thin):
    if moved is None:
        return piece
    return jnp.moveaxis(piece.reshape(moved), tuple(range(len(thin))), thin)


def with_plane_halo(shard, axes, dims, width):
    offsets = [(ox, oy) for ox in (-1, 0, 1) for oy in (-1, 0, 1) if (ox, oy) != (0, 0)]
    pieces = []
    layouts = []
    for offset in offsets:
        piece = shard
        thin = []
        for step, dim in zip(offset, dims):
            length = piece.shape[dim]
            if step == 1:
                piece = lax.slice_in_dim(piece, length - width, length, axis=dim)
            elif step == -1:
                piece = lax.slice_in_dim(piece, 0, width, axis=dim)
            if step != 0:
                thin.append(dim)
        piece, moved = as_rows(piece, thin)
        pieces.append(piece)
        layouts.append((moved, thin))
    key = ("plane",) + tuple(piece.shape for piece in pieces)
    if key not in HALO_IDS:
        HALO_IDS[key] = len(HALO_IDS)
    sizes = tuple(lax.axis_size(axis) for axis in axes)
    kernel = functools.partial(plane_kernel, axes=axes, sizes=sizes, offsets=tuple(offsets))
    vmem = pl.BlockSpec(memory_space=pltpu.VMEM)
    shapes = tuple(jax.ShapeDtypeStruct(piece.shape, piece.dtype) for piece in pieces)
    received = pl.pallas_call(
        kernel,
        out_shape=shapes,
        in_specs=[vmem] * len(pieces),
        out_specs=tuple([vmem] * len(pieces)),
        scratch_shapes=[pltpu.VMEM(piece.shape, piece.dtype) for piece in pieces]
        + [pltpu.SemaphoreType.DMA((len(pieces),)), pltpu.SemaphoreType.DMA((len(pieces),))],
        compiler_params=pltpu.CompilerParams(collective_id=HALO_IDS[key], has_side_effects=True),
    )(*pieces)
    got = {offset: from_rows(piece, *layout) for offset, piece, layout in zip(offsets, received, layouts)}
    got[(0, 0)] = shard
    rows = []
    for ox in (-1, 0, 1):
        rows.append(jnp.concatenate([got[(ox, oy)] for oy in (-1, 0, 1)], axis=dims[1]))
    return jnp.concatenate(rows, axis=dims[0])


def with_halo(shard, sides, width):
    for axis, dim in sides:
        length = shard.shape[dim]
        last = lax.slice_in_dim(shard, length - width, length, axis=dim)
        initial = lax.slice_in_dim(shard, 0, width, axis=dim)
        tiled = math.prod(initial.shape[:-2]) * -(-initial.shape[-2] // 8) * 8 * -(-initial.shape[-1] // 128) * 128
        if tiled <= 3 * initial.size:
            before, after = exchange(initial, last, axis)
        else:
            moved = jnp.moveaxis(initial, dim, 0).shape
            rows = (-1, moved[-1])
            before, after = exchange(
                jnp.moveaxis(initial, dim, 0).reshape(rows), jnp.moveaxis(last, dim, 0).reshape(rows), axis
            )
            before = jnp.moveaxis(before.reshape(moved), 0, dim)
            after = jnp.moveaxis(after.reshape(moved), 0, dim)
        shard = jnp.concatenate([before, shard, after], axis=dim)
    return shard


def recover(local_nodes, corner_vals, ratio_z):
    ex = local_nodes.shape[1] - 1
    ey = local_nodes.shape[2] - 1
    ratio_x = jnp.arange(ex + 1, dtype=jnp.float32) / ex
    ratio_y = jnp.arange(ey + 1, dtype=jnp.float32) / ey
    planes = []
    for high_z in (0, 1):
        plane = None
        for corner in range(high_z, 8, 2):
            along_x = ratio_x if corner // 4 == 1 else 1.0 - ratio_x
            along_y = ratio_y if corner // 2 % 2 == 1 else 1.0 - ratio_y
            basis = along_x[:, None] * along_y[None, :]
            term = basis[None] * corner_vals[:, corner][:, None, None]
            plane = term if plane is None else plane + term
        planes.append(plane[:, :, :, None])
    return local_nodes + planes[0] * (1.0 - ratio_z) + planes[1] * ratio_z


def average_rows(extended, dim, has_lower, has_upper):
    inner = extended.shape[dim] - 2
    own_rows = lax.slice_in_dim(extended, 1, inner + 1, axis=dim)
    rim_low = lax.slice_in_dim(extended, 0, 1, axis=dim)
    rim_high = lax.slice_in_dim(extended, inner + 1, inner + 2, axis=dim)
    shape_row = [1] * extended.ndim
    shape_row[dim] = inner
    rows = jnp.arange(inner, dtype=jnp.int32).reshape(shape_row)
    is_low = rows == 0
    is_high = rows == inner - 1
    factor = jnp.where(is_low & has_lower, 0.5, jnp.where(is_high & has_upper, 0.5, 1.0))
    rim_part = jnp.where(is_low, rim_low, 0.0) + jnp.where(is_high, rim_high, 0.0)
    return own_rows * factor + rim_part * 0.5


def energy_kernel(stiffness, base, up_y, up_z, up_yz, out, weights, *, count_x, chunks):
    sources = (base, up_z, up_y, up_yz)
    for a in range(24):
        weights[a * 24 + a] = stiffness[a, a]
        for b in range(a + 1, 24):
            weights[a * 24 + b] = stiffness[a, b] + stiffness[b, a]

    def row(i, carry):
        for first in chunks:
            vectors = []
            for component in range(3):
                for corner in range(8):
                    shift_x = corner // 4
                    source = sources[corner % 4]
                    vectors.append(source[component, i + shift_x, pl.ds(first, 8), :])
            total = None
            for a in range(24):
                inner = weights[a * 24 + a] * vectors[a]
                for b in range(a + 1, 24):
                    inner = inner + weights[a * 24 + b] * vectors[b]
                term = vectors[a] * inner
                total = term if total is None else total + term
            if first % 8 == 0:
                out[i, pl.ds(first, 8), :] = total
            else:
                keep = 8 - first % 8
                out[i, pl.ds(first + 8 - keep, keep), :] = total[8 - keep :]
        return carry

    lax.fori_loop(0, count_x, row, 0)


def element_energy(nodes, stiffness):
    count_x = nodes.shape[1] - 1
    count_y = nodes.shape[2] - 1
    count_z = nodes.shape[3] - 1
    shifted = [nodes[:, :, dy : dy + count_y, dz : dz + count_z] for dy, dz in ((0, 0), (1, 0), (0, 1), (1, 1))]
    chunks = tuple(range(0, count_y - 7, 8))
    if count_y % 8:
        chunks = chunks + (count_y - 8,)
    kernel = functools.partial(energy_kernel, count_x=count_x, chunks=chunks)
    vmem = pl.BlockSpec(memory_space=pltpu.VMEM)
    energy = pl.pallas_call(
        kernel,
        out_shape=jax.ShapeDtypeStruct((count_x, count_y, count_z), jnp.float32),
        in_specs=[pl.BlockSpec(memory_space=pltpu.SMEM)] + [vmem] * 4,
        out_specs=vmem,
        scratch_shapes=[pltpu.SMEM((24 * 24,), jnp.float32)],
    )(stiffness, *shifted)
    return energy


def smooth(field, axis, count):
    summed = None
    for offset in range(-RADIUS, RADIUS + 1):
        term_piece = lax.slice_in_dim(field, RADIUS + offset, RADIUS + offset + count, axis=axis)
        term_value = float(RADIUS + 1 - abs(offset)) * term_piece
        summed = term_value if summed is None else summed + term_value
    return summed


def edge_counts(count, position, parts):
    places = position * count + jnp.arange(count, dtype=jnp.int32)
    summed = None
    for offset in range(-RADIUS, RADIUS + 1):
        inside = ((places + offset >= 0) & (places + offset < count * parts)).astype(jnp.float32)
        term_value = float(RADIUS + 1 - abs(offset)) * inside
        summed = term_value if summed is None else summed + term_value
    return summed


def filter_field(field, sides):
    (axis_x, dim_x), (axis_y, dim_y), (axis_z, dim_z) = sides
    count_x, count_y = field.shape[dim_x], field.shape[dim_y]
    padded = with_plane_halo(field, (axis_x, axis_y), (dim_x, dim_y), RADIUS)
    field = smooth(smooth(padded, dim_x, count_x), dim_y, count_y)
    padded = with_halo(field, ((axis_z, dim_z),), RADIUS)
    return smooth(padded, dim_z, field.shape[dim_z])


def local(local_solution, top_nodes, coarse_solution, corner_dofs, density, element_stiffness):
    count_x, count_y, count_z = density.shape
    index_x = lax.axis_index("gx")
    index_y = lax.axis_index("gy")
    index_z = lax.axis_index("gz")
    normalizer = (
        edge_counts(count_x, index_x, lax.axis_size("gx"))[:, None, None]
        * edge_counts(count_y, index_y, lax.axis_size("gy"))[None, :, None]
        * edge_counts(count_z, index_z, lax.axis_size("gz"))[None, None, :]
    )
    sides = (("gx", 1), ("gy", 2), ("gz", 3))
    wanted = corner_dofs.reshape(8)
    gathered = gather_peers(coarse_solution, "gz")
    columns = gathered.transpose(1, 0, 2).reshape(coarse_solution.shape[0], -1)
    matches = wanted[:, None] == jnp.arange(columns.shape[1], dtype=jnp.int32)[None, :]
    corner_vals = jnp.sum(jnp.where(matches[None], columns[:, None, :], 0.0), axis=2)
    depth = local_solution.shape[3]
    full = jnp.concatenate([local_solution, top_nodes], axis=3)
    nodes = recover(full, corner_vals, jnp.arange(depth + 1, dtype=jnp.float32) / depth)
    lower_x = index_x > 0
    upper_x = index_x < lax.axis_size("gx") - 1
    lower_y = index_y > 0
    upper_y = index_y < lax.axis_size("gy") - 1
    lower_z = index_z > 0
    upper_z = index_z < lax.axis_size("gz") - 1
    extended = with_plane_halo(nodes, ("gx", "gy"), (1, 2), 1)
    extended = average_rows(extended, 1, lower_x, upper_x)
    averaged = average_rows(extended, 2, lower_y, upper_y)
    extended = with_halo(averaged, (("gz", 3),), 1)
    averaged = average_rows(extended, 3, lower_z, upper_z)
    energy = element_energy(averaged, element_stiffness)
    sens = penal_scale * density * density * energy
    smoothed = filter_field(jnp.stack([density * sens, density]), sides)
    numerator = smoothed[0]
    smooth_density = smoothed[1]
    return (numerator / (density * normalizer), smooth_density / normalizer)


def solution(mesh):
    in_specs = (
        P(None, "gx", "gy", "gz"),
        P(None, "gx", "gy", "gz"),
        P(None, "gz"),
        P("gx", "gy", "gz", None),
        P("gx", "gy", "gz"),
        P(),
    )
    out_specs = (P("gx", "gy", "gz"), P("gx", "gy", "gz"))
    return jax.shard_map(local, mesh=mesh, in_specs=in_specs, out_specs=out_specs, check_vma=False)
```

```python
import functools
import math

import jax
import jax.numpy as jnp
from jax import lax
from jax.sharding import PartitionSpec as P
from jax.experimental import pallas as pl
from jax.experimental.pallas import tpu as pltpu

RADIUS = 3


penal_scale = -3.0 / 96.0


def halo_kernel(low, high, before, after, landed_before, landed_after, send_sem, recv_sem, *, axis, count):
    me = lax.axis_index(axis)
    has_lower = me > 0
    has_upper = me < count - 1
    mesh_ids = pl.DeviceIdType.MESH
    barrier = pltpu.get_barrier_semaphore()

    @pl.when(has_lower)
    def _():
        pl.semaphore_signal(barrier, 1, device_id={axis: me - 1}, device_id_type=mesh_ids)

    @pl.when(has_upper)
    def _():
        pl.semaphore_signal(barrier, 1, device_id={axis: me + 1}, device_id_type=mesh_ids)

    pl.semaphore_wait(barrier, has_lower.astype(jnp.int32) + has_upper.astype(jnp.int32))

    to_upper = pltpu.make_async_remote_copy(
        src_ref=high,
        dst_ref=landed_before,
        send_sem=send_sem.at[0],
        recv_sem=recv_sem.at[0],
        device_id={axis: me + 1},
        device_id_type=mesh_ids,
    )
    to_lower = pltpu.make_async_remote_copy(
        src_ref=low,
        dst_ref=landed_after,
        send_sem=send_sem.at[1],
        recv_sem=recv_sem.at[1],
        device_id={axis: me - 1},
        device_id_type=mesh_ids,
    )

    @pl.when(has_upper)
    def _():
        to_upper.start()

    @pl.when(has_lower)
    def _():
        to_lower.start()

    @pl.when(has_upper)
    def _():
        to_upper.wait_send()
        to_lower.wait_recv()
        after[...] = landed_after[...]

    @pl.when(has_lower)
    def _():
        to_lower.wait_send()
        to_upper.wait_recv()
        before[...] = landed_before[...]

    @pl.when(jnp.logical_not(has_upper))
    def _():
        after[...] = jnp.zeros(after.shape, after.dtype)

    @pl.when(jnp.logical_not(has_lower))
    def _():
        before[...] = jnp.zeros(before.shape, before.dtype)


HALO_IDS = {}


def exchange(low, high, axis):
    key = (axis, low.shape)
    if key not in HALO_IDS:
        HALO_IDS[key] = len(HALO_IDS)
    kernel = functools.partial(halo_kernel, axis=axis, count=lax.axis_size(axis))
    vmem = pl.BlockSpec(memory_space=pltpu.VMEM)
    slab = jax.ShapeDtypeStruct(low.shape, low.dtype)
    return pl.pallas_call(
        kernel,
        out_shape=(slab, slab),
        in_specs=[vmem, vmem],
        out_specs=(vmem, vmem),
        scratch_shapes=[
            pltpu.VMEM(low.shape, low.dtype),
            pltpu.VMEM(low.shape, low.dtype),
            pltpu.SemaphoreType.DMA((2,)),
            pltpu.SemaphoreType.DMA((2,)),
        ],
        compiler_params=pltpu.CompilerParams(collective_id=HALO_IDS[key], has_side_effects=True),
    )(low, high)


def gather_kernel(shard, out, landed, send_sem, recv_sem, *, axis, count):
    me = lax.axis_index(axis)
    mesh_ids = pl.DeviceIdType.MESH
    barrier = pltpu.get_barrier_semaphore()
    for peer in range(count):

        @pl.when(peer != me)
        def _():
            pl.semaphore_signal(barrier, 1, device_id={axis: peer}, device_id_type=mesh_ids)

    pl.semaphore_wait(barrier, count - 1)
    copies = []
    for peer in range(count):
        copies.append(
            pltpu.make_async_remote_copy(
                src_ref=shard,
                dst_ref=landed.at[me],
                send_sem=send_sem.at[peer],
                recv_sem=recv_sem.at[me],
                device_id={axis: peer},
                device_id_type=mesh_ids,
            )
        )

        @pl.when(peer != me)
        def _():
            copies[peer].start()

    for peer in range(count):
        incoming = pltpu.make_async_remote_copy(
            src_ref=shard,
            dst_ref=landed.at[peer],
            send_sem=send_sem.at[peer],
            recv_sem=recv_sem.at[peer],
            device_id={axis: peer},
            device_id_type=mesh_ids,
        )

        @pl.when(peer != me)
        def _():
            copies[peer].wait_send()
            incoming.wait_recv()
            out[peer] = landed[peer]

    out[me] = shard[...]


def gather_peers(shard, axis):
    count = lax.axis_size(axis)
    kernel = functools.partial(gather_kernel, axis=axis, count=count)
    vmem = pl.BlockSpec(memory_space=pltpu.VMEM)
    stacked = (count,) + shard.shape
    return pl.pallas_call(
        kernel,
        out_shape=jax.ShapeDtypeStruct(stacked, shard.dtype),
        in_specs=[vmem],
        out_specs=vmem,
        scratch_shapes=[
            pltpu.VMEM(stacked, shard.dtype),
            pltpu.SemaphoreType.DMA((count,)),
            pltpu.SemaphoreType.DMA((count,)),
        ],
        compiler_params=pltpu.CompilerParams(collective_id=100, has_side_effects=True),
    )(shard)


def plane_kernel(*refs, axes, sizes, offsets):
    count = len(offsets)
    sends = refs[:count]
    outs = refs[count : 2 * count]
    landed = refs[2 * count : 3 * count]
    send_sem, recv_sem = refs[3 * count :]
    me = [lax.axis_index(axis) for axis in axes]
    mesh_ids = pl.DeviceIdType.MESH

    def exists(offset):
        inside = None
        for position, step, size in zip(me, offset, sizes):
            if step == 0:
                continue
            here = (position + step >= 0) & (position + step < size)
            inside = here if inside is None else inside & here
        return inside

    def target(offset):
        return {axis: position + step for axis, position, step in zip(axes, me, offset)}

    barrier = pltpu.get_barrier_semaphore()
    expected = 0
    for offset in offsets:

        @pl.when(exists(offset))
        def _():
            pl.semaphore_signal(barrier, 1, device_id=target(offset), device_id_type=mesh_ids)

        expected = expected + exists(offset).astype(jnp.int32)
    pl.semaphore_wait(barrier, expected)
    slot = {offset: k for k, offset in enumerate(offsets)}
    outgoing = []
    for k, offset in enumerate(offsets):
        back = slot[tuple(-step for step in offset)]
        outgoing.append(
            pltpu.make_async_remote_copy(
                src_ref=sends[k],
                dst_ref=landed[back],
                send_sem=send_sem.at[k],
                recv_sem=recv_sem.at[back],
                device_id=target(offset),
                device_id_type=mesh_ids,
            )
        )

        @pl.when(exists(offset))
        def _():
            outgoing[k].start()

    for k, offset in enumerate(offsets):
        back = slot[tuple(-step for step in offset)]
        incoming = pltpu.make_async_remote_copy(
            src_ref=sends[back],
            dst_ref=landed[k],
            send_sem=send_sem.at[back],
            recv_sem=recv_sem.at[k],
            device_id=target(offset),
            device_id_type=mesh_ids,
        )

        @pl.when(exists(offset))
        def _():
            outgoing[k].wait_send()
            incoming.wait_recv()
            outs[k][...] = landed[k][...]

        @pl.when(jnp.logical_not(exists(offset)))
        def _():
            outs[k][...] = jnp.zeros(outs[k].shape, outs[k].dtype)


def as_rows(piece, thin):
    tiled = math.prod(piece.shape[:-2]) * -(-piece.shape[-2] // 8) * 8 * -(-piece.shape[-1] // 128) * 128
    if tiled <= 3 * piece.size or tiled <= 65536:
        return piece, None
    moved = jnp.moveaxis(piece, thin, tuple(range(len(thin))))
    return moved.reshape(-1, moved.shape[-1]), moved.shape


def from_rows(piece, moved, thin):
    if moved is None:
        return piece
    return jnp.moveaxis(piece.reshape(moved), tuple(range(len(thin))), thin)


def with_plane_halo(shard, axes, dims, width):
    offsets = [(ox, oy) for ox in (-1, 0, 1) for oy in (-1, 0, 1) if (ox, oy) != (0, 0)]
    pieces = []
    layouts = []
    for offset in offsets:
        piece = shard
        thin = []
        for step, dim in zip(offset, dims):
            length = piece.shape[dim]
            if step == 1:
                piece = lax.slice_in_dim(piece, length - width, length, axis=dim)
            elif step == -1:
                piece = lax.slice_in_dim(piece, 0, width, axis=dim)
            if step != 0:
                thin.append(dim)
        piece, moved = as_rows(piece, thin)
        pieces.append(piece)
        layouts.append((moved, thin))
    key = ("plane",) + tuple(piece.shape for piece in pieces)
    if key not in HALO_IDS:
        HALO_IDS[key] = len(HALO_IDS)
    sizes = tuple(lax.axis_size(axis) for axis in axes)
    kernel = functools.partial(plane_kernel, axes=axes, sizes=sizes, offsets=tuple(offsets))
    vmem = pl.BlockSpec(memory_space=pltpu.VMEM)
    shapes = tuple(jax.ShapeDtypeStruct(piece.shape, piece.dtype) for piece in pieces)
    received = pl.pallas_call(
        kernel,
        out_shape=shapes,
        in_specs=[vmem] * len(pieces),
        out_specs=tuple([vmem] * len(pieces)),
        scratch_shapes=[pltpu.VMEM(piece.shape, piece.dtype) for piece in pieces]
        + [pltpu.SemaphoreType.DMA((len(pieces),)), pltpu.SemaphoreType.DMA((len(pieces),))],
        compiler_params=pltpu.CompilerParams(collective_id=HALO_IDS[key], has_side_effects=True),
    )(*pieces)
    got = {offset: from_rows(piece, *layout) for offset, piece, layout in zip(offsets, received, layouts)}
    got[(0, 0)] = shard
    rows = []
    for ox in (-1, 0, 1):
        rows.append(jnp.concatenate([got[(ox, oy)] for oy in (-1, 0, 1)], axis=dims[1]))
    return jnp.concatenate(rows, axis=dims[0])


def with_halo(shard, sides, width):
    for axis, dim in sides:
        length = shard.shape[dim]
        last = lax.slice_in_dim(shard, length - width, length, axis=dim)
        initial = lax.slice_in_dim(shard, 0, width, axis=dim)
        tiled = math.prod(initial.shape[:-2]) * -(-initial.shape[-2] // 8) * 8 * -(-initial.shape[-1] // 128) * 128
        if tiled <= 3 * initial.size:
            before, after = exchange(initial, last, axis)
        else:
            moved = jnp.moveaxis(initial, dim, 0).shape
            rows = (-1, moved[-1])
            before, after = exchange(
                jnp.moveaxis(initial, dim, 0).reshape(rows), jnp.moveaxis(last, dim, 0).reshape(rows), axis
            )
            before = jnp.moveaxis(before.reshape(moved), 0, dim)
            after = jnp.moveaxis(after.reshape(moved), 0, dim)
        shard = jnp.concatenate([before, shard, after], axis=dim)
    return shard


def recover(local_nodes, corner_vals, ratio_z):
    ex = local_nodes.shape[1] - 1
    ey = local_nodes.shape[2] - 1
    ratio_x = jnp.arange(ex + 1, dtype=jnp.float32) / ex
    ratio_y = jnp.arange(ey + 1, dtype=jnp.float32) / ey
    planes = []
    for high_z in (0, 1):
        plane = None
        for corner in range(high_z, 8, 2):
            along_x = ratio_x if corner // 4 == 1 else 1.0 - ratio_x
            along_y = ratio_y if corner // 2 % 2 == 1 else 1.0 - ratio_y
            basis = along_x[:, None] * along_y[None, :]
            term = basis[None] * corner_vals[:, corner][:, None, None]
            plane = term if plane is None else plane + term
        planes.append(plane[:, :, :, None])
    return local_nodes + planes[0] * (1.0 - ratio_z) + planes[1] * ratio_z


def average_rows(extended, dim, has_lower, has_upper):
    inner = extended.shape[dim] - 2
    own_rows = lax.slice_in_dim(extended, 1, inner + 1, axis=dim)
    rim_low = lax.slice_in_dim(extended, 0, 1, axis=dim)
    rim_high = lax.slice_in_dim(extended, inner + 1, inner + 2, axis=dim)
    shape_row = [1] * extended.ndim
    shape_row[dim] = inner
    rows = jnp.arange(inner, dtype=jnp.int32).reshape(shape_row)
    is_low = rows == 0
    is_high = rows == inner - 1
    factor = jnp.where(is_low & has_lower, 0.5, jnp.where(is_high & has_upper, 0.5, 1.0))
    rim_part = jnp.where(is_low, rim_low, 0.0) + jnp.where(is_high, rim_high, 0.0)
    return own_rows * factor + rim_part * 0.5


def energy_kernel(stiffness, nodes, out, weights, *, count_x, chunks):
    for a in range(24):
        weights[a * 24 + a] = stiffness[a, a]
        for b in range(a + 1, 24):
            weights[a * 24 + b] = stiffness[a, b] + stiffness[b, a]

    def row(i, carry):
        for first in chunks:
            vectors = []
            for component in range(3):
                for corner in range(8):
                    shift_x = corner // 4
                    shift_y = corner // 2 % 2
                    shift_z = corner % 2
                    vectors.append(nodes[component, i + shift_x, pl.ds(first + shift_y, 8), pl.ds(shift_z, 128)])
            total = None
            for a in range(24):
                inner = weights[a * 24 + a] * vectors[a]
                for b in range(a + 1, 24):
                    inner = inner + weights[a * 24 + b] * vectors[b]
                term = vectors[a] * inner
                total = term if total is None else total + term
            if first % 8 == 0:
                out[i, pl.ds(first, 8), :] = total
            else:
                keep = 8 - first % 8
                out[i, pl.ds(first + 8 - keep, keep), :] = total[8 - keep :]
        return carry

    lax.fori_loop(0, count_x, row, 0)


def element_energy(nodes, stiffness):
    count_x = nodes.shape[1] - 1
    count_y = nodes.shape[2] - 1
    count_z = nodes.shape[3] - 1
    chunks = tuple(range(0, count_y - 7, 8))
    if count_y % 8:
        chunks = chunks + (count_y - 8,)
    kernel = functools.partial(energy_kernel, count_x=count_x, chunks=chunks)
    vmem = pl.BlockSpec(memory_space=pltpu.VMEM)
    energy = pl.pallas_call(
        kernel,
        out_shape=jax.ShapeDtypeStruct((count_x, count_y, count_z), jnp.float32),
        in_specs=[pl.BlockSpec(memory_space=pltpu.SMEM), vmem],
        out_specs=vmem,
        scratch_shapes=[pltpu.SMEM((24 * 24,), jnp.float32)],
    )(stiffness, nodes)
    return energy


def smooth(field, axis, count):
    summed = None
    for offset in range(-RADIUS, RADIUS + 1):
        term_piece = lax.slice_in_dim(field, RADIUS + offset, RADIUS + offset + count, axis=axis)
        term_value = float(RADIUS + 1 - abs(offset)) * term_piece
        summed = term_value if summed is None else summed + term_value
    return summed


def edge_counts(count, position, parts):
    places = position * count + jnp.arange(count, dtype=jnp.int32)
    summed = None
    for offset in range(-RADIUS, RADIUS + 1):
        inside = ((places + offset >= 0) & (places + offset < count * parts)).astype(jnp.float32)
        term_value = float(RADIUS + 1 - abs(offset)) * inside
        summed = term_value if summed is None else summed + term_value
    return summed


def filter_field(field, sides):
    (axis_x, dim_x), (axis_y, dim_y), (axis_z, dim_z) = sides
    count_x, count_y = field.shape[dim_x], field.shape[dim_y]
    padded = with_plane_halo(field, (axis_x, axis_y), (dim_x, dim_y), RADIUS)
    field = smooth(smooth(padded, dim_x, count_x), dim_y, count_y)
    padded = with_halo(field, ((axis_z, dim_z),), RADIUS)
    return smooth(padded, dim_z, field.shape[dim_z])


def local(local_solution, top_nodes, coarse_solution, corner_dofs, density, element_stiffness):
    count_x, count_y, count_z = density.shape
    index_x = lax.axis_index("gx")
    index_y = lax.axis_index("gy")
    index_z = lax.axis_index("gz")
    normalizer = (
        edge_counts(count_x, index_x, lax.axis_size("gx"))[:, None, None]
        * edge_counts(count_y, index_y, lax.axis_size("gy"))[None, :, None]
        * edge_counts(count_z, index_z, lax.axis_size("gz"))[None, None, :]
    )
    sides = (("gx", 1), ("gy", 2), ("gz", 3))
    wanted = corner_dofs.reshape(8)
    gathered = gather_peers(coarse_solution, "gz")
    columns = gathered.transpose(1, 0, 2).reshape(coarse_solution.shape[0], -1)
    matches = wanted[:, None] == jnp.arange(columns.shape[1], dtype=jnp.int32)[None, :]
    corner_vals = jnp.sum(jnp.where(matches[None], columns[:, None, :], 0.0), axis=2)
    depth = local_solution.shape[3]
    full = jnp.concatenate([local_solution, top_nodes], axis=3)
    nodes = recover(full, corner_vals, jnp.arange(depth + 1, dtype=jnp.float32) / depth)
    lower_x = index_x > 0
    upper_x = index_x < lax.axis_size("gx") - 1
    lower_y = index_y > 0
    upper_y = index_y < lax.axis_size("gy") - 1
    lower_z = index_z > 0
    upper_z = index_z < lax.axis_size("gz") - 1
    extended = with_plane_halo(nodes, ("gx", "gy"), (1, 2), 1)
    extended = average_rows(extended, 1, lower_x, upper_x)
    averaged = average_rows(extended, 2, lower_y, upper_y)
    extended = with_halo(averaged, (("gz", 3),), 1)
    averaged = average_rows(extended, 3, lower_z, upper_z)
    energy = element_energy(averaged, element_stiffness)
    sens = penal_scale * density * density * energy
    smoothed = filter_field(jnp.stack([density * sens, density]), sides)
    numerator = smoothed[0]
    smooth_density = smoothed[1]
    return (numerator / (density * normalizer), smooth_density / normalizer)


def solution(mesh):
    in_specs = (
        P(None, "gx", "gy", "gz"),
        P(None, "gx", "gy", "gz"),
        P(None, "gz"),
        P("gx", "gy", "gz", None),
        P("gx", "gy", "gz"),
        P(),
    )
    out_specs = (P("gx", "gy", "gz"), P("gx", "gy", "gz"))
    return jax.shard_map(local, mesh=mesh, in_specs=in_specs, out_specs=out_specs, check_vma=False)
```

```python
import functools
import math

import jax
import jax.numpy as jnp
from jax import lax
from jax.sharding import PartitionSpec as P
from jax.experimental import pallas as pl
from jax.experimental.pallas import tpu as pltpu

RADIUS = 3


penal_scale = -3.0 / 96.0


def halo_kernel(low, high, before, after, landed_before, landed_after, send_sem, recv_sem, *, axis, count):
    me = lax.axis_index(axis)
    has_lower = me > 0
    has_upper = me < count - 1
    mesh_ids = pl.DeviceIdType.MESH
    barrier = pltpu.get_barrier_semaphore()

    @pl.when(has_lower)
    def _():
        pl.semaphore_signal(barrier, 1, device_id={axis: me - 1}, device_id_type=mesh_ids)

    @pl.when(has_upper)
    def _():
        pl.semaphore_signal(barrier, 1, device_id={axis: me + 1}, device_id_type=mesh_ids)

    pl.semaphore_wait(barrier, has_lower.astype(jnp.int32) + has_upper.astype(jnp.int32))

    to_upper = pltpu.make_async_remote_copy(
        src_ref=high,
        dst_ref=landed_before,
        send_sem=send_sem.at[0],
        recv_sem=recv_sem.at[0],
        device_id={axis: me + 1},
        device_id_type=mesh_ids,
    )
    to_lower = pltpu.make_async_remote_copy(
        src_ref=low,
        dst_ref=landed_after,
        send_sem=send_sem.at[1],
        recv_sem=recv_sem.at[1],
        device_id={axis: me - 1},
        device_id_type=mesh_ids,
    )

    @pl.when(has_upper)
    def _():
        to_upper.start()

    @pl.when(has_lower)
    def _():
        to_lower.start()

    @pl.when(has_upper)
    def _():
        to_upper.wait_send()
        to_lower.wait_recv()
        after[...] = landed_after[...]

    @pl.when(has_lower)
    def _():
        to_lower.wait_send()
        to_upper.wait_recv()
        before[...] = landed_before[...]

    @pl.when(jnp.logical_not(has_upper))
    def _():
        after[...] = jnp.zeros(after.shape, after.dtype)

    @pl.when(jnp.logical_not(has_lower))
    def _():
        before[...] = jnp.zeros(before.shape, before.dtype)


HALO_IDS = {}


def exchange(low, high, axis):
    key = (axis, low.shape)
    if key not in HALO_IDS:
        HALO_IDS[key] = len(HALO_IDS)
    kernel = functools.partial(halo_kernel, axis=axis, count=lax.axis_size(axis))
    vmem = pl.BlockSpec(memory_space=pltpu.VMEM)
    slab = jax.ShapeDtypeStruct(low.shape, low.dtype)
    return pl.pallas_call(
        kernel,
        out_shape=(slab, slab),
        in_specs=[vmem, vmem],
        out_specs=(vmem, vmem),
        scratch_shapes=[
            pltpu.VMEM(low.shape, low.dtype),
            pltpu.VMEM(low.shape, low.dtype),
            pltpu.SemaphoreType.DMA((2,)),
            pltpu.SemaphoreType.DMA((2,)),
        ],
        compiler_params=pltpu.CompilerParams(collective_id=HALO_IDS[key], has_side_effects=True),
    )(low, high)


def gather_kernel(shard, out, landed, send_sem, recv_sem, *, axis, count):
    me = lax.axis_index(axis)
    mesh_ids = pl.DeviceIdType.MESH
    barrier = pltpu.get_barrier_semaphore()
    for peer in range(count):

        @pl.when(peer != me)
        def _():
            pl.semaphore_signal(barrier, 1, device_id={axis: peer}, device_id_type=mesh_ids)

    pl.semaphore_wait(barrier, count - 1)
    copies = []
    for peer in range(count):
        copies.append(
            pltpu.make_async_remote_copy(
                src_ref=shard,
                dst_ref=landed.at[me],
                send_sem=send_sem.at[peer],
                recv_sem=recv_sem.at[me],
                device_id={axis: peer},
                device_id_type=mesh_ids,
            )
        )

        @pl.when(peer != me)
        def _():
            copies[peer].start()

    for peer in range(count):
        incoming = pltpu.make_async_remote_copy(
            src_ref=shard,
            dst_ref=landed.at[peer],
            send_sem=send_sem.at[peer],
            recv_sem=recv_sem.at[peer],
            device_id={axis: peer},
            device_id_type=mesh_ids,
        )

        @pl.when(peer != me)
        def _():
            copies[peer].wait_send()
            incoming.wait_recv()
            out[peer] = landed[peer]

    out[me] = shard[...]


def gather_peers(shard, axis):
    count = lax.axis_size(axis)
    kernel = functools.partial(gather_kernel, axis=axis, count=count)
    vmem = pl.BlockSpec(memory_space=pltpu.VMEM)
    stacked = (count,) + shard.shape
    return pl.pallas_call(
        kernel,
        out_shape=jax.ShapeDtypeStruct(stacked, shard.dtype),
        in_specs=[vmem],
        out_specs=vmem,
        scratch_shapes=[
            pltpu.VMEM(stacked, shard.dtype),
            pltpu.SemaphoreType.DMA((count,)),
            pltpu.SemaphoreType.DMA((count,)),
        ],
        compiler_params=pltpu.CompilerParams(collective_id=100, has_side_effects=True),
    )(shard)


def plane_kernel(*refs, axes, sizes, offsets):
    count = len(offsets)
    sends = refs[:count]
    outs = refs[count : 2 * count]
    landed = refs[2 * count : 3 * count]
    send_sem, recv_sem = refs[3 * count :]
    me = [lax.axis_index(axis) for axis in axes]
    mesh_ids = pl.DeviceIdType.MESH

    def exists(offset):
        inside = None
        for position, step, size in zip(me, offset, sizes):
            if step == 0:
                continue
            here = (position + step >= 0) & (position + step < size)
            inside = here if inside is None else inside & here
        return inside

    def target(offset):
        return {axis: position + step for axis, position, step in zip(axes, me, offset)}

    barrier = pltpu.get_barrier_semaphore()
    expected = 0
    for offset in offsets:

        @pl.when(exists(offset))
        def _():
            pl.semaphore_signal(barrier, 1, device_id=target(offset), device_id_type=mesh_ids)

        expected = expected + exists(offset).astype(jnp.int32)
    pl.semaphore_wait(barrier, expected)
    slot = {offset: k for k, offset in enumerate(offsets)}
    outgoing = []
    for k, offset in enumerate(offsets):
        back = slot[tuple(-step for step in offset)]
        outgoing.append(
            pltpu.make_async_remote_copy(
                src_ref=sends[k],
                dst_ref=landed[back],
                send_sem=send_sem.at[k],
                recv_sem=recv_sem.at[back],
                device_id=target(offset),
                device_id_type=mesh_ids,
            )
        )

        @pl.when(exists(offset))
        def _():
            outgoing[k].start()

    for k, offset in enumerate(offsets):
        back = slot[tuple(-step for step in offset)]
        incoming = pltpu.make_async_remote_copy(
            src_ref=sends[back],
            dst_ref=landed[k],
            send_sem=send_sem.at[back],
            recv_sem=recv_sem.at[k],
            device_id=target(offset),
            device_id_type=mesh_ids,
        )

        @pl.when(exists(offset))
        def _():
            outgoing[k].wait_send()
            incoming.wait_recv()
            outs[k][...] = landed[k][...]

        @pl.when(jnp.logical_not(exists(offset)))
        def _():
            outs[k][...] = jnp.zeros(outs[k].shape, outs[k].dtype)


def as_rows(piece, thin):
    sublanes = 1 if piece.shape[-2] == 1 else -(-piece.shape[-2] // 8) * 8
    tiled = math.prod(piece.shape[:-2]) * sublanes * -(-piece.shape[-1] // 128) * 128
    if tiled <= 3 * piece.size or tiled <= 65536:
        return piece, None
    moved = jnp.moveaxis(piece, thin, tuple(range(len(thin))))
    return moved.reshape(-1, moved.shape[-1]), moved.shape


def from_rows(piece, moved, thin):
    if moved is None:
        return piece
    return jnp.moveaxis(piece.reshape(moved), tuple(range(len(thin))), thin)


def with_plane_halo(shard, axes, dims, width):
    offsets = [(ox, oy) for ox in (-1, 0, 1) for oy in (-1, 0, 1) if (ox, oy) != (0, 0)]
    pieces = []
    layouts = []
    for offset in offsets:
        piece = shard
        thin = []
        for step, dim in zip(offset, dims):
            length = piece.shape[dim]
            if step == 1:
                piece = lax.slice_in_dim(piece, length - width, length, axis=dim)
            elif step == -1:
                piece = lax.slice_in_dim(piece, 0, width, axis=dim)
            if step != 0:
                thin.append(dim)
        piece, moved = as_rows(piece, thin)
        pieces.append(piece)
        layouts.append((moved, thin))
    key = ("plane",) + tuple(piece.shape for piece in pieces)
    if key not in HALO_IDS:
        HALO_IDS[key] = len(HALO_IDS)
    sizes = tuple(lax.axis_size(axis) for axis in axes)
    kernel = functools.partial(plane_kernel, axes=axes, sizes=sizes, offsets=tuple(offsets))
    vmem = pl.BlockSpec(memory_space=pltpu.VMEM)
    shapes = tuple(jax.ShapeDtypeStruct(piece.shape, piece.dtype) for piece in pieces)
    received = pl.pallas_call(
        kernel,
        out_shape=shapes,
        in_specs=[vmem] * len(pieces),
        out_specs=tuple([vmem] * len(pieces)),
        scratch_shapes=[pltpu.VMEM(piece.shape, piece.dtype) for piece in pieces]
        + [pltpu.SemaphoreType.DMA((len(pieces),)), pltpu.SemaphoreType.DMA((len(pieces),))],
        compiler_params=pltpu.CompilerParams(collective_id=HALO_IDS[key], has_side_effects=True),
    )(*pieces)
    got = {offset: from_rows(piece, *layout) for offset, piece, layout in zip(offsets, received, layouts)}
    got[(0, 0)] = shard
    rows = []
    for ox in (-1, 0, 1):
        rows.append(jnp.concatenate([got[(ox, oy)] for oy in (-1, 0, 1)], axis=dims[1]))
    return jnp.concatenate(rows, axis=dims[0])


def with_halo(shard, sides, width):
    for axis, dim in sides:
        length = shard.shape[dim]
        last = lax.slice_in_dim(shard, length - width, length, axis=dim)
        initial = lax.slice_in_dim(shard, 0, width, axis=dim)
        tiled = math.prod(initial.shape[:-2]) * -(-initial.shape[-2] // 8) * 8 * -(-initial.shape[-1] // 128) * 128
        if tiled <= 3 * initial.size:
            before, after = exchange(initial, last, axis)
        else:
            moved = jnp.moveaxis(initial, dim, 0).shape
            rows = (-1, moved[-1])
            before, after = exchange(
                jnp.moveaxis(initial, dim, 0).reshape(rows), jnp.moveaxis(last, dim, 0).reshape(rows), axis
            )
            before = jnp.moveaxis(before.reshape(moved), 0, dim)
            after = jnp.moveaxis(after.reshape(moved), 0, dim)
        shard = jnp.concatenate([before, shard, after], axis=dim)
    return shard


def recover(local_nodes, corner_vals, ratio_z):
    ex = local_nodes.shape[1] - 1
    ey = local_nodes.shape[2] - 1
    ratio_x = jnp.arange(ex + 1, dtype=jnp.float32) / ex
    ratio_y = jnp.arange(ey + 1, dtype=jnp.float32) / ey
    planes = []
    for high_z in (0, 1):
        plane = None
        for corner in range(high_z, 8, 2):
            along_x = ratio_x if corner // 4 == 1 else 1.0 - ratio_x
            along_y = ratio_y if corner // 2 % 2 == 1 else 1.0 - ratio_y
            basis = along_x[:, None] * along_y[None, :]
            term = basis[None] * corner_vals[:, corner][:, None, None]
            plane = term if plane is None else plane + term
        planes.append(plane[:, :, :, None])
    return local_nodes + planes[0] * (1.0 - ratio_z) + planes[1] * ratio_z


def average_rows(extended, dim, has_lower, has_upper):
    inner = extended.shape[dim] - 2
    own_rows = lax.slice_in_dim(extended, 1, inner + 1, axis=dim)
    rim_low = lax.slice_in_dim(extended, 0, 1, axis=dim)
    rim_high = lax.slice_in_dim(extended, inner + 1, inner + 2, axis=dim)
    shape_row = [1] * extended.ndim
    shape_row[dim] = inner
    rows = jnp.arange(inner, dtype=jnp.int32).reshape(shape_row)
    is_low = rows == 0
    is_high = rows == inner - 1
    factor = jnp.where(is_low & has_lower, 0.5, jnp.where(is_high & has_upper, 0.5, 1.0))
    rim_part = jnp.where(is_low, rim_low, 0.0) + jnp.where(is_high, rim_high, 0.0)
    return own_rows * factor + rim_part * 0.5


def energy_kernel(stiffness, base, up_y, up_z, up_yz, out, weights, *, count_x, chunks):
    sources = (base, up_z, up_y, up_yz)
    for a in range(24):
        weights[a * 24 + a] = stiffness[a, a]
        for b in range(a + 1, 24):
            weights[a * 24 + b] = stiffness[a, b] + stiffness[b, a]

    def row(i, carry):
        for first in chunks:
            vectors = []
            for component in range(3):
                for corner in range(8):
                    shift_x = corner // 4
                    source = sources[corner % 4]
                    vectors.append(source[component, i + shift_x, pl.ds(first, 8), :])
            total = None
            for a in range(24):
                inner = weights[a * 24 + a] * vectors[a]
                for b in range(a + 1, 24):
                    inner = inner + weights[a * 24 + b] * vectors[b]
                term = vectors[a] * inner
                total = term if total is None else total + term
            if first % 8 == 0:
                out[i, pl.ds(first, 8), :] = total
            else:
                keep = 8 - first % 8
                out[i, pl.ds(first + 8 - keep, keep), :] = total[8 - keep :]
        return carry

    lax.fori_loop(0, count_x, row, 0)


def element_energy(nodes, stiffness):
    count_x = nodes.shape[1] - 1
    count_y = nodes.shape[2] - 1
    count_z = nodes.shape[3] - 1
    shifted = [nodes[:, :, dy : dy + count_y, dz : dz + count_z] for dy, dz in ((0, 0), (1, 0), (0, 1), (1, 1))]
    chunks = tuple(range(0, count_y - 7, 8))
    if count_y % 8:
        chunks = chunks + (count_y - 8,)
    kernel = functools.partial(energy_kernel, count_x=count_x, chunks=chunks)
    vmem = pl.BlockSpec(memory_space=pltpu.VMEM)
    energy = pl.pallas_call(
        kernel,
        out_shape=jax.ShapeDtypeStruct((count_x, count_y, count_z), jnp.float32),
        in_specs=[pl.BlockSpec(memory_space=pltpu.SMEM)] + [vmem] * 4,
        out_specs=vmem,
        scratch_shapes=[pltpu.SMEM((24 * 24,), jnp.float32)],
    )(stiffness, *shifted)
    return energy


def smooth(field, axis, count):
    summed = None
    for offset in range(-RADIUS, RADIUS + 1):
        term_piece = lax.slice_in_dim(field, RADIUS + offset, RADIUS + offset + count, axis=axis)
        term_value = float(RADIUS + 1 - abs(offset)) * term_piece
        summed = term_value if summed is None else summed + term_value
    return summed


def edge_counts(count, position, parts):
    places = position * count + jnp.arange(count, dtype=jnp.int32)
    summed = None
    for offset in range(-RADIUS, RADIUS + 1):
        inside = ((places + offset >= 0) & (places + offset < count * parts)).astype(jnp.float32)
        term_value = float(RADIUS + 1 - abs(offset)) * inside
        summed = term_value if summed is None else summed + term_value
    return summed


def filter_field(field, sides):
    (axis_x, dim_x), (axis_y, dim_y), (axis_z, dim_z) = sides
    count_x, count_y = field.shape[dim_x], field.shape[dim_y]
    padded = with_plane_halo(field, (axis_x, axis_y), (dim_x, dim_y), RADIUS)
    field = smooth(smooth(padded, dim_x, count_x), dim_y, count_y)
    padded = with_halo(field, ((axis_z, dim_z),), RADIUS)
    return smooth(padded, dim_z, field.shape[dim_z])


def local(local_solution, top_nodes, coarse_solution, corner_dofs, density, element_stiffness):
    count_x, count_y, count_z = density.shape
    index_x = lax.axis_index("gx")
    index_y = lax.axis_index("gy")
    index_z = lax.axis_index("gz")
    normalizer = (
        edge_counts(count_x, index_x, lax.axis_size("gx"))[:, None, None]
        * edge_counts(count_y, index_y, lax.axis_size("gy"))[None, :, None]
        * edge_counts(count_z, index_z, lax.axis_size("gz"))[None, None, :]
    )
    sides = (("gx", 1), ("gy", 2), ("gz", 3))
    wanted = corner_dofs.reshape(8)
    gathered = gather_peers(coarse_solution, "gz")
    columns = gathered.transpose(1, 0, 2).reshape(coarse_solution.shape[0], -1)
    matches = wanted[:, None] == jnp.arange(columns.shape[1], dtype=jnp.int32)[None, :]
    corner_vals = jnp.sum(jnp.where(matches[None], columns[:, None, :], 0.0), axis=2)
    depth = local_solution.shape[3]
    full = jnp.concatenate([local_solution, top_nodes], axis=3)
    nodes = recover(full, corner_vals, jnp.arange(depth + 1, dtype=jnp.float32) / depth)
    lower_x = index_x > 0
    upper_x = index_x < lax.axis_size("gx") - 1
    lower_y = index_y > 0
    upper_y = index_y < lax.axis_size("gy") - 1
    lower_z = index_z > 0
    upper_z = index_z < lax.axis_size("gz") - 1
    extended = with_plane_halo(nodes, ("gx", "gy"), (1, 2), 1)
    extended = average_rows(extended, 1, lower_x, upper_x)
    averaged = average_rows(extended, 2, lower_y, upper_y)
    extended = with_halo(averaged, (("gz", 3),), 1)
    averaged = average_rows(extended, 3, lower_z, upper_z)
    energy = element_energy(averaged, element_stiffness)
    sens = penal_scale * density * density * energy
    smoothed = filter_field(jnp.stack([density * sens, density]), sides)
    numerator = smoothed[0]
    smooth_density = smoothed[1]
    return (numerator / (density * normalizer), smooth_density / normalizer)


def solution(mesh):
    in_specs = (
        P(None, "gx", "gy", "gz"),
        P(None, "gx", "gy", "gz"),
        P(None, "gz"),
        P("gx", "gy", "gz", None),
        P("gx", "gy", "gz"),
        P(),
    )
    out_specs = (P("gx", "gy", "gz"), P("gx", "gy", "gz"))
    return jax.shard_map(local, mesh=mesh, in_specs=in_specs, out_specs=out_specs, check_vma=False)
```

```python
import functools
import math

import jax
import jax.numpy as jnp
from jax import lax
from jax.sharding import PartitionSpec as P
from jax.experimental import pallas as pl
from jax.experimental.pallas import tpu as pltpu

RADIUS = 3


penal_scale = -3.0 / 96.0


def halo_kernel(low, high, before, after, landed_before, landed_after, send_sem, recv_sem, *, axis, count):
    me = lax.axis_index(axis)
    has_lower = me > 0
    has_upper = me < count - 1
    mesh_ids = pl.DeviceIdType.MESH
    barrier = pltpu.get_barrier_semaphore()

    @pl.when(has_lower)
    def _():
        pl.semaphore_signal(barrier, 1, device_id={axis: me - 1}, device_id_type=mesh_ids)

    @pl.when(has_upper)
    def _():
        pl.semaphore_signal(barrier, 1, device_id={axis: me + 1}, device_id_type=mesh_ids)

    pl.semaphore_wait(barrier, has_lower.astype(jnp.int32) + has_upper.astype(jnp.int32))

    to_upper = pltpu.make_async_remote_copy(
        src_ref=high,
        dst_ref=landed_before,
        send_sem=send_sem.at[0],
        recv_sem=recv_sem.at[0],
        device_id={axis: me + 1},
        device_id_type=mesh_ids,
    )
    to_lower = pltpu.make_async_remote_copy(
        src_ref=low,
        dst_ref=landed_after,
        send_sem=send_sem.at[1],
        recv_sem=recv_sem.at[1],
        device_id={axis: me - 1},
        device_id_type=mesh_ids,
    )

    @pl.when(has_upper)
    def _():
        to_upper.start()

    @pl.when(has_lower)
    def _():
        to_lower.start()

    @pl.when(has_upper)
    def _():
        to_upper.wait_send()
        to_lower.wait_recv()
        after[...] = landed_after[...]

    @pl.when(has_lower)
    def _():
        to_lower.wait_send()
        to_upper.wait_recv()
        before[...] = landed_before[...]

    @pl.when(jnp.logical_not(has_upper))
    def _():
        after[...] = jnp.zeros(after.shape, after.dtype)

    @pl.when(jnp.logical_not(has_lower))
    def _():
        before[...] = jnp.zeros(before.shape, before.dtype)


HALO_IDS = {}


def exchange(low, high, axis):
    key = (axis, low.shape)
    if key not in HALO_IDS:
        HALO_IDS[key] = len(HALO_IDS)
    kernel = functools.partial(halo_kernel, axis=axis, count=lax.axis_size(axis))
    vmem = pl.BlockSpec(memory_space=pltpu.VMEM)
    slab = jax.ShapeDtypeStruct(low.shape, low.dtype)
    return pl.pallas_call(
        kernel,
        out_shape=(slab, slab),
        in_specs=[vmem, vmem],
        out_specs=(vmem, vmem),
        scratch_shapes=[
            pltpu.VMEM(low.shape, low.dtype),
            pltpu.VMEM(low.shape, low.dtype),
            pltpu.SemaphoreType.DMA((2,)),
            pltpu.SemaphoreType.DMA((2,)),
        ],
        compiler_params=pltpu.CompilerParams(collective_id=HALO_IDS[key], has_side_effects=True),
    )(low, high)


def gather_kernel(shard, out, landed, send_sem, recv_sem, *, axis, count):
    me = lax.axis_index(axis)
    mesh_ids = pl.DeviceIdType.MESH
    barrier = pltpu.get_barrier_semaphore()
    for peer in range(count):

        @pl.when(peer != me)
        def _():
            pl.semaphore_signal(barrier, 1, device_id={axis: peer}, device_id_type=mesh_ids)

    pl.semaphore_wait(barrier, count - 1)
    copies = []
    for peer in range(count):
        copies.append(
            pltpu.make_async_remote_copy(
                src_ref=shard,
                dst_ref=landed.at[me],
                send_sem=send_sem.at[peer],
                recv_sem=recv_sem.at[me],
                device_id={axis: peer},
                device_id_type=mesh_ids,
            )
        )

        @pl.when(peer != me)
        def _():
            copies[peer].start()

    for peer in range(count):
        incoming = pltpu.make_async_remote_copy(
            src_ref=shard,
            dst_ref=landed.at[peer],
            send_sem=send_sem.at[peer],
            recv_sem=recv_sem.at[peer],
            device_id={axis: peer},
            device_id_type=mesh_ids,
        )

        @pl.when(peer != me)
        def _():
            copies[peer].wait_send()
            incoming.wait_recv()
            out[peer] = landed[peer]

    out[me] = shard[...]


def gather_peers(shard, axis):
    count = lax.axis_size(axis)
    kernel = functools.partial(gather_kernel, axis=axis, count=count)
    vmem = pl.BlockSpec(memory_space=pltpu.VMEM)
    stacked = (count,) + shard.shape
    return pl.pallas_call(
        kernel,
        out_shape=jax.ShapeDtypeStruct(stacked, shard.dtype),
        in_specs=[vmem],
        out_specs=vmem,
        scratch_shapes=[
            pltpu.VMEM(stacked, shard.dtype),
            pltpu.SemaphoreType.DMA((count,)),
            pltpu.SemaphoreType.DMA((count,)),
        ],
        compiler_params=pltpu.CompilerParams(collective_id=100, has_side_effects=True),
    )(shard)


def plane_kernel(*refs, axes, sizes, offsets):
    count = len(offsets)
    sends = refs[:count]
    outs = refs[count : 2 * count]
    landed = refs[2 * count : 3 * count]
    send_sem, recv_sem = refs[3 * count :]
    me = [lax.axis_index(axis) for axis in axes]
    mesh_ids = pl.DeviceIdType.MESH

    def exists(offset):
        inside = None
        for position, step, size in zip(me, offset, sizes):
            if step == 0:
                continue
            here = (position + step >= 0) & (position + step < size)
            inside = here if inside is None else inside & here
        return inside

    def target(offset):
        return {axis: position + step for axis, position, step in zip(axes, me, offset)}

    barrier = pltpu.get_barrier_semaphore()
    expected = 0
    for offset in offsets:

        @pl.when(exists(offset))
        def _():
            pl.semaphore_signal(barrier, 1, device_id=target(offset), device_id_type=mesh_ids)

        expected = expected + exists(offset).astype(jnp.int32)
    pl.semaphore_wait(barrier, expected)
    slot = {offset: k for k, offset in enumerate(offsets)}
    outgoing = []
    for k, offset in enumerate(offsets):
        back = slot[tuple(-step for step in offset)]
        outgoing.append(
            pltpu.make_async_remote_copy(
                src_ref=sends[k],
                dst_ref=landed[back],
                send_sem=send_sem.at[k],
                recv_sem=recv_sem.at[back],
                device_id=target(offset),
                device_id_type=mesh_ids,
            )
        )

        @pl.when(exists(offset))
        def _():
            outgoing[k].start()

    for k, offset in enumerate(offsets):
        back = slot[tuple(-step for step in offset)]
        incoming = pltpu.make_async_remote_copy(
            src_ref=sends[back],
            dst_ref=landed[k],
            send_sem=send_sem.at[back],
            recv_sem=recv_sem.at[k],
            device_id=target(offset),
            device_id_type=mesh_ids,
        )

        @pl.when(exists(offset))
        def _():
            outgoing[k].wait_send()
            incoming.wait_recv()
            outs[k][...] = landed[k][...]

        @pl.when(jnp.logical_not(exists(offset)))
        def _():
            outs[k][...] = jnp.zeros(outs[k].shape, outs[k].dtype)


def as_rows(piece, thin):
    sublanes = 1 if piece.shape[-2] == 1 else -(-piece.shape[-2] // 8) * 8
    tiled = math.prod(piece.shape[:-2]) * sublanes * -(-piece.shape[-1] // 128) * 128
    if tiled <= 3 * piece.size or tiled <= 65536:
        return piece, None
    moved = jnp.moveaxis(piece, thin, tuple(range(len(thin))))
    return moved.reshape(-1, moved.shape[-1]), moved.shape


def from_rows(piece, moved, thin):
    if moved is None:
        return piece
    return jnp.moveaxis(piece.reshape(moved), tuple(range(len(thin))), thin)


def with_plane_halo(shard, axes, dims, width):
    offsets = [(ox, oy) for ox in (-1, 0, 1) for oy in (-1, 0, 1) if (ox, oy) != (0, 0)]
    pieces = []
    layouts = []
    for offset in offsets:
        piece = shard
        thin = []
        for step, dim in zip(offset, dims):
            length = piece.shape[dim]
            if step == 1:
                piece = lax.slice_in_dim(piece, length - width, length, axis=dim)
            elif step == -1:
                piece = lax.slice_in_dim(piece, 0, width, axis=dim)
            if step != 0:
                thin.append(dim)
        piece, moved = as_rows(piece, thin)
        pieces.append(piece)
        layouts.append((moved, thin))
    key = ("plane",) + tuple(piece.shape for piece in pieces)
    if key not in HALO_IDS:
        HALO_IDS[key] = len(HALO_IDS)
    sizes = tuple(lax.axis_size(axis) for axis in axes)
    kernel = functools.partial(plane_kernel, axes=axes, sizes=sizes, offsets=tuple(offsets))
    vmem = pl.BlockSpec(memory_space=pltpu.VMEM)
    shapes = tuple(jax.ShapeDtypeStruct(piece.shape, piece.dtype) for piece in pieces)
    received = pl.pallas_call(
        kernel,
        out_shape=shapes,
        in_specs=[vmem] * len(pieces),
        out_specs=tuple([vmem] * len(pieces)),
        scratch_shapes=[pltpu.VMEM(piece.shape, piece.dtype) for piece in pieces]
        + [pltpu.SemaphoreType.DMA((len(pieces),)), pltpu.SemaphoreType.DMA((len(pieces),))],
        compiler_params=pltpu.CompilerParams(collective_id=HALO_IDS[key], has_side_effects=True),
    )(*pieces)
    got = {offset: from_rows(piece, *layout) for offset, piece, layout in zip(offsets, received, layouts)}
    got[(0, 0)] = shard
    rows = []
    for ox in (-1, 0, 1):
        rows.append(jnp.concatenate([got[(ox, oy)] for oy in (-1, 0, 1)], axis=dims[1]))
    return jnp.concatenate(rows, axis=dims[0])


def with_halo(shard, sides, width):
    for axis, dim in sides:
        length = shard.shape[dim]
        last = lax.slice_in_dim(shard, length - width, length, axis=dim)
        initial = lax.slice_in_dim(shard, 0, width, axis=dim)
        tiled = math.prod(initial.shape[:-2]) * -(-initial.shape[-2] // 8) * 8 * -(-initial.shape[-1] // 128) * 128
        if tiled <= 3 * initial.size:
            before, after = exchange(initial, last, axis)
        else:
            moved = jnp.moveaxis(initial, dim, 0).shape
            rows = (-1, moved[-1])
            before, after = exchange(
                jnp.moveaxis(initial, dim, 0).reshape(rows), jnp.moveaxis(last, dim, 0).reshape(rows), axis
            )
            before = jnp.moveaxis(before.reshape(moved), 0, dim)
            after = jnp.moveaxis(after.reshape(moved), 0, dim)
        shard = jnp.concatenate([before, shard, after], axis=dim)
    return shard


def recover(local_nodes, corner_vals, ratio_z):
    ex = local_nodes.shape[1] - 1
    ey = local_nodes.shape[2] - 1
    ratio_x = jnp.arange(ex + 1, dtype=jnp.float32) / ex
    ratio_y = jnp.arange(ey + 1, dtype=jnp.float32) / ey
    planes = []
    for high_z in (0, 1):
        plane = None
        for corner in range(high_z, 8, 2):
            along_x = ratio_x if corner // 4 == 1 else 1.0 - ratio_x
            along_y = ratio_y if corner // 2 % 2 == 1 else 1.0 - ratio_y
            basis = along_x[:, None] * along_y[None, :]
            term = basis[None] * corner_vals[:, corner][:, None, None]
            plane = term if plane is None else plane + term
        planes.append(plane[:, :, :, None])
    return local_nodes + planes[0] * (1.0 - ratio_z) + planes[1] * ratio_z


def average_rows(extended, dim, has_lower, has_upper):
    inner = extended.shape[dim] - 2
    own_rows = lax.slice_in_dim(extended, 1, inner + 1, axis=dim)
    rim_low = lax.slice_in_dim(extended, 0, 1, axis=dim)
    rim_high = lax.slice_in_dim(extended, inner + 1, inner + 2, axis=dim)
    shape_row = [1] * extended.ndim
    shape_row[dim] = inner
    rows = jnp.arange(inner, dtype=jnp.int32).reshape(shape_row)
    is_low = rows == 0
    is_high = rows == inner - 1
    factor = jnp.where(is_low & has_lower, 0.5, jnp.where(is_high & has_upper, 0.5, 1.0))
    rim_part = jnp.where(is_low, rim_low, 0.0) + jnp.where(is_high, rim_high, 0.0)
    return own_rows * factor + rim_part * 0.5


def energy_kernel(stiffness, base, up_y, up_z, up_yz, out, weights, *, count_x, chunks):
    sources = (base, up_z, up_y, up_yz)
    for a in range(24):
        weights[a * 24 + a] = stiffness[a, a]
        for b in range(a + 1, 24):
            weights[a * 24 + b] = stiffness[a, b] + stiffness[b, a]

    def row(i, carry):
        for first in chunks:
            vectors = []
            for component in range(3):
                for corner in range(8):
                    shift_x = corner // 4
                    source = sources[corner % 4]
                    vectors.append(source[component, i + shift_x, pl.ds(first, 8), :])
            total = None
            for a in range(24):
                inner = weights[a * 24 + a] * vectors[a]
                for b in range(a + 1, 24):
                    inner = inner + weights[a * 24 + b] * vectors[b]
                term = vectors[a] * inner
                total = term if total is None else total + term
            if first % 8 == 0:
                out[i, pl.ds(first, 8), :] = total
            else:
                keep = 8 - first % 8
                out[i, pl.ds(first + 8 - keep, keep), :] = total[8 - keep :]
        return carry

    lax.fori_loop(0, count_x, row, 0)


def element_energy(nodes, stiffness):
    count_x = nodes.shape[1] - 1
    count_y = nodes.shape[2] - 1
    count_z = nodes.shape[3] - 1
    shifted = [nodes[:, :, dy : dy + count_y, dz : dz + count_z] for dy, dz in ((0, 0), (1, 0), (0, 1), (1, 1))]
    chunks = tuple(range(0, count_y - 7, 8))
    if count_y % 8:
        chunks = chunks + (count_y - 8,)
    kernel = functools.partial(energy_kernel, count_x=count_x, chunks=chunks)
    vmem = pl.BlockSpec(memory_space=pltpu.VMEM)
    energy = pl.pallas_call(
        kernel,
        out_shape=jax.ShapeDtypeStruct((count_x, count_y, count_z), jnp.float32),
        in_specs=[pl.BlockSpec(memory_space=pltpu.SMEM)] + [vmem] * 4,
        out_specs=vmem,
        scratch_shapes=[pltpu.SMEM((24 * 24,), jnp.float32)],
    )(stiffness, *shifted)
    return energy


def smooth(field, axis, count):
    summed = None
    for offset in range(-RADIUS, RADIUS + 1):
        term_piece = lax.slice_in_dim(field, RADIUS + offset, RADIUS + offset + count, axis=axis)
        term_value = float(RADIUS + 1 - abs(offset)) * term_piece
        summed = term_value if summed is None else summed + term_value
    return summed


def edge_counts(count, position, parts):
    places = position * count + jnp.arange(count, dtype=jnp.int32)
    summed = None
    for offset in range(-RADIUS, RADIUS + 1):
        inside = ((places + offset >= 0) & (places + offset < count * parts)).astype(jnp.float32)
        term_value = float(RADIUS + 1 - abs(offset)) * inside
        summed = term_value if summed is None else summed + term_value
    return summed


def filter_field(field, sides):
    (axis_x, dim_x), (axis_y, dim_y), (axis_z, dim_z) = sides
    count_x, count_y = field.shape[dim_x], field.shape[dim_y]
    padded = with_plane_halo(field, (axis_x, axis_y), (dim_x, dim_y), RADIUS)
    field = smooth(smooth(padded, dim_x, count_x), dim_y, count_y)
    padded = with_halo(field, ((axis_z, dim_z),), RADIUS)
    return smooth(padded, dim_z, field.shape[dim_z])


def local(local_solution, top_nodes, coarse_solution, corner_dofs, density, element_stiffness):
    count_x, count_y, count_z = density.shape
    index_x = lax.axis_index("gx")
    index_y = lax.axis_index("gy")
    index_z = lax.axis_index("gz")
    normalizer = (
        edge_counts(count_x, index_x, lax.axis_size("gx"))[:, None, None]
        * edge_counts(count_y, index_y, lax.axis_size("gy"))[None, :, None]
        * edge_counts(count_z, index_z, lax.axis_size("gz"))[None, None, :]
    )
    sides = (("gx", 1), ("gy", 2), ("gz", 3))
    wanted = corner_dofs.reshape(8)
    gathered = gather_peers(coarse_solution, "gz")
    width = coarse_solution.shape[1]
    corner_vals = gathered[wanted // width, :, wanted % width].T
    depth = local_solution.shape[3]
    full = jnp.concatenate([local_solution, top_nodes], axis=3)
    nodes = recover(full, corner_vals, jnp.arange(depth + 1, dtype=jnp.float32) / depth)
    lower_x = index_x > 0
    upper_x = index_x < lax.axis_size("gx") - 1
    lower_y = index_y > 0
    upper_y = index_y < lax.axis_size("gy") - 1
    lower_z = index_z > 0
    upper_z = index_z < lax.axis_size("gz") - 1
    extended = with_plane_halo(nodes, ("gx", "gy"), (1, 2), 1)
    extended = average_rows(extended, 1, lower_x, upper_x)
    averaged = average_rows(extended, 2, lower_y, upper_y)
    extended = with_halo(averaged, (("gz", 3),), 1)
    averaged = average_rows(extended, 3, lower_z, upper_z)
    energy = element_energy(averaged, element_stiffness)
    sens = penal_scale * density * density * energy
    smoothed = filter_field(jnp.stack([density * sens, density]), sides)
    numerator = smoothed[0]
    smooth_density = smoothed[1]
    return (numerator / (density * normalizer), smooth_density / normalizer)


def solution(mesh):
    in_specs = (
        P(None, "gx", "gy", "gz"),
        P(None, "gx", "gy", "gz"),
        P(None, "gz"),
        P("gx", "gy", "gz", None),
        P("gx", "gy", "gz"),
        P(),
    )
    out_specs = (P("gx", "gy", "gz"), P("gx", "gy", "gz"))
    return jax.shard_map(local, mesh=mesh, in_specs=in_specs, out_specs=out_specs, check_vma=False)
```

```python
import functools
import itertools
import math

import jax
import jax.numpy as jnp
from jax import lax
from jax.sharding import PartitionSpec as P
from jax.experimental import pallas as pl
from jax.experimental.pallas import tpu as pltpu

RADIUS = 3


penal_scale = -3.0 / 96.0


def halo_kernel(low, high, before, after, landed_before, landed_after, send_sem, recv_sem, *, axis, count):
    me = lax.axis_index(axis)
    has_lower = me > 0
    has_upper = me < count - 1
    mesh_ids = pl.DeviceIdType.MESH
    barrier = pltpu.get_barrier_semaphore()

    @pl.when(has_lower)
    def _():
        pl.semaphore_signal(barrier, 1, device_id={axis: me - 1}, device_id_type=mesh_ids)

    @pl.when(has_upper)
    def _():
        pl.semaphore_signal(barrier, 1, device_id={axis: me + 1}, device_id_type=mesh_ids)

    pl.semaphore_wait(barrier, has_lower.astype(jnp.int32) + has_upper.astype(jnp.int32))

    to_upper = pltpu.make_async_remote_copy(
        src_ref=high,
        dst_ref=landed_before,
        send_sem=send_sem.at[0],
        recv_sem=recv_sem.at[0],
        device_id={axis: me + 1},
        device_id_type=mesh_ids,
    )
    to_lower = pltpu.make_async_remote_copy(
        src_ref=low,
        dst_ref=landed_after,
        send_sem=send_sem.at[1],
        recv_sem=recv_sem.at[1],
        device_id={axis: me - 1},
        device_id_type=mesh_ids,
    )

    @pl.when(has_upper)
    def _():
        to_upper.start()

    @pl.when(has_lower)
    def _():
        to_lower.start()

    @pl.when(has_upper)
    def _():
        to_upper.wait_send()
        to_lower.wait_recv()
        after[...] = landed_after[...]

    @pl.when(has_lower)
    def _():
        to_lower.wait_send()
        to_upper.wait_recv()
        before[...] = landed_before[...]

    @pl.when(jnp.logical_not(has_upper))
    def _():
        after[...] = jnp.zeros(after.shape, after.dtype)

    @pl.when(jnp.logical_not(has_lower))
    def _():
        before[...] = jnp.zeros(before.shape, before.dtype)


HALO_IDS = {}


def exchange(low, high, axis):
    key = (axis, low.shape)
    if key not in HALO_IDS:
        HALO_IDS[key] = len(HALO_IDS)
    kernel = functools.partial(halo_kernel, axis=axis, count=lax.axis_size(axis))
    vmem = pl.BlockSpec(memory_space=pltpu.VMEM)
    slab = jax.ShapeDtypeStruct(low.shape, low.dtype)
    return pl.pallas_call(
        kernel,
        out_shape=(slab, slab),
        in_specs=[vmem, vmem],
        out_specs=(vmem, vmem),
        scratch_shapes=[
            pltpu.VMEM(low.shape, low.dtype),
            pltpu.VMEM(low.shape, low.dtype),
            pltpu.SemaphoreType.DMA((2,)),
            pltpu.SemaphoreType.DMA((2,)),
        ],
        compiler_params=pltpu.CompilerParams(collective_id=HALO_IDS[key], has_side_effects=True),
    )(low, high)


def gather_kernel(shard, out, landed, send_sem, recv_sem, *, axis, count):
    me = lax.axis_index(axis)
    mesh_ids = pl.DeviceIdType.MESH
    barrier = pltpu.get_barrier_semaphore()
    for peer in range(count):

        @pl.when(peer != me)
        def _():
            pl.semaphore_signal(barrier, 1, device_id={axis: peer}, device_id_type=mesh_ids)

    pl.semaphore_wait(barrier, count - 1)
    copies = []
    for peer in range(count):
        copies.append(
            pltpu.make_async_remote_copy(
                src_ref=shard,
                dst_ref=landed.at[me],
                send_sem=send_sem.at[peer],
                recv_sem=recv_sem.at[me],
                device_id={axis: peer},
                device_id_type=mesh_ids,
            )
        )

        @pl.when(peer != me)
        def _():
            copies[peer].start()

    for peer in range(count):
        incoming = pltpu.make_async_remote_copy(
            src_ref=shard,
            dst_ref=landed.at[peer],
            send_sem=send_sem.at[peer],
            recv_sem=recv_sem.at[peer],
            device_id={axis: peer},
            device_id_type=mesh_ids,
        )

        @pl.when(peer != me)
        def _():
            copies[peer].wait_send()
            incoming.wait_recv()
            out[peer] = landed[peer]

    out[me] = shard[...]


def gather_peers(shard, axis):
    count = lax.axis_size(axis)
    kernel = functools.partial(gather_kernel, axis=axis, count=count)
    vmem = pl.BlockSpec(memory_space=pltpu.VMEM)
    stacked = (count,) + shard.shape
    return pl.pallas_call(
        kernel,
        out_shape=jax.ShapeDtypeStruct(stacked, shard.dtype),
        in_specs=[vmem],
        out_specs=vmem,
        scratch_shapes=[
            pltpu.VMEM(stacked, shard.dtype),
            pltpu.SemaphoreType.DMA((count,)),
            pltpu.SemaphoreType.DMA((count,)),
        ],
        compiler_params=pltpu.CompilerParams(collective_id=100, has_side_effects=True),
    )(shard)


def plane_kernel(*refs, axes, sizes, offsets):
    count = len(offsets)
    sends = refs[:count]
    outs = refs[count : 2 * count]
    landed = refs[2 * count : 3 * count]
    send_sem, recv_sem = refs[3 * count :]
    me = [lax.axis_index(axis) for axis in axes]
    mesh_ids = pl.DeviceIdType.MESH

    def exists(offset):
        inside = None
        for position, step, size in zip(me, offset, sizes):
            if step == 0:
                continue
            here = (position + step >= 0) & (position + step < size)
            inside = here if inside is None else inside & here
        return inside

    def target(offset):
        return {axis: position + step for axis, position, step in zip(axes, me, offset)}

    barrier = pltpu.get_barrier_semaphore()
    expected = 0
    for offset in offsets:

        @pl.when(exists(offset))
        def _():
            pl.semaphore_signal(barrier, 1, device_id=target(offset), device_id_type=mesh_ids)

        expected = expected + exists(offset).astype(jnp.int32)
    pl.semaphore_wait(barrier, expected)
    slot = {offset: k for k, offset in enumerate(offsets)}
    outgoing = []
    for k, offset in enumerate(offsets):
        back = slot[tuple(-step for step in offset)]
        outgoing.append(
            pltpu.make_async_remote_copy(
                src_ref=sends[k],
                dst_ref=landed[back],
                send_sem=send_sem.at[k],
                recv_sem=recv_sem.at[back],
                device_id=target(offset),
                device_id_type=mesh_ids,
            )
        )

        @pl.when(exists(offset))
        def _():
            outgoing[k].start()

    for k, offset in enumerate(offsets):
        back = slot[tuple(-step for step in offset)]
        incoming = pltpu.make_async_remote_copy(
            src_ref=sends[back],
            dst_ref=landed[k],
            send_sem=send_sem.at[back],
            recv_sem=recv_sem.at[k],
            device_id=target(offset),
            device_id_type=mesh_ids,
        )

        @pl.when(exists(offset))
        def _():
            outgoing[k].wait_send()
            incoming.wait_recv()
            outs[k][...] = landed[k][...]

        @pl.when(jnp.logical_not(exists(offset)))
        def _():
            outs[k][...] = jnp.zeros(outs[k].shape, outs[k].dtype)


def as_rows(piece, thin):
    sublanes = 1 if piece.shape[-2] == 1 else -(-piece.shape[-2] // 8) * 8
    tiled = math.prod(piece.shape[:-2]) * sublanes * -(-piece.shape[-1] // 128) * 128
    if tiled <= 3 * piece.size or tiled <= 65536:
        return piece, None
    moved = jnp.moveaxis(piece, thin, tuple(range(len(thin))))
    return moved.reshape(-1, moved.shape[-1]), moved.shape


def from_rows(piece, moved, thin):
    if moved is None:
        return piece
    return jnp.moveaxis(piece.reshape(moved), tuple(range(len(thin))), thin)


def with_box_halo(shard, axes, dims, width):
    steps = (-1, 0, 1)
    offsets = [offset for offset in itertools.product(steps, repeat=len(axes)) if any(offset)]
    pieces = []
    layouts = []
    for offset in offsets:
        piece = shard
        thin = []
        for step, dim in zip(offset, dims):
            length = piece.shape[dim]
            if step == 1:
                piece = lax.slice_in_dim(piece, length - width, length, axis=dim)
            elif step == -1:
                piece = lax.slice_in_dim(piece, 0, width, axis=dim)
            if step != 0:
                thin.append(dim)
        piece, moved = as_rows(piece, thin)
        pieces.append(piece)
        layouts.append((moved, thin))
    key = ("box",) + tuple(piece.shape for piece in pieces)
    if key not in HALO_IDS:
        HALO_IDS[key] = len(HALO_IDS)
    sizes = tuple(lax.axis_size(axis) for axis in axes)
    kernel = functools.partial(plane_kernel, axes=axes, sizes=sizes, offsets=tuple(offsets))
    vmem = pl.BlockSpec(memory_space=pltpu.VMEM)
    shapes = tuple(jax.ShapeDtypeStruct(piece.shape, piece.dtype) for piece in pieces)
    received = pl.pallas_call(
        kernel,
        out_shape=shapes,
        in_specs=[vmem] * len(pieces),
        out_specs=tuple([vmem] * len(pieces)),
        scratch_shapes=[pltpu.VMEM(piece.shape, piece.dtype) for piece in pieces]
        + [pltpu.SemaphoreType.DMA((len(pieces),)), pltpu.SemaphoreType.DMA((len(pieces),))],
        compiler_params=pltpu.CompilerParams(collective_id=HALO_IDS[key], has_side_effects=True),
    )(*pieces)
    got = {offset: from_rows(piece, *layout) for offset, piece, layout in zip(offsets, received, layouts)}
    got[(0,) * len(axes)] = shard

    def assemble(prefix):
        level = len(prefix)
        if level == len(axes):
            return got[prefix]
        return jnp.concatenate([assemble(prefix + (step,)) for step in steps], axis=dims[level])

    return assemble(())


def with_halo(shard, sides, width):
    for axis, dim in sides:
        length = shard.shape[dim]
        last = lax.slice_in_dim(shard, length - width, length, axis=dim)
        initial = lax.slice_in_dim(shard, 0, width, axis=dim)
        tiled = math.prod(initial.shape[:-2]) * -(-initial.shape[-2] // 8) * 8 * -(-initial.shape[-1] // 128) * 128
        if tiled <= 3 * initial.size:
            before, after = exchange(initial, last, axis)
        else:
            moved = jnp.moveaxis(initial, dim, 0).shape
            rows = (-1, moved[-1])
            before, after = exchange(
                jnp.moveaxis(initial, dim, 0).reshape(rows), jnp.moveaxis(last, dim, 0).reshape(rows), axis
            )
            before = jnp.moveaxis(before.reshape(moved), 0, dim)
            after = jnp.moveaxis(after.reshape(moved), 0, dim)
        shard = jnp.concatenate([before, shard, after], axis=dim)
    return shard


def recover(local_nodes, corner_vals, ratio_z):
    ex = local_nodes.shape[1] - 1
    ey = local_nodes.shape[2] - 1
    ratio_x = jnp.arange(ex + 1, dtype=jnp.float32) / ex
    ratio_y = jnp.arange(ey + 1, dtype=jnp.float32) / ey
    planes = []
    for high_z in (0, 1):
        plane = None
        for corner in range(high_z, 8, 2):
            along_x = ratio_x if corner // 4 == 1 else 1.0 - ratio_x
            along_y = ratio_y if corner // 2 % 2 == 1 else 1.0 - ratio_y
            basis = along_x[:, None] * along_y[None, :]
            term = basis[None] * corner_vals[:, corner][:, None, None]
            plane = term if plane is None else plane + term
        planes.append(plane[:, :, :, None])
    return local_nodes + planes[0] * (1.0 - ratio_z) + planes[1] * ratio_z


def average_rows(extended, dim, has_lower, has_upper):
    inner = extended.shape[dim] - 2
    own_rows = lax.slice_in_dim(extended, 1, inner + 1, axis=dim)
    rim_low = lax.slice_in_dim(extended, 0, 1, axis=dim)
    rim_high = lax.slice_in_dim(extended, inner + 1, inner + 2, axis=dim)
    shape_row = [1] * extended.ndim
    shape_row[dim] = inner
    rows = jnp.arange(inner, dtype=jnp.int32).reshape(shape_row)
    is_low = rows == 0
    is_high = rows == inner - 1
    factor = jnp.where(is_low & has_lower, 0.5, jnp.where(is_high & has_upper, 0.5, 1.0))
    rim_part = jnp.where(is_low, rim_low, 0.0) + jnp.where(is_high, rim_high, 0.0)
    return own_rows * factor + rim_part * 0.5


def energy_kernel(stiffness, base, up_y, up_z, up_yz, out, weights, *, count_x, chunks):
    sources = (base, up_z, up_y, up_yz)
    for a in range(24):
        weights[a * 24 + a] = stiffness[a, a]
        for b in range(a + 1, 24):
            weights[a * 24 + b] = stiffness[a, b] + stiffness[b, a]

    def row(i, carry):
        for first in chunks:
            vectors = []
            for component in range(3):
                for corner in range(8):
                    shift_x = corner // 4
                    source = sources[corner % 4]
                    vectors.append(source[component, i + shift_x, pl.ds(first, 8), :])
            total = None
            for a in range(24):
                inner = weights[a * 24 + a] * vectors[a]
                for b in range(a + 1, 24):
                    inner = inner + weights[a * 24 + b] * vectors[b]
                term = vectors[a] * inner
                total = term if total is None else total + term
            if first % 8 == 0:
                out[i, pl.ds(first, 8), :] = total
            else:
                keep = 8 - first % 8
                out[i, pl.ds(first + 8 - keep, keep), :] = total[8 - keep :]
        return carry

    lax.fori_loop(0, count_x, row, 0)


def element_energy(nodes, stiffness):
    count_x = nodes.shape[1] - 1
    count_y = nodes.shape[2] - 1
    count_z = nodes.shape[3] - 1
    shifted = [nodes[:, :, dy : dy + count_y, dz : dz + count_z] for dy, dz in ((0, 0), (1, 0), (0, 1), (1, 1))]
    chunks = tuple(range(0, count_y - 7, 8))
    if count_y % 8:
        chunks = chunks + (count_y - 8,)
    kernel = functools.partial(energy_kernel, count_x=count_x, chunks=chunks)
    vmem = pl.BlockSpec(memory_space=pltpu.VMEM)
    energy = pl.pallas_call(
        kernel,
        out_shape=jax.ShapeDtypeStruct((count_x, count_y, count_z), jnp.float32),
        in_specs=[pl.BlockSpec(memory_space=pltpu.SMEM)] + [vmem] * 4,
        out_specs=vmem,
        scratch_shapes=[pltpu.SMEM((24 * 24,), jnp.float32)],
    )(stiffness, *shifted)
    return energy


def smooth(field, axis, count):
    summed = None
    for offset in range(-RADIUS, RADIUS + 1):
        term_piece = lax.slice_in_dim(field, RADIUS + offset, RADIUS + offset + count, axis=axis)
        term_value = float(RADIUS + 1 - abs(offset)) * term_piece
        summed = term_value if summed is None else summed + term_value
    return summed


def edge_counts(count, position, parts):
    places = position * count + jnp.arange(count, dtype=jnp.int32)
    summed = None
    for offset in range(-RADIUS, RADIUS + 1):
        inside = ((places + offset >= 0) & (places + offset < count * parts)).astype(jnp.float32)
        term_value = float(RADIUS + 1 - abs(offset)) * inside
        summed = term_value if summed is None else summed + term_value
    return summed


def filter_field(field, sides):
    axes = tuple(axis for axis, _ in sides)
    dims = tuple(dim for _, dim in sides)
    counts = [field.shape[dim] for dim in dims]
    padded = with_box_halo(field, axes, dims, RADIUS)
    for dim, count in zip(dims, counts):
        padded = smooth(padded, dim, count)
    return padded


def local(local_solution, top_nodes, coarse_solution, corner_dofs, density, element_stiffness):
    count_x, count_y, count_z = density.shape
    index_x = lax.axis_index("gx")
    index_y = lax.axis_index("gy")
    index_z = lax.axis_index("gz")
    normalizer = (
        edge_counts(count_x, index_x, lax.axis_size("gx"))[:, None, None]
        * edge_counts(count_y, index_y, lax.axis_size("gy"))[None, :, None]
        * edge_counts(count_z, index_z, lax.axis_size("gz"))[None, None, :]
    )
    sides = (("gx", 1), ("gy", 2), ("gz", 3))
    wanted = corner_dofs.reshape(8)
    gathered = gather_peers(coarse_solution, "gz")
    columns = gathered.transpose(1, 0, 2).reshape(coarse_solution.shape[0], -1)
    matches = wanted[:, None] == jnp.arange(columns.shape[1], dtype=jnp.int32)[None, :]
    corner_vals = jnp.sum(jnp.where(matches[None], columns[:, None, :], 0.0), axis=2)
    depth = local_solution.shape[3]
    full = jnp.concatenate([local_solution, top_nodes], axis=3)
    nodes = recover(full, corner_vals, jnp.arange(depth + 1, dtype=jnp.float32) / depth)
    lower_x = index_x > 0
    upper_x = index_x < lax.axis_size("gx") - 1
    lower_y = index_y > 0
    upper_y = index_y < lax.axis_size("gy") - 1
    lower_z = index_z > 0
    upper_z = index_z < lax.axis_size("gz") - 1
    extended = with_box_halo(nodes, ("gx", "gy", "gz"), (1, 2, 3), 1)
    extended = average_rows(extended, 1, lower_x, upper_x)
    extended = average_rows(extended, 2, lower_y, upper_y)
    averaged = average_rows(extended, 3, lower_z, upper_z)
    energy = element_energy(averaged, element_stiffness)
    sens = penal_scale * density * density * energy
    smoothed = filter_field(jnp.stack([density * sens, density]), sides)
    numerator = smoothed[0]
    smooth_density = smoothed[1]
    return (numerator / (density * normalizer), smooth_density / normalizer)


def solution(mesh):
    in_specs = (
        P(None, "gx", "gy", "gz"),
        P(None, "gx", "gy", "gz"),
        P(None, "gz"),
        P("gx", "gy", "gz", None),
        P("gx", "gy", "gz"),
        P(),
    )
    out_specs = (P("gx", "gy", "gz"), P("gx", "gy", "gz"))
    return jax.shard_map(local, mesh=mesh, in_specs=in_specs, out_specs=out_specs, check_vma=False)
```

```python
import functools
import math

import jax
import jax.numpy as jnp
from jax import lax
from jax.sharding import PartitionSpec as P
from jax.experimental import pallas as pl
from jax.experimental.pallas import tpu as pltpu

RADIUS = 3


penal_scale = -3.0 / 96.0


def halo_kernel(low, high, before, after, landed_before, landed_after, send_sem, recv_sem, *, axis, count):
    me = lax.axis_index(axis)
    has_lower = me > 0
    has_upper = me < count - 1
    mesh_ids = pl.DeviceIdType.MESH
    barrier = pltpu.get_barrier_semaphore()

    @pl.when(has_lower)
    def _():
        pl.semaphore_signal(barrier, 1, device_id={axis: me - 1}, device_id_type=mesh_ids)

    @pl.when(has_upper)
    def _():
        pl.semaphore_signal(barrier, 1, device_id={axis: me + 1}, device_id_type=mesh_ids)

    pl.semaphore_wait(barrier, has_lower.astype(jnp.int32) + has_upper.astype(jnp.int32))

    to_upper = pltpu.make_async_remote_copy(
        src_ref=high,
        dst_ref=landed_before,
        send_sem=send_sem.at[0],
        recv_sem=recv_sem.at[0],
        device_id={axis: me + 1},
        device_id_type=mesh_ids,
    )
    to_lower = pltpu.make_async_remote_copy(
        src_ref=low,
        dst_ref=landed_after,
        send_sem=send_sem.at[1],
        recv_sem=recv_sem.at[1],
        device_id={axis: me - 1},
        device_id_type=mesh_ids,
    )

    @pl.when(has_upper)
    def _():
        to_upper.start()

    @pl.when(has_lower)
    def _():
        to_lower.start()

    @pl.when(has_upper)
    def _():
        to_upper.wait_send()
        to_lower.wait_recv()
        after[...] = landed_after[...]

    @pl.when(has_lower)
    def _():
        to_lower.wait_send()
        to_upper.wait_recv()
        before[...] = landed_before[...]

    @pl.when(jnp.logical_not(has_upper))
    def _():
        after[...] = jnp.zeros(after.shape, after.dtype)

    @pl.when(jnp.logical_not(has_lower))
    def _():
        before[...] = jnp.zeros(before.shape, before.dtype)


HALO_IDS = {}


def exchange(low, high, axis):
    key = (axis, low.shape)
    if key not in HALO_IDS:
        HALO_IDS[key] = len(HALO_IDS)
    kernel = functools.partial(halo_kernel, axis=axis, count=lax.axis_size(axis))
    vmem = pl.BlockSpec(memory_space=pltpu.VMEM)
    slab = jax.ShapeDtypeStruct(low.shape, low.dtype)
    return pl.pallas_call(
        kernel,
        out_shape=(slab, slab),
        in_specs=[vmem, vmem],
        out_specs=(vmem, vmem),
        scratch_shapes=[
            pltpu.VMEM(low.shape, low.dtype),
            pltpu.VMEM(low.shape, low.dtype),
            pltpu.SemaphoreType.DMA((2,)),
            pltpu.SemaphoreType.DMA((2,)),
        ],
        compiler_params=pltpu.CompilerParams(collective_id=HALO_IDS[key], has_side_effects=True),
    )(low, high)


def gather_kernel(shard, out, landed, send_sem, recv_sem, *, axis, count):
    me = lax.axis_index(axis)
    mesh_ids = pl.DeviceIdType.MESH
    barrier = pltpu.get_barrier_semaphore()
    for peer in range(count):

        @pl.when(peer != me)
        def _():
            pl.semaphore_signal(barrier, 1, device_id={axis: peer}, device_id_type=mesh_ids)

    pl.semaphore_wait(barrier, count - 1)
    copies = []
    for peer in range(count):
        copies.append(
            pltpu.make_async_remote_copy(
                src_ref=shard,
                dst_ref=landed.at[me],
                send_sem=send_sem.at[peer],
                recv_sem=recv_sem.at[me],
                device_id={axis: peer},
                device_id_type=mesh_ids,
            )
        )

        @pl.when(peer != me)
        def _():
            copies[peer].start()

    for peer in range(count):
        incoming = pltpu.make_async_remote_copy(
            src_ref=shard,
            dst_ref=landed.at[peer],
            send_sem=send_sem.at[peer],
            recv_sem=recv_sem.at[peer],
            device_id={axis: peer},
            device_id_type=mesh_ids,
        )

        @pl.when(peer != me)
        def _():
            copies[peer].wait_send()
            incoming.wait_recv()
            out[peer] = landed[peer]

    out[me] = shard[...]


def gather_peers(shard, axis):
    count = lax.axis_size(axis)
    kernel = functools.partial(gather_kernel, axis=axis, count=count)
    vmem = pl.BlockSpec(memory_space=pltpu.VMEM)
    stacked = (count,) + shard.shape
    return pl.pallas_call(
        kernel,
        out_shape=jax.ShapeDtypeStruct(stacked, shard.dtype),
        in_specs=[vmem],
        out_specs=vmem,
        scratch_shapes=[
            pltpu.VMEM(stacked, shard.dtype),
            pltpu.SemaphoreType.DMA((count,)),
            pltpu.SemaphoreType.DMA((count,)),
        ],
        compiler_params=pltpu.CompilerParams(collective_id=100, has_side_effects=True),
    )(shard)


def plane_kernel(*refs, axes, sizes, offsets):
    count = len(offsets)
    sends = refs[:count]
    outs = refs[count : 2 * count]
    landed = refs[2 * count : 3 * count]
    send_sem, recv_sem = refs[3 * count :]
    me = [lax.axis_index(axis) for axis in axes]
    mesh_ids = pl.DeviceIdType.MESH

    def exists(offset):
        inside = None
        for position, step, size in zip(me, offset, sizes):
            if step == 0:
                continue
            here = (position + step >= 0) & (position + step < size)
            inside = here if inside is None else inside & here
        return inside

    def target(offset):
        return {axis: position + step for axis, position, step in zip(axes, me, offset)}

    barrier = pltpu.get_barrier_semaphore()
    expected = 0
    for offset in offsets:

        @pl.when(exists(offset))
        def _():
            pl.semaphore_signal(barrier, 1, device_id=target(offset), device_id_type=mesh_ids)

        expected = expected + exists(offset).astype(jnp.int32)
    pl.semaphore_wait(barrier, expected)
    slot = {offset: k for k, offset in enumerate(offsets)}
    outgoing = []
    for k, offset in enumerate(offsets):
        back = slot[tuple(-step for step in offset)]
        outgoing.append(
            pltpu.make_async_remote_copy(
                src_ref=sends[k],
                dst_ref=landed[back],
                send_sem=send_sem.at[k],
                recv_sem=recv_sem.at[back],
                device_id=target(offset),
                device_id_type=mesh_ids,
            )
        )

        @pl.when(exists(offset))
        def _():
            outgoing[k].start()

    for k, offset in enumerate(offsets):
        back = slot[tuple(-step for step in offset)]
        incoming = pltpu.make_async_remote_copy(
            src_ref=sends[back],
            dst_ref=landed[k],
            send_sem=send_sem.at[back],
            recv_sem=recv_sem.at[k],
            device_id=target(offset),
            device_id_type=mesh_ids,
        )

        @pl.when(exists(offset))
        def _():
            outgoing[k].wait_send()
            incoming.wait_recv()
            outs[k][...] = landed[k][...]

        @pl.when(jnp.logical_not(exists(offset)))
        def _():
            outs[k][...] = jnp.zeros(outs[k].shape, outs[k].dtype)


def as_rows(piece, thin):
    sublanes = 1 if piece.shape[-2] == 1 else -(-piece.shape[-2] // 8) * 8
    tiled = math.prod(piece.shape[:-2]) * sublanes * -(-piece.shape[-1] // 128) * 128
    if tiled <= 3 * piece.size or tiled <= 65536:
        return piece, None
    moved = jnp.moveaxis(piece, thin, tuple(range(len(thin))))
    return moved.reshape(-1, moved.shape[-1]), moved.shape


def from_rows(piece, moved, thin):
    if moved is None:
        return piece
    return jnp.moveaxis(piece.reshape(moved), tuple(range(len(thin))), thin)


def with_plane_halo(shard, axes, dims, width):
    offsets = [(ox, oy) for ox in (-1, 0, 1) for oy in (-1, 0, 1) if (ox, oy) != (0, 0)]
    pieces = []
    layouts = []
    for offset in offsets:
        piece = shard
        thin = []
        for step, dim in zip(offset, dims):
            length = piece.shape[dim]
            if step == 1:
                piece = lax.slice_in_dim(piece, length - width, length, axis=dim)
            elif step == -1:
                piece = lax.slice_in_dim(piece, 0, width, axis=dim)
            if step != 0:
                thin.append(dim)
        piece, moved = as_rows(piece, thin)
        pieces.append(piece)
        layouts.append((moved, thin))
    key = ("plane",) + tuple(piece.shape for piece in pieces)
    if key not in HALO_IDS:
        HALO_IDS[key] = len(HALO_IDS)
    sizes = tuple(lax.axis_size(axis) for axis in axes)
    kernel = functools.partial(plane_kernel, axes=axes, sizes=sizes, offsets=tuple(offsets))
    vmem = pl.BlockSpec(memory_space=pltpu.VMEM)
    shapes = tuple(jax.ShapeDtypeStruct(piece.shape, piece.dtype) for piece in pieces)
    received = pl.pallas_call(
        kernel,
        out_shape=shapes,
        in_specs=[vmem] * len(pieces),
        out_specs=tuple([vmem] * len(pieces)),
        scratch_shapes=[pltpu.VMEM(piece.shape, piece.dtype) for piece in pieces]
        + [pltpu.SemaphoreType.DMA((len(pieces),)), pltpu.SemaphoreType.DMA((len(pieces),))],
        compiler_params=pltpu.CompilerParams(collective_id=HALO_IDS[key], has_side_effects=True),
    )(*pieces)
    got = {offset: from_rows(piece, *layout) for offset, piece, layout in zip(offsets, received, layouts)}
    got[(0, 0)] = shard
    rows = []
    for ox in (-1, 0, 1):
        rows.append(jnp.concatenate([got[(ox, oy)] for oy in (-1, 0, 1)], axis=dims[1]))
    return jnp.concatenate(rows, axis=dims[0])


def with_halo(shard, sides, width):
    for axis, dim in sides:
        length = shard.shape[dim]
        last = lax.slice_in_dim(shard, length - width, length, axis=dim)
        initial = lax.slice_in_dim(shard, 0, width, axis=dim)
        tiled = math.prod(initial.shape[:-2]) * -(-initial.shape[-2] // 8) * 8 * -(-initial.shape[-1] // 128) * 128
        if tiled <= 3 * initial.size:
            before, after = exchange(initial, last, axis)
        else:
            moved = jnp.moveaxis(initial, dim, 0).shape
            rows = (-1, moved[-1])
            before, after = exchange(
                jnp.moveaxis(initial, dim, 0).reshape(rows), jnp.moveaxis(last, dim, 0).reshape(rows), axis
            )
            before = jnp.moveaxis(before.reshape(moved), 0, dim)
            after = jnp.moveaxis(after.reshape(moved), 0, dim)
        shard = jnp.concatenate([before, shard, after], axis=dim)
    return shard


def recover(local_nodes, corner_vals, ratio_z):
    ex = local_nodes.shape[1] - 1
    ey = local_nodes.shape[2] - 1
    ratio_x = jnp.arange(ex + 1, dtype=jnp.float32) / ex
    ratio_y = jnp.arange(ey + 1, dtype=jnp.float32) / ey
    planes = []
    for high_z in (0, 1):
        plane = None
        for corner in range(high_z, 8, 2):
            along_x = ratio_x if corner // 4 == 1 else 1.0 - ratio_x
            along_y = ratio_y if corner // 2 % 2 == 1 else 1.0 - ratio_y
            basis = along_x[:, None] * along_y[None, :]
            term = basis[None] * corner_vals[:, corner][:, None, None]
            plane = term if plane is None else plane + term
        planes.append(plane[:, :, :, None])
    return local_nodes + planes[0] * (1.0 - ratio_z) + planes[1] * ratio_z


def average_rows(extended, dim, has_lower, has_upper):
    inner = extended.shape[dim] - 2
    own_rows = lax.slice_in_dim(extended, 1, inner + 1, axis=dim)
    rim_low = lax.slice_in_dim(extended, 0, 1, axis=dim)
    rim_high = lax.slice_in_dim(extended, inner + 1, inner + 2, axis=dim)
    shape_row = [1] * extended.ndim
    shape_row[dim] = inner
    rows = jnp.arange(inner, dtype=jnp.int32).reshape(shape_row)
    is_low = rows == 0
    is_high = rows == inner - 1
    factor = jnp.where(is_low & has_lower, 0.5, jnp.where(is_high & has_upper, 0.5, 1.0))
    rim_part = jnp.where(is_low, rim_low, 0.0) + jnp.where(is_high, rim_high, 0.0)
    return own_rows * factor + rim_part * 0.5


def quadratic(weights, vectors):
    total = None
    for a in range(24):
        inner = weights[a * 24 + a] * vectors[a]
        for b in range(a + 1, 24):
            inner = inner + weights[a * 24 + b] * vectors[b]
        term = vectors[a] * inner
        total = term if total is None else total + term
    return total


def energy_kernel(stiffness, base, up_y, up_z, up_yz, out, weights, *, count_x, count_y):
    sources = (base, up_z, up_y, up_yz)
    for a in range(24):
        weights[a * 24 + a] = stiffness[a, a]
        for b in range(a + 1, 24):
            weights[a * 24 + b] = stiffness[a, b] + stiffness[b, a]
    tail = count_y % 8
    full = count_y - tail

    def load(i, first, rows):
        vectors = []
        for component in range(3):
            for corner in range(8):
                source = sources[corner % 4]
                vectors.append(source[component, i + corner // 4, pl.ds(first, rows), :])
        return vectors

    def pair(step, carry):
        for i in (2 * step, 2 * step + 1):
            for first in range(0, full, 8):
                out[i, pl.ds(first, 8), :] = quadratic(weights, load(i, first, 8))
        low = load(2 * step, full, tail)
        high = load(2 * step + 1, full, tail)
        total = quadratic(weights, [jnp.concatenate([a, b], axis=0) for a, b in zip(low, high)])
        out[2 * step, pl.ds(full, tail), :] = total[:tail]
        out[2 * step + 1, pl.ds(full, tail), :] = total[tail:]
        return carry

    lax.fori_loop(0, count_x // 2, pair, 0)


def element_energy(nodes, stiffness):
    count_x = nodes.shape[1] - 1
    count_y = nodes.shape[2] - 1
    count_z = nodes.shape[3] - 1
    shifted = [nodes[:, :, dy : dy + count_y, dz : dz + count_z] for dy, dz in ((0, 0), (1, 0), (0, 1), (1, 1))]
    kernel = functools.partial(energy_kernel, count_x=count_x, count_y=count_y)
    vmem = pl.BlockSpec(memory_space=pltpu.VMEM)
    energy = pl.pallas_call(
        kernel,
        out_shape=jax.ShapeDtypeStruct((count_x, count_y, count_z), jnp.float32),
        in_specs=[pl.BlockSpec(memory_space=pltpu.SMEM)] + [vmem] * 4,
        out_specs=vmem,
        scratch_shapes=[pltpu.SMEM((24 * 24,), jnp.float32)],
    )(stiffness, *shifted)
    return energy


def smooth(field, axis, count):
    summed = None
    for offset in range(-RADIUS, RADIUS + 1):
        term_piece = lax.slice_in_dim(field, RADIUS + offset, RADIUS + offset + count, axis=axis)
        term_value = float(RADIUS + 1 - abs(offset)) * term_piece
        summed = term_value if summed is None else summed + term_value
    return summed


def edge_counts(count, position, parts):
    places = position * count + jnp.arange(count, dtype=jnp.int32)
    summed = None
    for offset in range(-RADIUS, RADIUS + 1):
        inside = ((places + offset >= 0) & (places + offset < count * parts)).astype(jnp.float32)
        term_value = float(RADIUS + 1 - abs(offset)) * inside
        summed = term_value if summed is None else summed + term_value
    return summed


def filter_field(field, sides):
    (axis_x, dim_x), (axis_y, dim_y), (axis_z, dim_z) = sides
    count_x, count_y = field.shape[dim_x], field.shape[dim_y]
    padded = with_plane_halo(field, (axis_x, axis_y), (dim_x, dim_y), RADIUS)
    field = smooth(smooth(padded, dim_x, count_x), dim_y, count_y)
    padded = with_halo(field, ((axis_z, dim_z),), RADIUS)
    return smooth(padded, dim_z, field.shape[dim_z])


def local(local_solution, top_nodes, coarse_solution, corner_dofs, density, element_stiffness):
    count_x, count_y, count_z = density.shape
    index_x = lax.axis_index("gx")
    index_y = lax.axis_index("gy")
    index_z = lax.axis_index("gz")
    normalizer = (
        edge_counts(count_x, index_x, lax.axis_size("gx"))[:, None, None]
        * edge_counts(count_y, index_y, lax.axis_size("gy"))[None, :, None]
        * edge_counts(count_z, index_z, lax.axis_size("gz"))[None, None, :]
    )
    sides = (("gx", 1), ("gy", 2), ("gz", 3))
    wanted = corner_dofs.reshape(8)
    gathered = gather_peers(coarse_solution, "gz")
    columns = gathered.transpose(1, 0, 2).reshape(coarse_solution.shape[0], -1)
    matches = wanted[:, None] == jnp.arange(columns.shape[1], dtype=jnp.int32)[None, :]
    corner_vals = jnp.sum(jnp.where(matches[None], columns[:, None, :], 0.0), axis=2)
    depth = local_solution.shape[3]
    full = jnp.concatenate([local_solution, top_nodes], axis=3)
    nodes = recover(full, corner_vals, jnp.arange(depth + 1, dtype=jnp.float32) / depth)
    lower_x = index_x > 0
    upper_x = index_x < lax.axis_size("gx") - 1
    lower_y = index_y > 0
    upper_y = index_y < lax.axis_size("gy") - 1
    lower_z = index_z > 0
    upper_z = index_z < lax.axis_size("gz") - 1
    extended = with_plane_halo(nodes, ("gx", "gy"), (1, 2), 1)
    extended = average_rows(extended, 1, lower_x, upper_x)
    averaged = average_rows(extended, 2, lower_y, upper_y)
    extended = with_halo(averaged, (("gz", 3),), 1)
    averaged = average_rows(extended, 3, lower_z, upper_z)
    energy = element_energy(averaged, element_stiffness)
    sens = penal_scale * density * density * energy
    smoothed = filter_field(jnp.stack([density * sens, density]), sides)
    numerator = smoothed[0]
    smooth_density = smoothed[1]
    return (numerator / (density * normalizer), smooth_density / normalizer)


def solution(mesh):
    in_specs = (
        P(None, "gx", "gy", "gz"),
        P(None, "gx", "gy", "gz"),
        P(None, "gz"),
        P("gx", "gy", "gz", None),
        P("gx", "gy", "gz"),
        P(),
    )
    out_specs = (P("gx", "gy", "gz"), P("gx", "gy", "gz"))
    return jax.shard_map(local, mesh=mesh, in_specs=in_specs, out_specs=out_specs, check_vma=False)
```

```python
import functools
import math

import jax
import jax.numpy as jnp
from jax import lax
from jax.sharding import PartitionSpec as P
from jax.experimental import pallas as pl
from jax.experimental.pallas import tpu as pltpu

RADIUS = 3


penal_scale = -3.0 / 96.0


def halo_kernel(low, high, before, after, landed_before, landed_after, send_sem, recv_sem, *, axis, count):
    me = lax.axis_index(axis)
    has_lower = me > 0
    has_upper = me < count - 1
    mesh_ids = pl.DeviceIdType.MESH
    barrier = pltpu.get_barrier_semaphore()

    @pl.when(has_lower)
    def _():
        pl.semaphore_signal(barrier, 1, device_id={axis: me - 1}, device_id_type=mesh_ids)

    @pl.when(has_upper)
    def _():
        pl.semaphore_signal(barrier, 1, device_id={axis: me + 1}, device_id_type=mesh_ids)

    pl.semaphore_wait(barrier, has_lower.astype(jnp.int32) + has_upper.astype(jnp.int32))

    to_upper = pltpu.make_async_remote_copy(
        src_ref=high,
        dst_ref=landed_before,
        send_sem=send_sem.at[0],
        recv_sem=recv_sem.at[0],
        device_id={axis: me + 1},
        device_id_type=mesh_ids,
    )
    to_lower = pltpu.make_async_remote_copy(
        src_ref=low,
        dst_ref=landed_after,
        send_sem=send_sem.at[1],
        recv_sem=recv_sem.at[1],
        device_id={axis: me - 1},
        device_id_type=mesh_ids,
    )

    @pl.when(has_upper)
    def _():
        to_upper.start()

    @pl.when(has_lower)
    def _():
        to_lower.start()

    @pl.when(has_upper)
    def _():
        to_upper.wait_send()
        to_lower.wait_recv()
        after[...] = landed_after[...]

    @pl.when(has_lower)
    def _():
        to_lower.wait_send()
        to_upper.wait_recv()
        before[...] = landed_before[...]

    @pl.when(jnp.logical_not(has_upper))
    def _():
        after[...] = jnp.zeros(after.shape, after.dtype)

    @pl.when(jnp.logical_not(has_lower))
    def _():
        before[...] = jnp.zeros(before.shape, before.dtype)


HALO_IDS = {}


def exchange(low, high, axis):
    key = (axis, low.shape)
    if key not in HALO_IDS:
        HALO_IDS[key] = len(HALO_IDS)
    kernel = functools.partial(halo_kernel, axis=axis, count=lax.axis_size(axis))
    vmem = pl.BlockSpec(memory_space=pltpu.VMEM)
    slab = jax.ShapeDtypeStruct(low.shape, low.dtype)
    return pl.pallas_call(
        kernel,
        out_shape=(slab, slab),
        in_specs=[vmem, vmem],
        out_specs=(vmem, vmem),
        scratch_shapes=[
            pltpu.VMEM(low.shape, low.dtype),
            pltpu.VMEM(low.shape, low.dtype),
            pltpu.SemaphoreType.DMA((2,)),
            pltpu.SemaphoreType.DMA((2,)),
        ],
        compiler_params=pltpu.CompilerParams(collective_id=HALO_IDS[key], has_side_effects=True),
    )(low, high)


def gather_kernel(shard, out, landed, send_sem, recv_sem, *, axis, count):
    me = lax.axis_index(axis)
    mesh_ids = pl.DeviceIdType.MESH
    barrier = pltpu.get_barrier_semaphore()
    for peer in range(count):

        @pl.when(peer != me)
        def _():
            pl.semaphore_signal(barrier, 1, device_id={axis: peer}, device_id_type=mesh_ids)

    pl.semaphore_wait(barrier, count - 1)
    copies = []
    for peer in range(count):
        copies.append(
            pltpu.make_async_remote_copy(
                src_ref=shard,
                dst_ref=landed.at[me],
                send_sem=send_sem.at[peer],
                recv_sem=recv_sem.at[me],
                device_id={axis: peer},
                device_id_type=mesh_ids,
            )
        )

        @pl.when(peer != me)
        def _():
            copies[peer].start()

    for peer in range(count):
        incoming = pltpu.make_async_remote_copy(
            src_ref=shard,
            dst_ref=landed.at[peer],
            send_sem=send_sem.at[peer],
            recv_sem=recv_sem.at[peer],
            device_id={axis: peer},
            device_id_type=mesh_ids,
        )

        @pl.when(peer != me)
        def _():
            copies[peer].wait_send()
            incoming.wait_recv()
            out[peer] = landed[peer]

    out[me] = shard[...]


def gather_peers(shard, axis):
    count = lax.axis_size(axis)
    kernel = functools.partial(gather_kernel, axis=axis, count=count)
    vmem = pl.BlockSpec(memory_space=pltpu.VMEM)
    stacked = (count,) + shard.shape
    return pl.pallas_call(
        kernel,
        out_shape=jax.ShapeDtypeStruct(stacked, shard.dtype),
        in_specs=[vmem],
        out_specs=vmem,
        scratch_shapes=[
            pltpu.VMEM(stacked, shard.dtype),
            pltpu.SemaphoreType.DMA((count,)),
            pltpu.SemaphoreType.DMA((count,)),
        ],
        compiler_params=pltpu.CompilerParams(collective_id=100, has_side_effects=True),
    )(shard)


def plane_kernel(*refs, axes, sizes, offsets):
    count = len(offsets)
    sends = refs[:count]
    outs = refs[count : 2 * count]
    landed = refs[2 * count : 3 * count]
    send_sem, recv_sem = refs[3 * count :]
    me = [lax.axis_index(axis) for axis in axes]
    mesh_ids = pl.DeviceIdType.MESH

    def exists(offset):
        inside = None
        for position, step, size in zip(me, offset, sizes):
            if step == 0:
                continue
            here = (position + step >= 0) & (position + step < size)
            inside = here if inside is None else inside & here
        return inside

    def target(offset):
        return {axis: position + step for axis, position, step in zip(axes, me, offset)}

    barrier = pltpu.get_barrier_semaphore()
    expected = 0
    for offset in offsets:

        @pl.when(exists(offset))
        def _():
            pl.semaphore_signal(barrier, 1, device_id=target(offset), device_id_type=mesh_ids)

        expected = expected + exists(offset).astype(jnp.int32)
    pl.semaphore_wait(barrier, expected)
    slot = {offset: k for k, offset in enumerate(offsets)}
    outgoing = []
    for k, offset in enumerate(offsets):
        back = slot[tuple(-step for step in offset)]
        outgoing.append(
            pltpu.make_async_remote_copy(
                src_ref=sends[k],
                dst_ref=landed[back],
                send_sem=send_sem.at[k],
                recv_sem=recv_sem.at[back],
                device_id=target(offset),
                device_id_type=mesh_ids,
            )
        )

        @pl.when(exists(offset))
        def _():
            outgoing[k].start()

    for k, offset in enumerate(offsets):
        back = slot[tuple(-step for step in offset)]
        incoming = pltpu.make_async_remote_copy(
            src_ref=sends[back],
            dst_ref=landed[k],
            send_sem=send_sem.at[back],
            recv_sem=recv_sem.at[k],
            device_id=target(offset),
            device_id_type=mesh_ids,
        )

        @pl.when(exists(offset))
        def _():
            outgoing[k].wait_send()
            incoming.wait_recv()
            outs[k][...] = landed[k][...]

        @pl.when(jnp.logical_not(exists(offset)))
        def _():
            outs[k][...] = jnp.zeros(outs[k].shape, outs[k].dtype)


def as_rows(piece, thin):
    sublanes = 1 if piece.shape[-2] == 1 else -(-piece.shape[-2] // 8) * 8
    tiled = math.prod(piece.shape[:-2]) * sublanes * -(-piece.shape[-1] // 128) * 128
    if tiled <= 3 * piece.size or tiled <= 65536:
        return piece, None
    moved = jnp.moveaxis(piece, thin, tuple(range(len(thin))))
    return moved.reshape(-1, moved.shape[-1]), moved.shape


def from_rows(piece, moved, thin):
    if moved is None:
        return piece
    return jnp.moveaxis(piece.reshape(moved), tuple(range(len(thin))), thin)


def with_plane_halo(shard, axes, dims, width):
    offsets = [(ox, oy) for ox in (-1, 0, 1) for oy in (-1, 0, 1) if (ox, oy) != (0, 0)]
    pieces = []
    layouts = []
    for offset in offsets:
        piece = shard
        thin = []
        for step, dim in zip(offset, dims):
            length = piece.shape[dim]
            if step == 1:
                piece = lax.slice_in_dim(piece, length - width, length, axis=dim)
            elif step == -1:
                piece = lax.slice_in_dim(piece, 0, width, axis=dim)
            if step != 0:
                thin.append(dim)
        piece, moved = as_rows(piece, thin)
        pieces.append(piece)
        layouts.append((moved, thin))
    key = ("plane",) + tuple(piece.shape for piece in pieces)
    if key not in HALO_IDS:
        HALO_IDS[key] = len(HALO_IDS)
    sizes = tuple(lax.axis_size(axis) for axis in axes)
    kernel = functools.partial(plane_kernel, axes=axes, sizes=sizes, offsets=tuple(offsets))
    vmem = pl.BlockSpec(memory_space=pltpu.VMEM)
    shapes = tuple(jax.ShapeDtypeStruct(piece.shape, piece.dtype) for piece in pieces)
    received = pl.pallas_call(
        kernel,
        out_shape=shapes,
        in_specs=[vmem] * len(pieces),
        out_specs=tuple([vmem] * len(pieces)),
        scratch_shapes=[pltpu.VMEM(piece.shape, piece.dtype) for piece in pieces]
        + [pltpu.SemaphoreType.DMA((len(pieces),)), pltpu.SemaphoreType.DMA((len(pieces),))],
        compiler_params=pltpu.CompilerParams(collective_id=HALO_IDS[key], has_side_effects=True),
    )(*pieces)
    got = {offset: from_rows(piece, *layout) for offset, piece, layout in zip(offsets, received, layouts)}
    got[(0, 0)] = shard
    rows = []
    for ox in (-1, 0, 1):
        rows.append(jnp.concatenate([got[(ox, oy)] for oy in (-1, 0, 1)], axis=dims[1]))
    return jnp.concatenate(rows, axis=dims[0])


def with_halo(shard, sides, width):
    for axis, dim in sides:
        length = shard.shape[dim]
        last = lax.slice_in_dim(shard, length - width, length, axis=dim)
        initial = lax.slice_in_dim(shard, 0, width, axis=dim)
        tiled = math.prod(initial.shape[:-2]) * -(-initial.shape[-2] // 8) * 8 * -(-initial.shape[-1] // 128) * 128
        if tiled <= 3 * initial.size:
            before, after = exchange(initial, last, axis)
        else:
            moved = jnp.moveaxis(initial, dim, 0).shape
            rows = (-1, moved[-1])
            before, after = exchange(
                jnp.moveaxis(initial, dim, 0).reshape(rows), jnp.moveaxis(last, dim, 0).reshape(rows), axis
            )
            before = jnp.moveaxis(before.reshape(moved), 0, dim)
            after = jnp.moveaxis(after.reshape(moved), 0, dim)
        shard = jnp.concatenate([before, shard, after], axis=dim)
    return shard


def recover(local_nodes, corner_vals, ratio_z):
    ex = local_nodes.shape[1] - 1
    ey = local_nodes.shape[2] - 1
    ratio_x = jnp.arange(ex + 1, dtype=jnp.float32) / ex
    ratio_y = jnp.arange(ey + 1, dtype=jnp.float32) / ey
    planes = []
    for high_z in (0, 1):
        plane = None
        for corner in range(high_z, 8, 2):
            along_x = ratio_x if corner // 4 == 1 else 1.0 - ratio_x
            along_y = ratio_y if corner // 2 % 2 == 1 else 1.0 - ratio_y
            basis = along_x[:, None] * along_y[None, :]
            term = basis[None] * corner_vals[:, corner][:, None, None]
            plane = term if plane is None else plane + term
        planes.append(plane[:, :, :, None])
    return local_nodes + planes[0] * (1.0 - ratio_z) + planes[1] * ratio_z


def average_rows(extended, dim, has_lower, has_upper):
    inner = extended.shape[dim] - 2
    own_rows = lax.slice_in_dim(extended, 1, inner + 1, axis=dim)
    rim_low = lax.slice_in_dim(extended, 0, 1, axis=dim)
    rim_high = lax.slice_in_dim(extended, inner + 1, inner + 2, axis=dim)
    shape_row = [1] * extended.ndim
    shape_row[dim] = inner
    rows = jnp.arange(inner, dtype=jnp.int32).reshape(shape_row)
    is_low = rows == 0
    is_high = rows == inner - 1
    factor = jnp.where(is_low & has_lower, 0.5, jnp.where(is_high & has_upper, 0.5, 1.0))
    rim_part = jnp.where(is_low, rim_low, 0.0) + jnp.where(is_high, rim_high, 0.0)
    return own_rows * factor + rim_part * 0.5


def quadratic(weights, vectors):
    total = None
    for a in range(24):
        inner = weights[a * 24 + a] * vectors[a]
        for b in range(a + 1, 24):
            inner = inner + weights[a * 24 + b] * vectors[b]
        term = vectors[a] * inner
        total = term if total is None else total + term
    return total


def energy_kernel(stiffness, base, up_y, up_z, up_yz, density, out, weights, *, count_x, count_y):
    sources = (base, up_z, up_y, up_yz)
    for a in range(24):
        weights[a * 24 + a] = stiffness[a, a]
        for b in range(a + 1, 24):
            weights[a * 24 + b] = stiffness[a, b] + stiffness[b, a]
    tail = count_y % 8
    full = count_y - tail

    def load(i, first, rows):
        vectors = []
        for component in range(3):
            for corner in range(8):
                source = sources[corner % 4]
                vectors.append(source[component, i + corner // 4, pl.ds(first, rows), :])
        return vectors

    def put(i, first, rows, energy):
        local_density = density[i, pl.ds(first, rows), :]
        sens = penal_scale * local_density * local_density * energy
        out[0, i, pl.ds(first, rows), :] = local_density * sens
        out[1, i, pl.ds(first, rows), :] = local_density

    def pair(step, carry):
        for i in (2 * step, 2 * step + 1):
            for first in range(0, full, 8):
                put(i, first, 8, quadratic(weights, load(i, first, 8)))
        low = load(2 * step, full, tail)
        high = load(2 * step + 1, full, tail)
        total = quadratic(weights, [jnp.concatenate([a, b], axis=0) for a, b in zip(low, high)])
        put(2 * step, full, tail, total[:tail])
        put(2 * step + 1, full, tail, total[tail:])
        return carry

    lax.fori_loop(0, count_x // 2, pair, 0)


def weighted_sensitivity(nodes, stiffness, density):
    count_x = nodes.shape[1] - 1
    count_y = nodes.shape[2] - 1
    count_z = nodes.shape[3] - 1
    shifted = [nodes[:, :, dy : dy + count_y, dz : dz + count_z] for dy, dz in ((0, 0), (1, 0), (0, 1), (1, 1))]
    kernel = functools.partial(energy_kernel, count_x=count_x, count_y=count_y)
    vmem = pl.BlockSpec(memory_space=pltpu.VMEM)
    energy = pl.pallas_call(
        kernel,
        out_shape=jax.ShapeDtypeStruct((2, count_x, count_y, count_z), jnp.float32),
        in_specs=[pl.BlockSpec(memory_space=pltpu.SMEM)] + [vmem] * 5,
        out_specs=vmem,
        scratch_shapes=[pltpu.SMEM((24 * 24,), jnp.float32)],
    )(stiffness, *shifted, density)
    return energy


def smooth(field, axis, count):
    summed = None
    for offset in range(-RADIUS, RADIUS + 1):
        term_piece = lax.slice_in_dim(field, RADIUS + offset, RADIUS + offset + count, axis=axis)
        term_value = float(RADIUS + 1 - abs(offset)) * term_piece
        summed = term_value if summed is None else summed + term_value
    return summed


def edge_counts(count, position, parts):
    places = position * count + jnp.arange(count, dtype=jnp.int32)
    summed = None
    for offset in range(-RADIUS, RADIUS + 1):
        inside = ((places + offset >= 0) & (places + offset < count * parts)).astype(jnp.float32)
        term_value = float(RADIUS + 1 - abs(offset)) * inside
        summed = term_value if summed is None else summed + term_value
    return summed


def filter_field(field, sides):
    (axis_x, dim_x), (axis_y, dim_y), (axis_z, dim_z) = sides
    count_x, count_y = field.shape[dim_x], field.shape[dim_y]
    padded = with_plane_halo(field, (axis_x, axis_y), (dim_x, dim_y), RADIUS)
    field = smooth(smooth(padded, dim_x, count_x), dim_y, count_y)
    padded = with_halo(field, ((axis_z, dim_z),), RADIUS)
    return smooth(padded, dim_z, field.shape[dim_z])


def local(local_solution, top_nodes, coarse_solution, corner_dofs, density, element_stiffness):
    count_x, count_y, count_z = density.shape
    index_x = lax.axis_index("gx")
    index_y = lax.axis_index("gy")
    index_z = lax.axis_index("gz")
    normalizer = (
        edge_counts(count_x, index_x, lax.axis_size("gx"))[:, None, None]
        * edge_counts(count_y, index_y, lax.axis_size("gy"))[None, :, None]
        * edge_counts(count_z, index_z, lax.axis_size("gz"))[None, None, :]
    )
    sides = (("gx", 1), ("gy", 2), ("gz", 3))
    wanted = corner_dofs.reshape(8)
    gathered = gather_peers(coarse_solution, "gz")
    columns = gathered.transpose(1, 0, 2).reshape(coarse_solution.shape[0], -1)
    matches = wanted[:, None] == jnp.arange(columns.shape[1], dtype=jnp.int32)[None, :]
    corner_vals = jnp.sum(jnp.where(matches[None], columns[:, None, :], 0.0), axis=2)
    depth = local_solution.shape[3]
    full = jnp.concatenate([local_solution, top_nodes], axis=3)
    nodes = recover(full, corner_vals, jnp.arange(depth + 1, dtype=jnp.float32) / depth)
    lower_x = index_x > 0
    upper_x = index_x < lax.axis_size("gx") - 1
    lower_y = index_y > 0
    upper_y = index_y < lax.axis_size("gy") - 1
    lower_z = index_z > 0
    upper_z = index_z < lax.axis_size("gz") - 1
    extended = with_plane_halo(nodes, ("gx", "gy"), (1, 2), 1)
    extended = average_rows(extended, 1, lower_x, upper_x)
    averaged = average_rows(extended, 2, lower_y, upper_y)
    extended = with_halo(averaged, (("gz", 3),), 1)
    averaged = average_rows(extended, 3, lower_z, upper_z)
    smoothed = filter_field(weighted_sensitivity(averaged, element_stiffness, density), sides)
    numerator = smoothed[0]
    smooth_density = smoothed[1]
    return (numerator / (density * normalizer), smooth_density / normalizer)


def solution(mesh):
    in_specs = (
        P(None, "gx", "gy", "gz"),
        P(None, "gx", "gy", "gz"),
        P(None, "gz"),
        P("gx", "gy", "gz", None),
        P("gx", "gy", "gz"),
        P(),
    )
    out_specs = (P("gx", "gy", "gz"), P("gx", "gy", "gz"))
    return jax.shard_map(local, mesh=mesh, in_specs=in_specs, out_specs=out_specs, check_vma=False)
```
